256 devices in a mesh: wide: 32 (over x, z), narrow: 8 (over y, core).
Axes of the slice: x: 4, y: 4, z: 8, core: 2. Of those that a mesh axis runs over, the one named last changes fastest.
Arguments:
- pdfs: float32 [19, 1024, 8192], P(None, 'wide', 'narrow'), may hold values from 0.05 to 1
- link_flags: int32 [2, 1024, 8192], P(None, 'wide', 'narrow'), may hold values from 0 to 1022, as said below
- block_level: int32 [32, 8], P('wide', 'narrow'), may hold values from 0 to 1
- grain_pos: float32 [3, 262144], P(None, ('wide', 'narrow')), may hold values from 0 to 32
- grain_vel: float32 [3, 262144], P(None, ('wide', 'narrow')), may hold values from -3 to 3
- grain_radius: float32 [262144], P(('wide', 'narrow')), may hold values from 0.5 to 1.5
- grain_cell: int32 [262144], P(('wide', 'narrow')), may hold values from 0 to 32767
- contact_pairs: int32 [2, 786432], P(None, ('wide', 'narrow')), may hold values from 0 to 1023
- contact_spring: float32 [3, 786432], P(None, ('wide', 'narrow')), may hold values from -6 to 6
- iface_source: int32 [262144], P(('wide', 'narrow')), may hold values from 0 to 32767
- iface_offset: int32 [1024], replicated, may hold values from -2 to 2, as said below
- iface_slot: int32 [1024], replicated, may hold values from 0 to 1023, each once
- iface_target: int32 [262144], P(('wide', 'narrow')), may hold values from 0 to 32767, as said below
- migrant_slots: int32 [2, 16384], P(None, ('wide', 'narrow')), may hold values from 0 to 1023, as said below
Outputs:
- pdfs_next: float32 [19, 1024, 8192], P(None, 'wide', 'narrow')
- grain_pos_next: float32 [3, 262144], P(None, ('wide', 'narrow'))
- grain_vel_next: float32 [3, 262144], P(None, ('wide', 'narrow'))
- grain_radius_next: float32 [262144], P(('wide', 'narrow'))
- contact_spring_next: float32 [3, 786432], P(None, ('wide', 'narrow'))
The draws below stay inside these ranges and needn't reach their ends.
Inputs may be any that keep to these rules, and one draw needn't show every extreme that they name: `iface_offset`: each of -2, -1, 0, 1, 2 occurs; each nonzero value occurs at most 1024 // 4 times, and one of them exactly so; the same row r goes the same number of blocks along the length from every block, staying at its place across the width. `iface_slot`: the same for every block. `iface_target`: distinct within a block. `iface_source`: local cell indices. `migrant_slots`: the 128 slots of a block are distinct; every block sends exactly 64 grains each way. `contact_pairs`: slots of grains of the same block. `grain_cell`: local cell indices. `link_flags`: bit 0 of row 0 is never set and row 1 uses bits 0 to 8 only; in the bottom layer (z = 0) the links of all directions with c_z = 1 are solid, in the top layer those with c_z = -1.
All inputs are finite; a program needn't handle non-finite values.
Results may differ from the reference program's by a relative error of at most 0.00002.
Values sent between devices are 32-bit elements; how exact they have to be, the bound alone decides.
A program may use at most 128 MiB of HBM per device.

```python
import math
import jax
import jax.numpy as jnp

DIRS = 19
CELLS_X = 32
CELLS_Y = 32
CELLS_Z = 32
IFACE_ROWS = 1024
GRAINS_DEV = 1024
MIGRANTS = 64
CONTACTS_DEV = 3072
LEN_X = 1024
LEN_Y = 256
GRAINS = 262144
CONTACTS = 786432
IFACE = 262144
N_WIDE = 32
N_NARROW = 8


UPWARD = (5, 11, 14, 15, 18)


DOWNWARD = (6, 12, 13, 16, 17)


def draw_link_flags(key, part):
    width = LEN_Y * CELLS_Z
    height = jnp.arange(width, dtype=jnp.int32) % CELLS_Z
    bottom = (height == 0).astype(jnp.int32)[None, :]
    top = (height == CELLS_Z - 1).astype(jnp.int32)[None, :]
    lower_word = jnp.zeros((LEN_X, width), jnp.int32)
    upper_word = jnp.zeros((LEN_X, width), jnp.int32)
    for index in range(1, 19):
        draws = jax.random.randint(jax.random.fold_in(key, index), (LEN_X, width), 0, 100)
        solid = (draws < 15).astype(jnp.int32)
        if index in UPWARD:
            solid = jnp.maximum(solid, bottom)
        if index in DOWNWARD:
            solid = jnp.maximum(solid, top)
        if index < 10:
            lower_word = lower_word + solid * 2 ** index
        else:
            upper_word = upper_word + solid * 2 ** (index - 10)
    return jnp.stack([lower_word, upper_word]).astype(jnp.int32)


def draw_iface_offset(key, part):
    quota = IFACE_ROWS // 4
    lowest = IFACE_ROWS // 5
    others = jax.random.randint(jax.random.fold_in(key, 1), (3,), lowest, quota).astype(jnp.int32)
    nonzero_counts = jnp.concatenate([jnp.array([quota], dtype=jnp.int32), others])
    nonzero_values = jax.random.permutation(jax.random.fold_in(key, 2), jnp.array([-2, -1, 1, 2], dtype=jnp.int32))
    zero_count = IFACE_ROWS - jnp.sum(nonzero_counts)
    counts = jnp.concatenate([nonzero_counts, zero_count[None]]).astype(jnp.int32)
    values = jnp.concatenate([nonzero_values, jnp.zeros((1,), jnp.int32)])
    ends = jnp.cumsum(counts).astype(jnp.int32)
    position = jnp.arange(IFACE_ROWS, dtype=jnp.int32)
    which = jnp.sum((position[:, None] >= ends[None, :]).astype(jnp.int32), axis=1)
    joined = values[which]
    return jax.random.permutation(jax.random.fold_in(key, 3), joined).astype(jnp.int32)


def draw_iface_target(key, part):
    blocks = IFACE // IFACE_ROWS
    cells = CELLS_X * CELLS_Y * CELLS_Z
    keys = jax.random.split(jax.random.fold_in(key, 3), blocks)

    def choose(single):
        return jax.random.permutation(single, cells)[:IFACE_ROWS].astype(jnp.int32)
    return jax.vmap(choose)(keys).reshape(-1)


def draw_migrant_slots(key, part):
    blocks = GRAINS // GRAINS_DEV
    keys = jax.random.split(jax.random.fold_in(key, 4), blocks)

    def choose(single):
        return jax.random.permutation(single, GRAINS_DEV)[:2 * MIGRANTS].astype(jnp.int32)
    picked = jax.vmap(choose)(keys).reshape(blocks, 2, MIGRANTS)
    return jnp.transpose(picked, (1, 0, 2)).reshape(2, blocks * MIGRANTS)


def touch_ends(values, stream_key, low, high):
    index_at = [jax.random.randint(jax.random.fold_in(stream_key, axis), (), 0, length) for axis, length in enumerate(values.shape)]
    widest = values.shape.index(max(values.shape))
    neighbour = index_at[:widest] + [(index_at[widest] + 1) % values.shape[widest]] + index_at[widest + 1:]
    return values.at[tuple(index_at)].set(low).at[tuple(neighbour)].set(high)


def steps_of(rng, shape, cuts, least, top_value):
    def one(axis_at, blocks):
        steps = jax.random.uniform(jax.random.fold_in(jax.random.fold_in(rng, 6), axis_at), (blocks,), jnp.float32, least / len(cuts), top_value / len(cuts))
        return jnp.repeat(jnp.exp(steps), shape[axis_at] // blocks).reshape((-1,) + (1,) * (len(shape) - axis_at - 1))

    level = one(*cuts[0])
    for cut in cuts[1:]:
        level = level * one(*cut)
    return level


def bell_draw(own_key, extent, scale, limit, shards=(), held_as=jnp.bfloat16):
    entries = scale * jax.random.normal(own_key, extent, jnp.float32)
    if shards:
        entries = entries * steps_of(own_key, extent, shards, -0.22, 0.18)
    return jnp.clip(entries, -limit, limit).astype(held_as)


def setup_inputs(seed: int = 0) -> dict:
    streams_of = jax.random.split(jax.random.key(seed), 15)
    return {
        "pdfs": jnp.clip(0.05 + 0.95 * jax.random.uniform(streams_of[0], (DIRS, LEN_X, LEN_Y * CELLS_Z), jnp.float32) ** steps_of(streams_of[0], (DIRS, LEN_X, LEN_Y * CELLS_Z), ((1, 32), (2, 8)), -0.2, 0.2), 0.05, 1.0),
        "link_flags": draw_link_flags(jax.random.fold_in(streams_of[14], 71), 0),
        "block_level": touch_ends(jax.random.randint(streams_of[2], (N_WIDE, N_NARROW), 0, 2), jax.random.fold_in(streams_of[2], 1), 0, 1).astype(jnp.int32),
        "grain_pos": jnp.clip(32.0 * jax.random.uniform(streams_of[3], (3, GRAINS), jnp.float32) ** steps_of(streams_of[3], (3, GRAINS), ((1, 256),), -0.2, 0.2), 0.0, 32.0),
        "grain_vel": bell_draw(streams_of[4], (3, GRAINS), 0.5, 3.0, ((1, 256),), jnp.float32),
        "grain_radius": jnp.clip(jnp.exp(math.log(1.5) - 1.0986123 * jax.random.uniform(streams_of[5], (GRAINS,), jnp.float32) ** steps_of(streams_of[5], (GRAINS,), ((0, 256),), -0.2, 0.2)), 0.5, 1.5),
        "grain_cell": touch_ends(jax.random.randint(streams_of[6], (GRAINS,), 0, CELLS_X * CELLS_Y * CELLS_Z), jax.random.fold_in(streams_of[6], 1), 0, (CELLS_X * CELLS_Y * CELLS_Z) - 1).astype(jnp.int32),
        "contact_pairs": touch_ends(jax.random.randint(streams_of[7], (2, CONTACTS), 0, GRAINS_DEV), jax.random.fold_in(streams_of[7], 1), 0, GRAINS_DEV - 1).astype(jnp.int32),
        "contact_spring": bell_draw(streams_of[8], (3, CONTACTS), 1.0, 6.0, ((1, 256),), jnp.float32),
        "iface_source": touch_ends(jax.random.randint(streams_of[9], (IFACE,), 0, CELLS_X * CELLS_Y * CELLS_Z), jax.random.fold_in(streams_of[9], 1), 0, (CELLS_X * CELLS_Y * CELLS_Z) - 1).astype(jnp.int32),
        "iface_offset": draw_iface_offset(jax.random.fold_in(streams_of[14], 71), 0),
        "iface_slot": jax.random.permutation(streams_of[11], IFACE_ROWS).astype(jnp.int32),
        "iface_target": draw_iface_target(jax.random.fold_in(streams_of[14], 71), 0),
        "migrant_slots": draw_migrant_slots(jax.random.fold_in(streams_of[14], 71), 0),
    }


VELOCITY = ((0, 0, 0), (1, 0, 0), (-1, 0, 0), (0, 1, 0), (0, -1, 0), (0, 0, 1), (0, 0, -1),
            (1, 1, 0), (-1, -1, 0), (1, -1, 0), (-1, 1, 0), (1, 0, 1), (-1, 0, -1), (1, 0, -1),
            (-1, 0, 1), (0, 1, 1), (0, -1, -1), (0, 1, -1), (0, -1, 1))
OPPOSITE = (0, 2, 1, 4, 3, 6, 5, 8, 7, 10, 9, 12, 11, 14, 13, 16, 15, 18, 17)
WEIGHT = (1.0 / 3.0,) + (1.0 / 18.0,) * 6 + (1.0 / 36.0,) * 12
tau_coarse = 1.0
tau_fine = 1.5
drag_coef = 0.5
mass_coef = 10.0
spring_coef = 0.2
dashpot_coef = 0.05
gravity_z = -0.01
blend_coef = 0.5


def moments(pdfs):
    density = pdfs[0]
    for index in range(1, 19):
        density = density + pdfs[index]
    parts = []
    for axis_pick in range(3):
        total = jnp.zeros_like(density)
        for index in range(19):
            factor = VELOCITY[index][axis_pick]
            if factor != 0:
                total = total + factor * pdfs[index]
        parts.append(total)
    return density, jnp.stack(parts)


def relaxation(pdfs, density, shifted, relax_time):
    square = shifted[0] * shifted[0] + shifted[1] * shifted[1] + shifted[2] * shifted[2]
    result = []
    for index in range(19):
        shift_x, shift_y, shift_z = VELOCITY[index]
        along = shift_x * shifted[0] + shift_y * shifted[1] + shift_z * shifted[2]
        equilibrium = WEIGHT[index] * density * (1.0 + 3.0 * along + 4.5 * along * along - 1.5 * square)
        result.append(pdfs[index] - (pdfs[index] - equilibrium) / relax_time)
    return jnp.stack(result)


def solid_link(link_flags, index):
    row_pick = 0 if index < 10 else 1
    bit_pick = index if index < 10 else index - 10
    return (link_flags[row_pick] // (2 ** bit_pick)) % 2 == 1


def reference(pdfs, link_flags, block_level, grain_pos, grain_vel, grain_radius, grain_cell,
              contact_pairs, contact_spring, iface_source, iface_offset, iface_slot, iface_target,
              migrant_slots):
    plane_size = CELLS_Y * CELLS_Z
    density, momentum = moments(pdfs)
    velocity = momentum / density[None]
    grain_dev = jnp.arange(GRAINS, dtype=jnp.int32) // GRAINS_DEV
    grain_x = (grain_dev // N_NARROW) * CELLS_X + grain_cell // plane_size
    grain_yz = (grain_dev % N_NARROW) * plane_size + grain_cell % plane_size
    fluid_at = velocity[:, grain_x, grain_yz]
    drag_rate = drag_coef * grain_radius
    grain_force = drag_rate[None] * (fluid_at - grain_vel)
    fluid_force = jnp.zeros_like(momentum).at[:, grain_x, grain_yz].add(-grain_force)
    tau_block = jnp.where(block_level == 1, tau_fine, tau_coarse).astype(jnp.float32)
    relax_time = jnp.repeat(jnp.repeat(tau_block, CELLS_X, axis=0), plane_size, axis=1)
    shifted = (momentum + relax_time[None] * fluid_force) / density[None]
    post = relaxation(pdfs, density, shifted, relax_time)

    post_grid = post.reshape(DIRS, LEN_X, LEN_Y, CELLS_Z)
    read = []
    for index in range(19):
        shift_x, shift_y, shift_z = VELOCITY[index]
        moved = jnp.roll(post_grid[index], (shift_x, shift_y, shift_z), axis=(0, 1, 2)).reshape(LEN_X, LEN_Y * CELLS_Z)
        solid = solid_link(link_flags, index)
        read.append(jnp.where(solid, post[OPPOSITE[index]], moved))
    read = jnp.stack(read)

    row_dev = jnp.arange(IFACE, dtype=jnp.int32) // IFACE_ROWS
    row_index = jnp.arange(IFACE, dtype=jnp.int32) % IFACE_ROWS
    source_x = (row_dev // N_NARROW) * CELLS_X + iface_source // plane_size
    source_yz = (row_dev % N_NARROW) * plane_size + iface_source % plane_size
    outgoing = read[:, source_x, source_yz]
    dest_wide = (row_dev // N_NARROW + iface_offset[row_index]) % N_WIDE
    dest_dev = dest_wide * N_NARROW + row_dev % N_NARROW
    target = iface_target[dest_dev * IFACE_ROWS + iface_slot[row_index]]
    target_x = dest_wide * CELLS_X + target // plane_size
    target_yz = (row_dev % N_NARROW) * plane_size + target % plane_size
    pdfs_next = read.at[:, target_x, target_yz].set(blend_coef * (read[:, target_x, target_yz] + outgoing))

    pair_dev = jnp.arange(CONTACTS, dtype=jnp.int32) // CONTACTS_DEV
    first = pair_dev * GRAINS_DEV + contact_pairs[0]
    second = pair_dev * GRAINS_DEV + contact_pairs[1]
    relative = grain_vel[:, second] - grain_vel[:, first]
    contact_force = spring_coef * contact_spring + dashpot_coef * relative
    total_force = grain_force.at[:, first].add(contact_force).at[:, second].add(-contact_force)
    grain_mass = mass_coef * grain_radius * grain_radius * grain_radius
    gravity = jnp.array([0.0, 0.0, gravity_z], dtype=jnp.float32)
    moved_vel = grain_vel + total_force / grain_mass[None] + gravity[:, None]
    moved_pos = grain_pos + moved_vel
    spring_next = contact_spring + relative

    state = jnp.concatenate([moved_pos, moved_vel, grain_radius[None]], axis=0)
    slots = migrant_slots.reshape(2, N_WIDE, N_NARROW, MIGRANTS)
    wide_pos = jnp.arange(N_WIDE, dtype=jnp.int32)[:, None, None]
    narrow_pos = jnp.arange(N_NARROW, dtype=jnp.int32)[None, :, None]
    result = state
    for row_pick, distance, displace in ((0, -1, 1.0), (1, 1, -1.0)):
        own = ((wide_pos * N_NARROW + narrow_pos) * GRAINS_DEV + slots[row_pick]).reshape(-1)
        source_wide = (wide_pos - distance) % N_WIDE
        source = ((source_wide * N_NARROW + narrow_pos) * GRAINS_DEV + jnp.roll(slots[row_pick], distance, axis=0)).reshape(-1)
        shift_vec = jnp.zeros((7, 1), jnp.float32).at[0, 0].set(displace * CELLS_X)
        result = result.at[:, own].set(state[:, source] + shift_vec)
    return pdfs_next, result[0:3], result[3:6], result[6], spring_next
```

```python
import functools

import jax
import jax.numpy as jnp
from jax import lax
from jax.experimental import pallas as pl
from jax.experimental.pallas import tpu as pltpu
from jax.sharding import PartitionSpec as P

VELOCITY = (
    (0, 0, 0), (1, 0, 0), (-1, 0, 0), (0, 1, 0), (0, -1, 0), (0, 0, 1), (0, 0, -1),
    (1, 1, 0), (-1, -1, 0), (1, -1, 0), (-1, 1, 0), (1, 0, 1), (-1, 0, -1), (1, 0, -1),
    (-1, 0, 1), (0, 1, 1), (0, -1, -1), (0, 1, -1), (0, -1, 1),
)
OPPOSITE = (0, 2, 1, 4, 3, 6, 5, 8, 7, 10, 9, 12, 11, 14, 13, 16, 15, 18, 17)
tau_coarse = 1.0
tau_fine = 1.5
drag_coef = 0.5
mass_coef = 10.0
spring_coef = 0.2
dashpot_coef = 0.05
gravity_z = -0.01
blend_coef = 0.5

NX = 32
NYZ = 1024
TOP = 8
EXT = NX + 16
X_PLUS = (1, 7, 9, 11, 13)
X_MINUS = (2, 8, 10, 12, 14)
Y_PLUS = (3, 7, 10, 15, 17)
Y_MINUS = (4, 8, 9, 16, 18)
DISTANCE = (-2, 2, -1, 1)
MESH = pl.DeviceIdType.MESH
F32 = jnp.float32
BF16 = jnp.bfloat16
NT = (((1,), (1,)), ((), ()))
NN = (((1,), (0,)), ((), ()))


def iota(shape, axis):
    return lax.broadcasted_iota(jnp.int32, shape, axis)


def split2(value):
    high = value.astype(BF16).astype(F32)
    return high, value - high


def split3(value):
    high = value.astype(BF16).astype(F32)
    rest = value - high
    middle = rest.astype(BF16).astype(F32)
    return high, middle, rest - middle


def one_hot(row, size, start=0):
    lanes = row.shape[1]
    return jnp.where(iota((size, lanes), 0) + start == row, 1.0, 0.0).astype(BF16)


def fill_one_hot(ref, row):
    step = 128

    @pl.loop(0, NYZ // step)
    def _(i):
        start = pl.multiple_of(i * step, step)
        ref[pl.ds(start, step), :] = one_hot(row, step, start)


def dot(a, b, dims):
    return lax.dot_general(a, b, dims, preferred_element_type=F32)


def pack_interface(off_ref, slot_ref, src_ref, tgt_ref):
    off = off_ref[...]
    s8 = iota((8, NYZ), 0)
    dval = jnp.where(s8 == 0, DISTANCE[0], jnp.where(s8 == 1, DISTANCE[1], jnp.where(s8 == 2, DISTANCE[2], jnp.where(
        s8 == 3, DISTANCE[3], jnp.where(s8 == 4, 0, 99)))))
    member = jnp.where(off == dval, 1.0, 0.0)
    blocks = [member[:, b * 128:(b + 1) * 128] for b in range(8)]
    before = jnp.where(iota((128, 128), 0) < iota((128, 128), 1), 1.0, 0.0).astype(BF16)
    local = dot(jnp.concatenate(blocks, axis=0).astype(BF16), before, NN)
    running = jnp.zeros((8, 1), F32)
    ranks = []
    for b in range(8):
        ranks.append(local[b * 8:(b + 1) * 8] + running)
        running = running + jnp.sum(blocks[b], axis=1, keepdims=True)
    counts = [running[i:i + 1, :] for i in range(4)]
    ends = []
    total = jnp.zeros((1, 1), F32)
    for i in range(4):
        total = total + (256.0 - counts[i])
        ends.append(total)
    s128 = iota((8, 128), 0)
    base = (s128 * 256).astype(F32)
    positions = []
    for b in range(8):
        sent = jnp.sum(jnp.where(s128 < 4, blocks[b] * (base + ranks[b]), 0.0), axis=0, keepdims=True)
        z = ranks[b][4:5]
        stay = 768.0 + counts[3] + z - ends[2]
        for i in (2, 1, 0):
            start = ends[i - 1] if i else 0.0
            stay = jnp.where(z < ends[i], 256.0 * i + counts[i] + z - start, stay)
        positions.append(sent + blocks[b][4:5] * stay)
    pos = jnp.concatenate(positions, axis=1).astype(jnp.int32)
    src = src_ref[...]
    slot = slot_ref[...]
    values = jnp.where(s8 == 0, src >> 8, jnp.where(s8 == 1, src & 255, jnp.where(s8 == 2, slot >> 8, jnp.where(
        s8 == 3, slot & 255, 0)))).astype(F32)
    pos_high = pos >> 7
    stacked = jnp.concatenate([jnp.where(pos_high == h, values, 0.0) for h in range(8)], axis=0).astype(BF16)
    packed = dot(stacked, one_hot(pos & 127, 128), NT)
    src_packed = jnp.concatenate([packed[h * 8:h * 8 + 1] * 256.0 + packed[h * 8 + 1:h * 8 + 2] for h in range(8)], axis=1)
    slot_high = jnp.concatenate([packed[h * 8 + 2:h * 8 + 3] for h in range(8)], axis=1).astype(jnp.int32)
    slot_low = jnp.concatenate([packed[h * 8 + 3:h * 8 + 4] for h in range(8)], axis=1).astype(jnp.int32)
    slot_packed = slot_high * 256 + slot_low
    tgt = tgt_ref[...]
    table = jnp.concatenate([(tgt >> 8).astype(F32), (tgt & 255).astype(F32)], axis=0).astype(BF16)
    found = dot(table, one_hot(slot_packed & 127, 128), NN)
    chosen = s8 == (slot_packed >> 7)
    tgt_high = jnp.sum(jnp.where(chosen, found[0:8], 0.0), axis=0, keepdims=True)
    tgt_low = jnp.sum(jnp.where(chosen, found[8:16], 0.0), axis=0, keepdims=True)
    tgt_packed = (tgt_high * 256.0 + tgt_low).astype(jnp.int32)
    return src_packed.astype(jnp.int32), tgt_packed, counts


def step_kernel(
    pdfs_hbm, flags_hbm, level_ref, pos_ref, vel_ref, rad_ref, cell_ref, pairs_ref, spring_ref, src_ref, off_ref, slot_ref,
    tgt_ref, mig_ref,
    read_ref, arrived_ref, tgtp_ref, state_ref, newcomers_ref, spring_out_ref,
    pdfs, flags, onehot, moved_in, ext, velf, velb, rows16, edge_x, edge_y, edge_c, halo_x, halo_y, halo_yp, halo_c, splits, gathered,
    received, leaving, joined, fluid, force,
    load_sem, send_sem, recv_sem,
):
    a, b = lax.axis_index("wide"), lax.axis_index("narrow")
    n_wide, n_narrow = lax.axis_size("wide"), lax.axis_size("narrow")

    def device(dx, dy):
        return (lax.rem(a + dx + n_wide, n_wide), lax.rem(b + dy + n_narrow, n_narrow))

    load_p = pltpu.make_async_copy(pdfs_hbm, pdfs, load_sem.at[0])
    load_f = pltpu.make_async_copy(flags_hbm, flags, load_sem.at[1])
    load_p.start()
    load_f.start()
    around = [(dx, dy) for dx in (-1, 0, 1) for dy in (-1, 0, 1) if dx or dy] + [(-2, 0), (2, 0)]
    barrier = pltpu.get_barrier_semaphore()
    for dx, dy in around:
        pl.semaphore_signal(barrier, inc=1, device_id=device(dx, dy), device_id_type=MESH)

    cell = cell_ref[...]
    grain_x = cell >> 10
    fill_one_hot(onehot, cell & 1023)
    drag = drag_coef * rad_ref[...]
    in_row = iota((NX, NYZ), 0) == grain_x
    weights = [drag] + [drag * vel_ref[c:c + 1, :] for c in range(3)]
    for k, weight in enumerate(weights):
        for part, value in enumerate(split2(weight)):
            moved_in[pl.ds((part * 4 + k) * NX, NX), :] = jnp.where(in_row, value, 0.0).astype(BF16)

    @pl.loop(0, 4)
    def _(i):
        cols = pl.ds(pl.multiple_of(i * 256, 256), 256)
        got = dot(moved_in[...], onehot[cols, :], NT)
        force[:, cols] = got[0:128] + got[128:256]

    level = level_ref[0, 0]
    tau = jnp.where(level == 1, tau_fine, tau_coarse).astype(F32)
    omega = jnp.where(level == 1, 1.0 / tau_fine, 1.0 / tau_coarse).astype(F32)
    keep = jnp.where(level == 1, 1.0 - 1.0 / tau_fine, 0.0).astype(F32)
    load_p.wait()

    @pl.loop(0, 32)
    def _(i):
        row = pl.multiple_of((i // 8) * 8, 8)
        rows = pl.ds(row, 8)
        cols = pl.ds(pl.multiple_of((i % 8) * 128, 128), 128)
        p = [pdfs[q, rows, cols] for q in range(19)]
        pair_sum = {q: p[q] + p[q + 1] for q in range(1, 19, 2)}
        pair_dif = {q: p[q] - p[q + 1] for q in range(1, 19, 2)}
        density = p[0] + ((pair_sum[1] + pair_sum[3]) + (pair_sum[5] + pair_sum[7])) + (
            (pair_sum[9] + pair_sum[11]) + (pair_sum[13] + pair_sum[15]) + pair_sum[17])
        mom = (
            (pair_dif[1] + pair_dif[7]) + (pair_dif[9] + pair_dif[11]) + pair_dif[13],
            (pair_dif[3] + pair_dif[7]) + (pair_dif[15] - pair_dif[9]) + pair_dif[17],
            (pair_dif[5] + pair_dif[11]) + (pair_dif[15] - pair_dif[13]) - pair_dif[17],
        )
        inverse = 1.0 / density
        pull = tau * inverse
        resist = force[pl.ds(row, 8), cols]
        shifted = []
        for c in range(3):
            v = mom[c] * inverse
            velf[pl.ds(c * NX + row, 8), cols] = v
            shifted.append(v + pull * (force[pl.ds((c + 1) * NX + row, 8), cols] - v * resist))
        square = 1.5 * (shifted[0] * shifted[0] + shifted[1] * shifted[1] + shifted[2] * shifted[2])
        base = 1.0 - square
        dense = omega * density
        out_rows = pl.ds(TOP + row, 8)
        ext[0, out_rows, cols] = keep * p[0] + (dense * (1.0 / 3.0)) * base
        for q in range(1, 19, 2):
            along = None
            for c in range(3):
                if VELOCITY[q][c] == 1:
                    along = shifted[c] if along is None else along + shifted[c]
                elif VELOCITY[q][c] == -1:
                    along = along - shifted[c]
            scaled = dense * (1.0 / 18.0 if q < 7 else 1.0 / 36.0)
            even = scaled * (base + 4.5 * along * along)
            odd = scaled * (3.0 * along)
            ext[q, out_rows, cols] = keep * p[q] + (even + odd)
            ext[q + 1, out_rows, cols] = keep * p[q + 1] + (even - odd)

    for k in range(5):
        edge_x[0, k:k + 1, :] = ext[X_PLUS[k], TOP + NX - 1:TOP + NX, :]
        edge_x[1, k:k + 1, :] = ext[X_MINUS[k], TOP:TOP + 1, :]
        edge_y[0, k] = ext[Y_PLUS[k], TOP:TOP + NX, 896:1024]
        edge_y[1, k] = ext[Y_MINUS[k], TOP:TOP + NX, 0:128]
    edge_c[0, 0:1, :] = ext[7, TOP + NX - 1:TOP + NX, 896:1024]
    edge_c[1, 0:1, :] = ext[8, TOP:TOP + 1, 0:128]
    edge_c[2, 0:1, :] = ext[9, TOP + NX - 1:TOP + NX, 0:128]
    edge_c[3, 0:1, :] = ext[10, TOP:TOP + 1, 896:1024]
    pl.semaphore_wait(barrier, len(around))

    def send(index, source, target, dx, dy):
        copy = pltpu.make_async_remote_copy(
            src_ref=source, dst_ref=target, send_sem=send_sem.at[index], recv_sem=recv_sem.at[index],
            device_id=device(dx, dy), device_id_type=MESH)
        copy.start()
        return copy

    halo = [
        send(0, edge_x.at[0], halo_x.at[0], 1, 0),
        send(1, edge_x.at[1], halo_x.at[1], -1, 0),
        send(2, edge_y.at[0], halo_y.at[0], 0, 1),
        send(3, edge_y.at[1], halo_y.at[1], 0, -1),
        send(4, edge_c.at[0], halo_c.at[0], 1, 1),
        send(5, edge_c.at[1], halo_c.at[1], -1, -1),
        send(6, edge_c.at[2], halo_c.at[2], 1, -1),
        send(7, edge_c.at[3], halo_c.at[3], -1, 1),
    ]

    for part, value in enumerate(split2(velf[...])):
        velb[pl.ds(part * 96, 96), :] = value.astype(BF16)

    @pl.loop(0, 4)
    def _(i):
        cols = pl.ds(pl.multiple_of(i * 256, 256), 256)
        got = dot(velb[...], onehot[:, cols], NN)
        got = got[0:96] + got[96:192]
        here = iota((NX, 256), 0) == (cell_ref[:, cols] >> 10)
        for c in range(3):
            fluid[c:c + 1, cols] = jnp.sum(jnp.where(here, got[c * NX:(c + 1) * NX], 0.0), axis=0, keepdims=True)

    pair_index = jnp.concatenate([pairs_ref[0:1, :], pairs_ref[1:2, :]], axis=1)
    pair_high = pair_index >> 7
    pair_hot = one_hot(pair_index & 127, 128)
    vel = vel_ref[...]
    rows16[...] = jnp.zeros_like(rows16)
    for part, value in enumerate(split3(vel)):
        rows16[part * 3:part * 3 + 3, 0:NYZ] = value
    table = jnp.concatenate([rows16[:, h * 128:(h + 1) * 128] for h in range(8)], axis=0).astype(BF16)
    found = dot(table, pair_hot, NN)
    at_pair = jnp.where(pair_high == 0, found[0:16], 0.0)
    for h in range(1, 8):
        at_pair = jnp.where(pair_high == h, found[h * 16:(h + 1) * 16], at_pair)
    at_pair = at_pair[0:3] + at_pair[3:6] + at_pair[6:9]
    relative = at_pair[:, 3072:6144] - at_pair[:, 0:3072]
    spring = spring_ref[...]
    spring_out_ref[...] = spring + relative
    contact = spring_coef * spring + dashpot_coef * relative
    for part, value in enumerate(split3(contact)):
        rows16[part * 3:part * 3 + 3, 0:3072] = value
        rows16[part * 3:part * 3 + 3, 3072:6144] = -value
    both = rows16[...]
    spread = jnp.concatenate([jnp.where(pair_high == h, both, 0.0).astype(BF16) for h in range(8)], axis=0)
    summed = dot(spread, pair_hot, NT)
    parts = [summed[h * 16:h * 16 + 3] + summed[h * 16 + 3:h * 16 + 6] + summed[h * 16 + 6:h * 16 + 9] for h in range(8)]
    summed = jnp.concatenate(parts, axis=1)
    radius = rad_ref[...]
    total = (drag_coef * radius) * (fluid[0:3, :] - vel) + summed
    mass = mass_coef * radius * radius * radius
    falling = jnp.where(iota((3, NYZ), 0) == 2, gravity_z, 0.0)
    moved_vel = vel + total / mass + falling
    state_ref[0:3, :] = pos_ref[...] + moved_vel
    state_ref[3:6, :] = moved_vel
    state_ref[6:7, :] = radius
    state_ref[7:8, :] = jnp.ones_like(radius)

    slots = jnp.concatenate([mig_ref[0:1, :], mig_ref[1:2, :]], axis=1)
    mig_hot = one_hot(slots, NYZ)
    state = jnp.concatenate(split3(state_ref[...]), axis=0).astype(BF16)
    out = dot(state, mig_hot, NN)
    leaving[...] = out[0:8] + out[8:16] + out[16:24]
    migrate = [send(8, leaving, joined.at[0], -1, 0), send(9, leaving, joined.at[1], 1, 0)]

    src_packed, tgt_packed, counts = pack_interface(off_ref, slot_ref, src_ref, tgt_ref)
    tgtp_ref[...] = tgt_packed
    fill_one_hot(onehot, src_packed & 1023)

    load_f.wait()
    for copy in halo:
        copy.wait()
    for k in range(5):
        ext[X_PLUS[k], TOP - 1:TOP, :] = halo_x[0, k:k + 1, :]
        ext[X_MINUS[k], TOP + NX:TOP + NX + 1, :] = halo_x[1, k:k + 1, :]
        for side in range(2):
            halo_yp[side, k, TOP:TOP + NX, :] = halo_y[side, k]
    halo_yp[0, 1, TOP - 1:TOP, :] = halo_c[0, 0:1, :]
    halo_yp[1, 1, TOP + NX:TOP + NX + 1, :] = halo_c[1, 0:1, :]
    halo_yp[1, 2, TOP - 1:TOP, :] = halo_c[2, 0:1, :]
    halo_yp[0, 2, TOP + NX:TOP + NX + 1, :] = halo_c[3, 0:1, :]
    lane = iota((NX, 128), 1)
    for q in range(19):
        cx, cy, cz = VELOCITY[q]
        shift = cy * 32 + cz
        rows = slice(TOP - cx, TOP - cx + NX)
        value = ext[q, rows, :]
        if shift:
            value = pltpu.roll(value, shift % NYZ, 1)
        if cy == 1:
            edge = pltpu.roll(halo_yp[0, Y_PLUS.index(q), rows, :], shift % 128, 1)
            value = jnp.concatenate([jnp.where(lane < 32, edge, value[:, 0:128]), value[:, 128:]], axis=1)
        if cy == -1:
            edge = halo_yp[1, Y_MINUS.index(q), rows, :]
            edge = pltpu.roll(edge, shift % 128, 1)
            value = jnp.concatenate([value[:, :896], jnp.where(lane >= 96, edge, value[:, 896:])], axis=1)
        if q:
            bit = 1 << (q if q < 10 else q - 10)
            solid = (flags[0 if q < 10 else 1] & bit) != 0
            value = jnp.where(solid, ext[OPPOSITE[q], TOP:TOP + NX, :], value)
        read_ref[q] = value
        high, low = split2(value)
        splits[pl.ds(q * NX, NX), :] = high.astype(BF16)
        splits[pl.ds((19 + q) * NX, NX), :] = low.astype(BF16)

    rows_out = []
    for i in range(4):
        cols = slice(i * 256, (i + 1) * 256)
        got = dot(splits[...], onehot[:, cols], NN)
        here = iota((NX, 256), 0) == (src_packed[:, cols] >> 10)
        for q in range(19):
            both_parts = got[q * NX:(q + 1) * NX] + got[(19 + q) * NX:(20 + q) * NX]
            gathered[i, q:q + 1, :] = jnp.sum(jnp.where(here, both_parts, 0.0), axis=0, keepdims=True)
        rows_out.append(send(10 + i, gathered.at[i], received.at[i], DISTANCE[i], 0))

    for copy in migrate:
        copy.wait()
    mig_lane = iota((8, 128), 1)
    change = jnp.where(iota((8, 128), 0) == 0, jnp.where(mig_lane < 64, float(NX), -float(NX)), 0.0)
    newcomers_ref[...] = jnp.where(mig_lane < 64, joined[0], joined[1]) + change
    for i in range(4):
        rows_out[i].wait()
        stays = iota((24, 256), 1).astype(F32) >= counts[i]
        arrived_ref[:, i * 256:(i + 1) * 256] = jnp.where(stays, gathered[i], received[i])


def finish_kernel(
    read_ref, arrived_ref, tgtp_ref, state_ref, newcomers_ref, mig_ref, spring_ref,
    next_ref, pos_ref, vel_ref, rad_ref, spring_out_ref,
    spread,
):
    step = pl.program_id(0)
    target = tgtp_ref[...]

    @pl.when(step == 0)
    def _():
        here = iota((NX, NYZ), 0) == (target >> 10)
        for q in range(19):
            for part, value in enumerate(split2(arrived_ref[q:q + 1, :])):
                spread[pl.ds((part * 19 + q) * NX, NX), :] = jnp.where(here, value, 0.0).astype(BF16)
        spread[pl.ds(38 * NX, NX), :] = jnp.where(here, 1.0, 0.0).astype(BF16)
        slots = jnp.concatenate([mig_ref[0:1, :], mig_ref[1:2, :]], axis=1)
        mig_hot = one_hot(slots, NYZ)
        arrived = jnp.concatenate(split3(newcomers_ref[...]), axis=0).astype(BF16)
        placed = dot(arrived, mig_hot, NT)
        placed = placed[0:8] + placed[8:16] + placed[16:24]
        result = jnp.where(placed[7:8] > 0.5, placed, state_ref[...])
        pos_ref[...] = result[0:3]
        vel_ref[...] = result[3:6]
        rad_ref[...] = result[6:7]
        spring_out_ref[...] = spring_ref[...]

    hot = one_hot(target & 1023, 256, step * 256)
    got = dot(spread[...], hot, NT)
    hit = got[38 * NX:39 * NX] > 0.5
    for q in range(19):
        value = read_ref[q]
        carried = got[q * NX:(q + 1) * NX] + got[(19 + q) * NX:(20 + q) * NX]
        next_ref[q] = jnp.where(hit, blend_coef * (value + carried), value)


def shards(
    pdfs, link_flags, block_level, grain_pos, grain_vel, grain_radius, grain_cell, contact_pairs, contact_spring, iface_source,
    iface_offset, iface_slot, iface_target, migrant_slots,
):
    row = (1, NYZ)
    vmem = pl.BlockSpec(memory_space=pltpu.VMEM)
    hbm = pl.BlockSpec(memory_space=pl.ANY)
    outs = pl.pallas_call(
        step_kernel,
        name="step",
        out_shape=(
            jax.ShapeDtypeStruct((19, NX, NYZ), F32),
            jax.ShapeDtypeStruct((24, NYZ), F32),
            jax.ShapeDtypeStruct(row, jnp.int32),
            jax.ShapeDtypeStruct((8, NYZ), F32),
            jax.ShapeDtypeStruct((8, 128), F32),
            jax.ShapeDtypeStruct((3, 3072), F32),
        ),
        in_specs=[hbm, hbm, pl.BlockSpec(memory_space=pltpu.SMEM)] + [vmem] * 11,
        out_specs=(vmem,) * 6,
        scratch_shapes=[
            pltpu.VMEM((19, NX, NYZ), F32),
            pltpu.VMEM((2, NX, NYZ), jnp.int32),
            pltpu.VMEM((NYZ, NYZ), BF16),
            pltpu.VMEM((8 * NX, NYZ), BF16),
            pltpu.VMEM((19, EXT, NYZ), F32),
            pltpu.VMEM((3 * NX, NYZ), F32),
            pltpu.VMEM((6 * NX, NYZ), BF16),
            pltpu.VMEM((16, 6144), F32),
            pltpu.VMEM((2, 8, NYZ), F32),
            pltpu.VMEM((2, 5, NX, 128), F32),
            pltpu.VMEM((4, 8, 128), F32),
            pltpu.VMEM((2, 8, NYZ), F32),
            pltpu.VMEM((2, 5, NX, 128), F32),
            pltpu.VMEM((2, 5, EXT, 128), F32),
            pltpu.VMEM((4, 8, 128), F32),
            pltpu.VMEM((38 * NX, NYZ), BF16),
            pltpu.VMEM((4, 24, 256), F32),
            pltpu.VMEM((4, 24, 256), F32),
            pltpu.VMEM((8, 128), F32),
            pltpu.VMEM((2, 8, 128), F32),
            pltpu.VMEM((8, NYZ), F32),
            pltpu.VMEM((4 * NX, NYZ), F32),
            pltpu.SemaphoreType.DMA((2,)),
            pltpu.SemaphoreType.DMA((14,)),
            pltpu.SemaphoreType.DMA((14,)),
        ],
        compiler_params=pltpu.CompilerParams(collective_id=0, has_side_effects=True, vmem_limit_bytes=56 << 20),
    )(
        pdfs, link_flags, block_level, grain_pos, grain_vel, grain_radius.reshape(row), grain_cell.reshape(row), contact_pairs,
        contact_spring, iface_source.reshape(row), iface_offset.reshape(row), iface_slot.reshape(row),
        iface_target.reshape(8, 128), migrant_slots,
    )
    read, arrived, tgtp, state, newcomers, spring_next = outs

    def whole(shape):
        return pl.BlockSpec(shape, lambda i: (0,) * len(shape))

    block = pl.BlockSpec((19, NX, 256), lambda i: (0, 0, i))
    result = pl.pallas_call(
        finish_kernel,
        name="finish",
        grid=(4,),
        out_shape=(
            jax.ShapeDtypeStruct((19, NX, NYZ), F32),
            jax.ShapeDtypeStruct((3, NYZ), F32),
            jax.ShapeDtypeStruct((3, NYZ), F32),
            jax.ShapeDtypeStruct(row, F32),
            jax.ShapeDtypeStruct((3, 3072), F32),
        ),
        in_specs=[block, whole((24, NYZ)), whole(row), whole((8, NYZ)), whole((8, 128)), whole((2, 64)), whole((3, 3072))],
        out_specs=(block, whole((3, NYZ)), whole((3, NYZ)), whole(row), whole((3, 3072))),
        scratch_shapes=[pltpu.VMEM((39 * NX, NYZ), BF16)],
        compiler_params=pltpu.CompilerParams(dimension_semantics=("arbitrary",), vmem_limit_bytes=40 << 20),
    )(read, arrived, tgtp, state, newcomers, migrant_slots, spring_next)
    pdfs_next, pos_next, vel_next, rad_next, spring_out = result
    return pdfs_next, pos_next, vel_next, rad_next.reshape(NYZ), spring_out


def solution(mesh):
    both = ("wide", "narrow")
    in_specs = (
        P(None, "wide", "narrow"), P(None, "wide", "narrow"), P("wide", "narrow"), P(None, both), P(None, both), P(both), P(both),
        P(None, both), P(None, both), P(both), P(), P(), P(both), P(None, both),
    )
    out_specs = (P(None, "wide", "narrow"), P(None, both), P(None, both), P(both), P(None, both))
    return jax.shard_map(shards, mesh=mesh, in_specs=in_specs, out_specs=out_specs, check_vma=False)
```

```python
import functools

import jax
import jax.numpy as jnp
from jax import lax
from jax.experimental import pallas as pl
from jax.experimental.pallas import tpu as pltpu
from jax.sharding import PartitionSpec as P

VELOCITY = (
    (0, 0, 0), (1, 0, 0), (-1, 0, 0), (0, 1, 0), (0, -1, 0), (0, 0, 1), (0, 0, -1),
    (1, 1, 0), (-1, -1, 0), (1, -1, 0), (-1, 1, 0), (1, 0, 1), (-1, 0, -1), (1, 0, -1),
    (-1, 0, 1), (0, 1, 1), (0, -1, -1), (0, 1, -1), (0, -1, 1),
)
OPPOSITE = (0, 2, 1, 4, 3, 6, 5, 8, 7, 10, 9, 12, 11, 14, 13, 16, 15, 18, 17)
tau_coarse = 1.0
tau_fine = 1.5
drag_coef = 0.5
mass_coef = 10.0
spring_coef = 0.2
dashpot_coef = 0.05
gravity_z = -0.01
blend_coef = 0.5

NX = 32
NYZ = 1024
TOP = 8
EXT = NX + 16
X_PLUS = (1, 7, 9, 11, 13)
X_MINUS = (2, 8, 10, 12, 14)
Y_PLUS = (3, 7, 10, 15, 17)
Y_MINUS = (4, 8, 9, 16, 18)
DISTANCE = (-2, 2, -1, 1)
MESH = pl.DeviceIdType.MESH
F32 = jnp.float32
BF16 = jnp.bfloat16
NT = (((1,), (1,)), ((), ()))
NN = (((1,), (0,)), ((), ()))


def iota(shape, axis):
    return lax.broadcasted_iota(jnp.int32, shape, axis)


def split2(value):
    high = value.astype(BF16).astype(F32)
    return high, value - high


def split3(value):
    high = value.astype(BF16).astype(F32)
    rest = value - high
    middle = rest.astype(BF16).astype(F32)
    return high, middle, rest - middle


def one_hot(row, size, start=0):
    lanes = row.shape[1]
    return jnp.where(iota((size, lanes), 0) + start == row, 1.0, 0.0).astype(BF16)


def fill_one_hot(ref, row):
    for start in range(0, NYZ, 128):
        ref[start:start + 128, :] = one_hot(row, 128, start)


def dot(a, b, dims):
    return lax.dot_general(a, b, dims, preferred_element_type=F32)


def pack_interface(off_ref, slot_ref, src_ref, tgt_ref):
    off = off_ref[...]
    s8 = iota((8, NYZ), 0)
    dval = jnp.where(s8 == 0, DISTANCE[0], jnp.where(s8 == 1, DISTANCE[1], jnp.where(s8 == 2, DISTANCE[2], jnp.where(
        s8 == 3, DISTANCE[3], jnp.where(s8 == 4, 0, 99)))))
    member = jnp.where(off == dval, 1.0, 0.0)
    blocks = [member[:, b * 128:(b + 1) * 128] for b in range(8)]
    before = jnp.where(iota((128, 128), 0) < iota((128, 128), 1), 1.0, 0.0).astype(BF16)
    local = dot(jnp.concatenate(blocks, axis=0).astype(BF16), before, NN)
    running = jnp.zeros((8, 1), F32)
    ranks = []
    for b in range(8):
        ranks.append(local[b * 8:(b + 1) * 8] + running)
        running = running + jnp.sum(blocks[b], axis=1, keepdims=True)
    counts = [running[i:i + 1, :] for i in range(4)]
    ends = []
    total = jnp.zeros((1, 1), F32)
    for i in range(4):
        total = total + (256.0 - counts[i])
        ends.append(total)
    s128 = iota((8, 128), 0)
    base = (s128 * 256).astype(F32)
    positions = []
    for b in range(8):
        sent = jnp.sum(jnp.where(s128 < 4, blocks[b] * (base + ranks[b]), 0.0), axis=0, keepdims=True)
        z = ranks[b][4:5]
        stay = 768.0 + counts[3] + z - ends[2]
        for i in (2, 1, 0):
            start = ends[i - 1] if i else 0.0
            stay = jnp.where(z < ends[i], 256.0 * i + counts[i] + z - start, stay)
        positions.append(sent + blocks[b][4:5] * stay)
    pos = jnp.concatenate(positions, axis=1).astype(jnp.int32)
    src = src_ref[...]
    slot = slot_ref[...]
    values = jnp.where(s8 == 0, src >> 8, jnp.where(s8 == 1, src & 255, jnp.where(s8 == 2, slot >> 8, jnp.where(
        s8 == 3, slot & 255, 0)))).astype(F32)
    pos_high = pos >> 7
    stacked = jnp.concatenate([jnp.where(pos_high == h, values, 0.0) for h in range(8)], axis=0).astype(BF16)
    packed = dot(stacked, one_hot(pos & 127, 128), NT)
    src_packed = jnp.concatenate([packed[h * 8:h * 8 + 1] * 256.0 + packed[h * 8 + 1:h * 8 + 2] for h in range(8)], axis=1)
    slot_high = jnp.concatenate([packed[h * 8 + 2:h * 8 + 3] for h in range(8)], axis=1).astype(jnp.int32)
    slot_low = jnp.concatenate([packed[h * 8 + 3:h * 8 + 4] for h in range(8)], axis=1).astype(jnp.int32)
    slot_packed = slot_high * 256 + slot_low
    tgt = tgt_ref[...]
    table = jnp.concatenate([(tgt >> 8).astype(F32), (tgt & 255).astype(F32)], axis=0).astype(BF16)
    found = dot(table, one_hot(slot_packed & 127, 128), NN)
    chosen = s8 == (slot_packed >> 7)
    tgt_high = jnp.sum(jnp.where(chosen, found[0:8], 0.0), axis=0, keepdims=True)
    tgt_low = jnp.sum(jnp.where(chosen, found[8:16], 0.0), axis=0, keepdims=True)
    tgt_packed = (tgt_high * 256.0 + tgt_low).astype(jnp.int32)
    return src_packed.astype(jnp.int32), tgt_packed, counts


def step_kernel(
    pdfs_hbm, flags_hbm, level_ref, pos_hbm, vel_hbm, rad_hbm, cell_hbm, pairs_hbm, spring_hbm, src_hbm, off_hbm, slot_hbm,
    tgt_hbm, mig_hbm,
    read_ref, arrived_ref, tgtp_ref, state_ref, newcomers_ref, spring_out_ref,
    pdfs, flags, pos_ref, vel_ref, rad_ref, cell_ref, pairs_ref, spring_ref, src_ref, off_ref, slot_ref, tgt_ref,
    mig_ref,
    onehot, source_hot, moved_in, ext, velf, velb, vel8, rows16, edge_x, edge_y, edge_c, halo_x, halo_y, halo_yp, halo_c, splits,
    gathered, received, leaving, joined, fluid, force,
    load_sem, send_sem, recv_sem,
):
    a, b = lax.axis_index("wide"), lax.axis_index("narrow")
    n_wide, n_narrow = lax.axis_size("wide"), lax.axis_size("narrow")

    def device(dx, dy):
        return (lax.rem(a + dx + n_wide, n_wide), lax.rem(b + dy + n_narrow, n_narrow))

    pairs_of = [
        (cell_hbm, cell_ref), (off_hbm, off_ref), (slot_hbm, slot_ref), (src_hbm, src_ref), (tgt_hbm, tgt_ref),
        (rad_hbm, rad_ref), (vel_hbm, vel_ref), (mig_hbm, mig_ref), (pdfs_hbm, pdfs),
        (pairs_hbm, pairs_ref), (pos_hbm, pos_ref), (spring_hbm, spring_ref), (flags_hbm, flags),
    ]
    loads = [pltpu.make_async_copy(x, y, load_sem.at[i]) for i, (x, y) in enumerate(pairs_of)]
    for load in loads:
        load.start()
    around = [(dx, dy) for dx in (-1, 0, 1) for dy in (-1, 0, 1) if dx or dy] + [(-2, 0), (2, 0)]
    barrier = pltpu.get_barrier_semaphore()
    for dx, dy in around:
        pl.semaphore_signal(barrier, inc=1, device_id=device(dx, dy), device_id_type=MESH)
    for load in loads[:8]:
        load.wait()

    src_packed, tgt_packed, counts = pack_interface(off_ref, slot_ref, src_ref, tgt_ref)
    tgtp_ref[...] = tgt_packed

    cell = cell_ref[...]
    grain_x = cell >> 10
    fill_one_hot(onehot, cell & 1023)
    drag = drag_coef * rad_ref[...]
    in_row = iota((NX, NYZ), 0) == grain_x
    weights = [drag] + [drag * vel_ref[c:c + 1, :] for c in range(3)]
    for k, weight in enumerate(weights):
        for part, value in enumerate(split2(weight)):
            moved_in[(part * 4 + k) * NX:(part * 4 + k + 1) * NX, :] = jnp.where(in_row, value, 0.0).astype(BF16)
    fill_one_hot(source_hot, src_packed & 1023)

    fine = level_ref[0, 0] == 1
    tau = jnp.where(fine, tau_fine, tau_coarse).astype(F32)
    omega = jnp.where(fine, 1.0 / tau_fine, 1.0 / tau_coarse).astype(F32)
    keep = jnp.where(fine, 1.0 - 1.0 / tau_fine, 0.0).astype(F32)

    def bring(i):
        cols = slice(i * 256, (i + 1) * 256)
        got = dot(moved_in[...], onehot[cols, :], NT)
        force[:, cols] = got[0:128] + got[128:256]

    def collide(row, col):
        rows = slice(row, row + 8)
        cols = slice(col, col + 128)
        p = [pdfs[q, rows, cols] for q in range(19)]
        pair_sum = {q: p[q] + p[q + 1] for q in range(1, 19, 2)}
        pair_dif = {q: p[q] - p[q + 1] for q in range(1, 19, 2)}
        density = p[0] + ((pair_sum[1] + pair_sum[3]) + (pair_sum[5] + pair_sum[7])) + (
            (pair_sum[9] + pair_sum[11]) + (pair_sum[13] + pair_sum[15]) + pair_sum[17])
        mom = (
            (pair_dif[1] + pair_dif[7]) + (pair_dif[9] + pair_dif[11]) + pair_dif[13],
            (pair_dif[3] + pair_dif[7]) + (pair_dif[15] - pair_dif[9]) + pair_dif[17],
            (pair_dif[5] + pair_dif[11]) + (pair_dif[15] - pair_dif[13]) - pair_dif[17],
        )
        inverse = 1.0 / density
        pull = tau * inverse
        resist = force[rows, cols]
        shifted = []
        for c in range(3):
            v = mom[c] * inverse
            velf[c * NX + row:c * NX + row + 8, cols] = v
            shifted.append(v + pull * (force[(c + 1) * NX + row:(c + 1) * NX + row + 8, cols] - v * resist))
        square = 1.5 * (shifted[0] * shifted[0] + shifted[1] * shifted[1] + shifted[2] * shifted[2])
        base = 1.0 - square
        dense = omega * density
        wide = dense * (1.0 / 18.0)
        slim = dense * (1.0 / 36.0)
        out_rows = slice(TOP + row, TOP + row + 8)
        ext[0, out_rows, cols] = keep * p[0] + (dense * (1.0 / 3.0)) * base
        for q in range(1, 19, 2):
            along = None
            for c in range(3):
                if VELOCITY[q][c] == 1:
                    along = shifted[c] if along is None else along + shifted[c]
                elif VELOCITY[q][c] == -1:
                    along = along - shifted[c]
            scaled = wide if q < 7 else slim
            even = scaled * (base + 4.5 * along * along)
            odd = scaled * (3.0 * along)
            ext[q, out_rows, cols] = keep * p[q] + (even + odd)
            ext[q + 1, out_rows, cols] = keep * p[q + 1] + (even - odd)

    bring(0)
    loads[8].wait()
    for i in range(4):
        if i < 3:
            bring(i + 1)
        for col in (i * 256, i * 256 + 128):
            for row in range(0, NX, 8):
                collide(row, col)

    for k in range(5):
        edge_x[0, k:k + 1, :] = ext[X_PLUS[k], TOP + NX - 1:TOP + NX, :]
        edge_x[1, k:k + 1, :] = ext[X_MINUS[k], TOP:TOP + 1, :]
        edge_y[0, k] = ext[Y_PLUS[k], TOP:TOP + NX, 896:1024]
        edge_y[1, k] = ext[Y_MINUS[k], TOP:TOP + NX, 0:128]
    edge_c[0, 0:1, :] = ext[7, TOP + NX - 1:TOP + NX, 896:1024]
    edge_c[1, 0:1, :] = ext[8, TOP:TOP + 1, 0:128]
    edge_c[2, 0:1, :] = ext[9, TOP + NX - 1:TOP + NX, 0:128]
    edge_c[3, 0:1, :] = ext[10, TOP:TOP + 1, 896:1024]
    pl.semaphore_wait(barrier, len(around))

    def send(index, source, target, dx, dy):
        copy = pltpu.make_async_remote_copy(
            src_ref=source, dst_ref=target, send_sem=send_sem.at[index], recv_sem=recv_sem.at[index],
            device_id=device(dx, dy), device_id_type=MESH)
        copy.start()
        return copy

    halo = [
        send(0, edge_x.at[0], halo_x.at[0], 1, 0),
        send(1, edge_x.at[1], halo_x.at[1], -1, 0),
        send(2, edge_y.at[0], halo_y.at[0], 0, 1),
        send(3, edge_y.at[1], halo_y.at[1], 0, -1),
        send(4, edge_c.at[0], halo_c.at[0], 1, 1),
        send(5, edge_c.at[1], halo_c.at[1], -1, -1),
        send(6, edge_c.at[2], halo_c.at[2], 1, -1),
        send(7, edge_c.at[3], halo_c.at[3], -1, 1),
    ]

    for part, value in enumerate(split2(velf[...])):
        velb[part * 96:part * 96 + 96, :] = value.astype(BF16)
    for i in range(4):
        cols = slice(i * 256, (i + 1) * 256)
        got = dot(velb[...], onehot[:, cols], NN)
        got = got[0:96] + got[96:192]
        here = iota((NX, 256), 0) == (cell_ref[:, cols] >> 10)
        for c in range(3):
            fluid[c:c + 1, cols] = jnp.sum(jnp.where(here, got[c * NX:(c + 1) * NX], 0.0), axis=0, keepdims=True)

    for load in loads[9:]:
        load.wait()
    for copy in halo:
        copy.wait()
    for k in range(5):
        ext[X_PLUS[k], TOP - 1:TOP, :] = halo_x[0, k:k + 1, :]
        ext[X_MINUS[k], TOP + NX:TOP + NX + 1, :] = halo_x[1, k:k + 1, :]
        for side in range(2):
            halo_yp[side, k, TOP:TOP + NX, :] = halo_y[side, k]
    halo_yp[0, 1, TOP - 1:TOP, :] = halo_c[0, 0:1, :]
    halo_yp[1, 1, TOP + NX:TOP + NX + 1, :] = halo_c[1, 0:1, :]
    halo_yp[1, 2, TOP - 1:TOP, :] = halo_c[2, 0:1, :]
    halo_yp[0, 2, TOP + NX:TOP + NX + 1, :] = halo_c[3, 0:1, :]
    lane = iota((NX, 128), 1)
    for q in range(19):
        cx, cy, cz = VELOCITY[q]
        shift = cy * 32 + cz
        rows = slice(TOP - cx, TOP - cx + NX)
        value = ext[q, rows, :]
        if shift:
            value = pltpu.roll(value, shift % NYZ, 1)
        if cy == 1:
            edge = pltpu.roll(halo_yp[0, Y_PLUS.index(q), rows, :], shift % 128, 1)
            value = jnp.concatenate([jnp.where(lane < 32, edge, value[:, 0:128]), value[:, 128:]], axis=1)
        if cy == -1:
            edge = halo_yp[1, Y_MINUS.index(q), rows, :]
            edge = pltpu.roll(edge, shift % 128, 1)
            value = jnp.concatenate([value[:, :896], jnp.where(lane >= 96, edge, value[:, 896:])], axis=1)
        if q:
            bit = 1 << (q if q < 10 else q - 10)
            solid = (flags[0 if q < 10 else 1] & bit) != 0
            value = jnp.where(solid, ext[OPPOSITE[q], TOP:TOP + NX, :], value)
        read_ref[q] = value
        high, low = split2(value)
        splits[q * NX:q * NX + NX, :] = high.astype(BF16)
        splits[(19 + q) * NX:(19 + q) * NX + NX, :] = low.astype(BF16)

    def extract(i):
        cols = slice(i * 256, (i + 1) * 256)
        got = dot(splits[...], source_hot[:, cols], NN)
        here = iota((NX, 256), 0) == (src_packed[:, cols] >> 10)
        for q in range(19):
            both_parts = got[q * NX:(q + 1) * NX] + got[(19 + q) * NX:(20 + q) * NX]
            gathered[i, q:q + 1, :] = jnp.sum(jnp.where(here, both_parts, 0.0), axis=0, keepdims=True)

    def contacts_in():
        vel8[...] = jnp.zeros_like(vel8)
        vel8[0:3, :] = vel_ref[...]
        vel8[4:7, :] = vel_ref[...]
        tables = [vel8[:, h * 128:(h + 1) * 128] for h in range(8)]
        half = iota((8, 128), 0) < 4
        for c in range(24):
            cols = slice(c * 128, (c + 1) * 128)
            index = jnp.where(half, pairs_ref[0:1, cols], pairs_ref[1:2, cols])
            low = index & 127
            high = index >> 7
            found = jnp.take_along_axis(tables[0], low, axis=1, mode="promise_in_bounds")
            for h in range(1, 8):
                found = jnp.where(high == h, jnp.take_along_axis(tables[h], low, axis=1, mode="promise_in_bounds"), found)
            relative = found[4:7] - found[0:3]
            spring = spring_ref[:, cols]
            spring_out_ref[:, cols] = spring + relative
            contact = spring_coef * spring + dashpot_coef * relative
            for part, value in enumerate(split3(contact)):
                rows16[part * 3:part * 3 + 3, cols] = value

    def contacts_out():
        rows16[9:16, :] = jnp.zeros((7, 3072), F32)
        forces = rows16[...]
        spread = []
        hots = []
        for side in range(2):
            index = pairs_ref[side:side + 1, :]
            high = index >> 7
            signed = -forces if side else forces
            spread.append(jnp.concatenate([jnp.where(high == h, signed, 0.0).astype(BF16) for h in range(8)], axis=0))
            hots.append(one_hot(index & 127, 128))
        summed = dot(jnp.concatenate(spread, axis=1), jnp.concatenate(hots, axis=1), NT)
        parts = [
            summed[h * 16:h * 16 + 3] + summed[h * 16 + 3:h * 16 + 6] + summed[h * 16 + 6:h * 16 + 9] for h in range(8)]
        return jnp.concatenate(parts, axis=1)

    def move_grains(summed):
        radius = rad_ref[...]
        vel = vel_ref[...]
        total = (drag_coef * radius) * (fluid[0:3, :] - vel) + summed
        mass = mass_coef * radius * radius * radius
        falling = jnp.where(iota((3, NYZ), 0) == 2, gravity_z, 0.0)
        moved_vel = vel + total / mass + falling
        state_ref[0:3, :] = pos_ref[...] + moved_vel
        state_ref[3:6, :] = moved_vel
        state_ref[6:7, :] = radius
        state_ref[7:8, :] = jnp.ones_like(radius)

    def leave():
        slots = jnp.concatenate([mig_ref[0:1, :], mig_ref[1:2, :]], axis=1)
        state = jnp.concatenate(split3(state_ref[...]), axis=0).astype(BF16)
        out = dot(state, one_hot(slots, NYZ), NN)
        leaving[...] = out[0:8] + out[8:16] + out[16:24]

    rows_out = []

    def send_region(i):
        rows_out.append(send(10 + i, gathered.at[i], received.at[i], DISTANCE[i], 0))

    extract(0)
    contacts_in()
    send_region(0)
    extract(1)
    summed = contacts_out()
    send_region(1)
    extract(2)
    move_grains(summed)
    leave()
    migrate = [send(8, leaving, joined.at[0], -1, 0), send(9, leaving, joined.at[1], 1, 0)]
    send_region(2)
    extract(3)
    send_region(3)

    for copy in migrate:
        copy.wait()
    mig_lane = iota((8, 128), 1)
    change = jnp.where(iota((8, 128), 0) == 0, jnp.where(mig_lane < 64, float(NX), -float(NX)), 0.0)
    newcomers_ref[...] = jnp.where(mig_lane < 64, joined[0], joined[1]) + change
    for i in range(4):
        rows_out[i].wait()
        stays = iota((24, 256), 1).astype(F32) >= counts[i]
        arrived_ref[:, i * 256:(i + 1) * 256] = jnp.where(stays, gathered[i], received[i])


def finish_kernel(
    read_ref, arrived_ref, tgtp_ref, state_ref, newcomers_ref, mig_ref, spring_ref,
    next_ref, pos_ref, vel_ref, rad_ref, spring_out_ref,
    spread,
):
    step = pl.program_id(0)
    target = tgtp_ref[...]

    @pl.when(step == 0)
    def _():
        here = iota((NX, NYZ), 0) == (target >> 10)
        for q in range(19):
            for part, value in enumerate(split2(arrived_ref[q:q + 1, :])):
                spread[pl.ds((part * 19 + q) * NX, NX), :] = jnp.where(here, value, 0.0).astype(BF16)
        spread[pl.ds(38 * NX, NX), :] = jnp.where(here, 1.0, 0.0).astype(BF16)
        slots = jnp.concatenate([mig_ref[0:1, :], mig_ref[1:2, :]], axis=1)
        mig_hot = one_hot(slots, NYZ)
        arrived = jnp.concatenate(split3(newcomers_ref[...]), axis=0).astype(BF16)
        placed = dot(arrived, mig_hot, NT)
        placed = placed[0:8] + placed[8:16] + placed[16:24]
        result = jnp.where(placed[7:8] > 0.5, placed, state_ref[...])
        pos_ref[...] = result[0:3]
        vel_ref[...] = result[3:6]
        rad_ref[...] = result[6:7]
        spring_out_ref[...] = spring_ref[...]

    cols = pl.ds(pl.multiple_of(step * 256, 256), 256)
    hot = one_hot(target & 1023, 256, step * 256)
    got = dot(spread[...], hot, NT)
    hit = got[38 * NX:39 * NX] > 0.5
    for q in range(19):
        value = read_ref[q, :, cols]
        carried = got[q * NX:(q + 1) * NX] + got[(19 + q) * NX:(20 + q) * NX]
        next_ref[q] = jnp.where(hit, blend_coef * (value + carried), value)


def shards(
    pdfs, link_flags, block_level, grain_pos, grain_vel, grain_radius, grain_cell, contact_pairs, contact_spring, iface_source,
    iface_offset, iface_slot, iface_target, migrant_slots,
):
    row = (1, NYZ)
    vmem = pl.BlockSpec(memory_space=pltpu.VMEM)
    hbm = pl.BlockSpec(memory_space=pl.ANY)
    outs = pl.pallas_call(
        step_kernel,
        name="step",
        out_shape=(
            pltpu.VMEM((19, NX, NYZ), F32),
            pltpu.VMEM((24, NYZ), F32),
            pltpu.VMEM(row, jnp.int32),
            pltpu.VMEM((8, NYZ), F32),
            pltpu.VMEM((8, 128), F32),
            pltpu.VMEM((3, 3072), F32),
        ),
        in_specs=[hbm] * 2 + [pl.BlockSpec(memory_space=pltpu.SMEM)] + [hbm] * 11,
        out_specs=(vmem,) * 6,
        scratch_shapes=[
            pltpu.VMEM((19, NX, NYZ), F32),
            pltpu.VMEM((2, NX, NYZ), jnp.int32),
            pltpu.VMEM((3, NYZ), F32),
            pltpu.VMEM((3, NYZ), F32),
            pltpu.VMEM(row, F32),
            pltpu.VMEM(row, jnp.int32),
            pltpu.VMEM((2, 3072), jnp.int32),
            pltpu.VMEM((3, 3072), F32),
            pltpu.VMEM(row, jnp.int32),
            pltpu.VMEM(row, jnp.int32),
            pltpu.VMEM(row, jnp.int32),
            pltpu.VMEM((8, 128), jnp.int32),
            pltpu.VMEM((2, 64), jnp.int32),
            pltpu.VMEM((NYZ, NYZ), BF16),
            pltpu.VMEM((NYZ, NYZ), BF16),
            pltpu.VMEM((8 * NX, NYZ), BF16),
            pltpu.VMEM((19, EXT, NYZ), F32),
            pltpu.VMEM((3 * NX, NYZ), F32),
            pltpu.VMEM((6 * NX, NYZ), BF16),
            pltpu.VMEM((8, NYZ), F32),
            pltpu.VMEM((16, 3072), F32),
            pltpu.VMEM((2, 8, NYZ), F32),
            pltpu.VMEM((2, 5, NX, 128), F32),
            pltpu.VMEM((4, 8, 128), F32),
            pltpu.VMEM((2, 8, NYZ), F32),
            pltpu.VMEM((2, 5, NX, 128), F32),
            pltpu.VMEM((2, 5, EXT, 128), F32),
            pltpu.VMEM((4, 8, 128), F32),
            pltpu.VMEM((38 * NX, NYZ), BF16),
            pltpu.VMEM((4, 24, 256), F32),
            pltpu.VMEM((4, 24, 256), F32),
            pltpu.VMEM((8, 128), F32),
            pltpu.VMEM((2, 8, 128), F32),
            pltpu.VMEM((8, NYZ), F32),
            pltpu.VMEM((4 * NX, NYZ), F32),
            pltpu.SemaphoreType.DMA((14,)),
            pltpu.SemaphoreType.DMA((14,)),
            pltpu.SemaphoreType.DMA((14,)),
        ],
        compiler_params=pltpu.CompilerParams(collective_id=0, has_side_effects=True, vmem_limit_bytes=64_300_000),
    )(
        pdfs, link_flags, block_level, grain_pos, grain_vel, grain_radius.reshape(row), grain_cell.reshape(row), contact_pairs,
        contact_spring, iface_source.reshape(row), iface_offset.reshape(row), iface_slot.reshape(row),
        iface_target.reshape(8, 128), migrant_slots,
    )
    read, arrived, tgtp, state, newcomers, spring_next = outs

    def whole(shape):
        return pl.BlockSpec(shape, lambda i: (0,) * len(shape))

    block = pl.BlockSpec((19, NX, 256), lambda i: (0, 0, i))
    result = pl.pallas_call(
        finish_kernel,
        name="finish",
        grid=(4,),
        out_shape=(
            jax.ShapeDtypeStruct((19, NX, NYZ), F32),
            jax.ShapeDtypeStruct((3, NYZ), F32),
            jax.ShapeDtypeStruct((3, NYZ), F32),
            jax.ShapeDtypeStruct(row, F32),
            jax.ShapeDtypeStruct((3, 3072), F32),
        ),
        in_specs=[vmem] * 7,
        out_specs=(block, whole((3, NYZ)), whole((3, NYZ)), whole(row), whole((3, 3072))),
        scratch_shapes=[pltpu.VMEM((39 * NX, NYZ), BF16)],
        compiler_params=pltpu.CompilerParams(dimension_semantics=("arbitrary",), vmem_limit_bytes=40 << 20),
    )(read, arrived, tgtp, state, newcomers, migrant_slots, spring_next)
    pdfs_next, pos_next, vel_next, rad_next, spring_out = result
    return pdfs_next, pos_next, vel_next, rad_next.reshape(NYZ), spring_out


def solution(mesh):
    both = ("wide", "narrow")
    in_specs = (
        P(None, "wide", "narrow"), P(None, "wide", "narrow"), P("wide", "narrow"), P(None, both), P(None, both), P(both), P(both),
        P(None, both), P(None, both), P(both), P(), P(), P(both), P(None, both),
    )
    out_specs = (P(None, "wide", "narrow"), P(None, both), P(None, both), P(both), P(None, both))
    return jax.shard_map(shards, mesh=mesh, in_specs=in_specs, out_specs=out_specs, check_vma=False)
```

```python
import functools

import jax
import jax.numpy as jnp
from jax import lax
from jax.experimental import pallas as pl
from jax.experimental.pallas import tpu as pltpu
from jax.sharding import PartitionSpec as P

VELOCITY = (
    (0, 0, 0), (1, 0, 0), (-1, 0, 0), (0, 1, 0), (0, -1, 0), (0, 0, 1), (0, 0, -1),
    (1, 1, 0), (-1, -1, 0), (1, -1, 0), (-1, 1, 0), (1, 0, 1), (-1, 0, -1), (1, 0, -1),
    (-1, 0, 1), (0, 1, 1), (0, -1, -1), (0, 1, -1), (0, -1, 1),
)
OPPOSITE = (0, 2, 1, 4, 3, 6, 5, 8, 7, 10, 9, 12, 11, 14, 13, 16, 15, 18, 17)
tau_coarse = 1.0
tau_fine = 1.5
drag_coef = 0.5
mass_coef = 10.0
spring_coef = 0.2
dashpot_coef = 0.05
gravity_z = -0.01
blend_coef = 0.5

ROOT2 = 1.4142135623730951
THREE_BY_ROOT2 = 2.1213203435596424
GROUPS = (tuple(range(19)), ())
NX = 32
NYZ = 1024
TOP = 8
EXT = NX + 16
X_PLUS = (1, 7, 9, 11, 13)
X_MINUS = (2, 8, 10, 12, 14)
Y_PLUS = (3, 7, 10, 15, 17)
Y_MINUS = (4, 8, 9, 16, 18)
DISTANCE = (-2, 2, -1, 1)
MESH = pl.DeviceIdType.MESH
F32 = jnp.float32
BF16 = jnp.bfloat16
NT = (((1,), (1,)), ((), ()))
NN = (((1,), (0,)), ((), ()))


def iota(shape, axis):
    return lax.broadcasted_iota(jnp.int32, shape, axis)


def split2(value):
    high = value.astype(BF16).astype(F32)
    return high, value - high


def split3(value):
    high = value.astype(BF16).astype(F32)
    rest = value - high
    middle = rest.astype(BF16).astype(F32)
    return high, middle, rest - middle


def one_hot(row, size, start=0):
    lanes = row.shape[1]
    return jnp.where(iota((size, lanes), 0) + start == row, 1.0, 0.0).astype(BF16)


def fill_one_hot(ref, row):
    for start in range(0, NYZ, 128):
        ref[start:start + 128, :] = one_hot(row, 128, start)


def dot(a, b, dims):
    return lax.dot_general(a, b, dims, preferred_element_type=F32)


def pack_interface(off_ref, slot_ref, src_ref, tgt_ref):
    off = off_ref[...]
    s8 = iota((8, NYZ), 0)
    dval = jnp.where(s8 == 0, DISTANCE[0], jnp.where(s8 == 1, DISTANCE[1], jnp.where(s8 == 2, DISTANCE[2], jnp.where(
        s8 == 3, DISTANCE[3], jnp.where(s8 == 4, 0, 99)))))
    member = jnp.where(off == dval, 1.0, 0.0)
    blocks = [member[:, b * 128:(b + 1) * 128] for b in range(8)]
    before = jnp.where(iota((128, 128), 0) < iota((128, 128), 1), 1.0, 0.0).astype(BF16)
    local = dot(jnp.concatenate(blocks, axis=0).astype(BF16), before, NN)
    running = jnp.zeros((8, 1), F32)
    ranks = []
    for b in range(8):
        ranks.append(local[b * 8:(b + 1) * 8] + running)
        running = running + jnp.sum(blocks[b], axis=1, keepdims=True)
    counts = [running[i:i + 1, :] for i in range(4)]
    ends = []
    total = jnp.zeros((1, 1), F32)
    for i in range(4):
        total = total + (256.0 - counts[i])
        ends.append(total)
    s128 = iota((8, 128), 0)
    base = (s128 * 256).astype(F32)
    positions = []
    for b in range(8):
        sent = jnp.sum(jnp.where(s128 < 4, blocks[b] * (base + ranks[b]), 0.0), axis=0, keepdims=True)
        z = ranks[b][4:5]
        stay = 768.0 + counts[3] + z - ends[2]
        for i in (2, 1, 0):
            start = ends[i - 1] if i else 0.0
            stay = jnp.where(z < ends[i], 256.0 * i + counts[i] + z - start, stay)
        positions.append(sent + blocks[b][4:5] * stay)
    pos = jnp.concatenate(positions, axis=1).astype(jnp.int32)
    src = src_ref[...]
    slot = slot_ref[...]
    values = jnp.where(s8 == 0, src >> 8, jnp.where(s8 == 1, src & 255, jnp.where(s8 == 2, slot >> 8, jnp.where(
        s8 == 3, slot & 255, 0)))).astype(F32)
    pos_high = pos >> 7
    stacked = jnp.concatenate([jnp.where(pos_high == h, values, 0.0) for h in range(8)], axis=0).astype(BF16)
    packed = dot(stacked, one_hot(pos & 127, 128), NT)
    src_packed = jnp.concatenate([packed[h * 8:h * 8 + 1] * 256.0 + packed[h * 8 + 1:h * 8 + 2] for h in range(8)], axis=1)
    slot_high = jnp.concatenate([packed[h * 8 + 2:h * 8 + 3] for h in range(8)], axis=1).astype(jnp.int32)
    slot_low = jnp.concatenate([packed[h * 8 + 3:h * 8 + 4] for h in range(8)], axis=1).astype(jnp.int32)
    slot_packed = slot_high * 256 + slot_low
    tgt = tgt_ref[...]
    table = jnp.concatenate([(tgt >> 8).astype(F32), (tgt & 255).astype(F32)], axis=0).astype(BF16)
    found = dot(table, one_hot(slot_packed & 127, 128), NN)
    chosen = s8 == (slot_packed >> 7)
    tgt_high = jnp.sum(jnp.where(chosen, found[0:8], 0.0), axis=0, keepdims=True)
    tgt_low = jnp.sum(jnp.where(chosen, found[8:16], 0.0), axis=0, keepdims=True)
    tgt_packed = (tgt_high * 256.0 + tgt_low).astype(jnp.int32)
    return src_packed.astype(jnp.int32), tgt_packed, counts


def step_kernel(
    pdfs_hbm, flags_hbm, level_ref, pos_hbm, vel_hbm, rad_hbm, cell_hbm, pairs_hbm, spring_hbm, src_hbm, off_hbm, slot_hbm,
    tgt_hbm, mig_hbm,
    read_ref, spread_ref, tgtp_ref, state_ref, newcomers_ref, spring_out_ref,
    pdfs, flags, pos_ref, vel_ref, rad_ref, cell_ref, pairs_ref, spring_ref, src_ref, off_ref, slot_ref, tgt_ref,
    mig_ref,
    onehot, source_hot, moved_in, ext, velf, velb, vel8, rows16, edge_x, edge_y, edge_c, halo_x, halo_y, halo_yp, halo_c, splits,
    gathered, received, leaving, joined, fluid, force,
    load_sem, send_sem, recv_sem,
):
    a, b = lax.axis_index("wide"), lax.axis_index("narrow")
    n_wide, n_narrow = lax.axis_size("wide"), lax.axis_size("narrow")

    def device(dx, dy):
        return (lax.rem(a + dx + n_wide, n_wide), lax.rem(b + dy + n_narrow, n_narrow))

    pairs_of = [
        (cell_hbm, cell_ref), (off_hbm, off_ref), (slot_hbm, slot_ref), (src_hbm, src_ref), (tgt_hbm, tgt_ref),
        (rad_hbm, rad_ref), (vel_hbm, vel_ref), (mig_hbm, mig_ref), (pdfs_hbm, pdfs),
        (pairs_hbm, pairs_ref), (pos_hbm, pos_ref), (spring_hbm, spring_ref), (flags_hbm, flags),
    ]
    loads = [pltpu.make_async_copy(x, y, load_sem.at[i]) for i, (x, y) in enumerate(pairs_of)]
    for load in loads:
        load.start()
    around = [(dx, dy) for dx in (-1, 0, 1) for dy in (-1, 0, 1) if dx or dy] + [(-2, 0), (2, 0)]
    barrier = pltpu.get_barrier_semaphore()
    for dx, dy in around:
        pl.semaphore_signal(barrier, inc=1, device_id=device(dx, dy), device_id_type=MESH)
    for load in loads[:8]:
        load.wait()

    src_packed, tgt_packed, counts = pack_interface(off_ref, slot_ref, src_ref, tgt_ref)
    tgtp_ref[...] = tgt_packed

    cell = cell_ref[...]
    grain_x = cell >> 10
    fill_one_hot(onehot, cell & 1023)
    drag = drag_coef * rad_ref[...]
    in_row = iota((NX, NYZ), 0) == grain_x
    weights = [drag] + [drag * vel_ref[c:c + 1, :] for c in range(3)]
    for k, weight in enumerate(weights):
        for part, value in enumerate(split2(weight)):
            moved_in[(part * 4 + k) * NX:(part * 4 + k + 1) * NX, :] = jnp.where(in_row, value, 0.0).astype(BF16)
    fill_one_hot(source_hot, src_packed & 1023)

    fine = level_ref[0, 0] == 1
    tau = jnp.where(fine, tau_fine, tau_coarse).astype(F32)
    omega = jnp.where(fine, 1.0 / tau_fine, 1.0 / tau_coarse).astype(F32)
    keep = jnp.where(fine, 1.0 - 1.0 / tau_fine, 0.0).astype(F32)

    def bring(i):
        cols = slice(i * 512, (i + 1) * 512)
        got = dot(moved_in[...], onehot[cols, :], NT)
        force[:, cols] = got[0:128] + got[128:256]

    def collide(row, col):
        rows = slice(row, row + 8)
        cols = slice(col, col + 128)
        p = [pdfs[q, rows, cols] for q in range(19)]
        pair_sum = {q: p[q] + p[q + 1] for q in range(1, 19, 2)}
        pair_dif = {q: p[q] - p[q + 1] for q in range(1, 19, 2)}
        density = p[0] + ((pair_sum[1] + pair_sum[3]) + (pair_sum[5] + pair_sum[7])) + (
            (pair_sum[9] + pair_sum[11]) + (pair_sum[13] + pair_sum[15]) + pair_sum[17])
        mom = (
            (pair_dif[1] + pair_dif[7]) + (pair_dif[9] + pair_dif[11]) + pair_dif[13],
            (pair_dif[3] + pair_dif[7]) + (pair_dif[15] - pair_dif[9]) + pair_dif[17],
            (pair_dif[5] + pair_dif[11]) + (pair_dif[15] - pair_dif[13]) - pair_dif[17],
        )
        inverse = 1.0 / density
        pull = tau * inverse
        resist = force[rows, cols]
        shifted = []
        for c in range(3):
            v = mom[c] * inverse
            velf[c * NX + row:c * NX + row + 8, cols] = v
            shifted.append(THREE_BY_ROOT2 * (v + pull * (force[(c + 1) * NX + row:(c + 1) * NX + row + 8, cols] - v * resist)))
        base = 1.0 - (shifted[0] * shifted[0] + shifted[1] * shifted[1] + shifted[2] * shifted[2]) * (1.0 / 3.0)
        dense = omega * density
        slim = dense * (1.0 / 36.0)
        wide = slim + slim
        slim_base = slim * base
        wide_base = slim_base + slim_base
        out_rows = slice(TOP + row, TOP + row + 8)
        ext[0, out_rows, cols] = keep * p[0] + 6.0 * wide_base
        for q in range(1, 19, 2):
            along = None
            for c in range(3):
                if VELOCITY[q][c] == 1:
                    along = shifted[c] if along is None else along + shifted[c]
                elif VELOCITY[q][c] == -1:
                    along = along - shifted[c]
            scaled = (wide if q < 7 else slim) * along
            even = (wide_base if q < 7 else slim_base) + scaled * along
            odd = ROOT2 * scaled
            ext[q, out_rows, cols] = keep * p[q] + (even + odd)
            ext[q + 1, out_rows, cols] = keep * p[q + 1] + (even - odd)

    bring(0)
    loads[8].wait()
    for i in range(2):
        if i < 1:
            bring(i + 1)
        for col in range(i * 512, i * 512 + 512, 128):
            for row in range(0, NX, 8):
                collide(row, col)

    for k in range(5):
        edge_x[0, k:k + 1, :] = ext[X_PLUS[k], TOP + NX - 1:TOP + NX, :]
        edge_x[1, k:k + 1, :] = ext[X_MINUS[k], TOP:TOP + 1, :]
        edge_y[0, k] = ext[Y_PLUS[k], TOP:TOP + NX, 896:1024]
        edge_y[1, k] = ext[Y_MINUS[k], TOP:TOP + NX, 0:128]
    edge_c[0, 0:1, :] = ext[7, TOP + NX - 1:TOP + NX, 896:1024]
    edge_c[1, 0:1, :] = ext[8, TOP:TOP + 1, 0:128]
    edge_c[2, 0:1, :] = ext[9, TOP + NX - 1:TOP + NX, 0:128]
    edge_c[3, 0:1, :] = ext[10, TOP:TOP + 1, 896:1024]
    pl.semaphore_wait(barrier, len(around))

    def send(index, source, target, dx, dy):
        copy = pltpu.make_async_remote_copy(
            src_ref=source, dst_ref=target, send_sem=send_sem.at[index], recv_sem=recv_sem.at[index],
            device_id=device(dx, dy), device_id_type=MESH)
        copy.start()
        return copy

    halo = [
        send(0, edge_x.at[0], halo_x.at[0], 1, 0),
        send(1, edge_x.at[1], halo_x.at[1], -1, 0),
        send(2, edge_y.at[0], halo_y.at[0], 0, 1),
        send(3, edge_y.at[1], halo_y.at[1], 0, -1),
        send(4, edge_c.at[0], halo_c.at[0], 1, 1),
        send(5, edge_c.at[1], halo_c.at[1], -1, -1),
        send(6, edge_c.at[2], halo_c.at[2], 1, -1),
        send(7, edge_c.at[3], halo_c.at[3], -1, 1),
    ]

    def fluid_at_grains():
        for part, value in enumerate(split2(velf[...])):
            velb[part * 96:part * 96 + 96, :] = value.astype(BF16)
        for i in range(2):
            cols = slice(i * 512, (i + 1) * 512)
            got = dot(velb[...], onehot[:, cols], NN)
            got = got[0:96] + got[96:192]
            here = iota((NX, 512), 0) == (cell_ref[:, cols] >> 10)
            for c in range(3):
                fluid[c:c + 1, cols] = jnp.sum(jnp.where(here, got[c * NX:(c + 1) * NX], 0.0), axis=0, keepdims=True)

    lane = iota((NX, 128), 1)

    def stream(group):
        for k, q in enumerate(group):
            cx, cy, cz = VELOCITY[q]
            shift = cy * 32 + cz
            rows = slice(TOP - cx, TOP - cx + NX)
            value = ext[q, rows, :]
            if shift:
                value = pltpu.roll(value, shift % NYZ, 1)
            if cy == 1:
                edge = pltpu.roll(halo_yp[0, Y_PLUS.index(q), rows, :], shift % 128, 1)
                value = jnp.concatenate([jnp.where(lane < 32, edge, value[:, 0:128]), value[:, 128:]], axis=1)
            if cy == -1:
                edge = pltpu.roll(halo_yp[1, Y_MINUS.index(q), rows, :], shift % 128, 1)
                value = jnp.concatenate([value[:, :896], jnp.where(lane >= 96, edge, value[:, 896:])], axis=1)
            if q:
                bit = 1 << (q if q < 10 else q - 10)
                solid = (flags[0 if q < 10 else 1] & bit) != 0
                value = jnp.where(solid, ext[OPPOSITE[q], TOP:TOP + NX, :], value)
            read_ref[q] = value
            high, low = split2(value)
            at = group[0] * 2 * NX + k * NX
            splits[at:at + NX, :] = high.astype(BF16)
            splits[at + len(group) * NX:at + (len(group) + 1) * NX, :] = low.astype(BF16)

    def extract(group, i, width=1):
        cols = slice(i * 256, (i + width) * 256)
        at, size = group[0] * 2 * NX, len(group) * NX
        got = dot(splits[at:at + 2 * size, :], source_hot[:, cols], NN)
        here = iota((NX, 256 * width), 0) == (src_packed[:, cols] >> 10)
        for k, q in enumerate(group):
            value = got[k * NX:(k + 1) * NX] + got[size + k * NX:size + (k + 1) * NX]
            value = jnp.sum(jnp.where(here, value, 0.0), axis=0, keepdims=True)
            for w in range(width):
                gathered[i + w, q:q + 1, :] = value[:, w * 256:(w + 1) * 256]

    def contacts_in():
        vel8[...] = jnp.zeros_like(vel8)
        vel8[0:3, :] = vel_ref[...]
        vel8[4:7, :] = vel_ref[...]
        tables = [vel8[:, h * 128:(h + 1) * 128] for h in range(8)]
        half = iota((8, 128), 0) < 4
        for c in range(24):
            cols = slice(c * 128, (c + 1) * 128)
            index = jnp.where(half, pairs_ref[0:1, cols], pairs_ref[1:2, cols])
            low = index & 127
            high = index >> 7
            found = jnp.take_along_axis(tables[0], low, axis=1, mode="promise_in_bounds")
            for h in range(1, 8):
                found = jnp.where(high == h, jnp.take_along_axis(tables[h], low, axis=1, mode="promise_in_bounds"), found)
            relative = found[4:7] - found[0:3]
            spring = spring_ref[:, cols]
            spring_out_ref[:, cols] = spring + relative
            contact = spring_coef * spring + dashpot_coef * relative
            for part, value in enumerate(split3(contact)):
                rows16[part * 3:part * 3 + 3, cols] = value

    def contacts_out():
        rows16[9:16, :] = jnp.zeros((7, 3072), F32)
        forces = rows16[...]
        spread = []
        hots = []
        for side in range(2):
            index = pairs_ref[side:side + 1, :]
            high = index >> 7
            signed = -forces if side else forces
            spread.append(jnp.concatenate([jnp.where(high == h, signed, 0.0).astype(BF16) for h in range(8)], axis=0))
            hots.append(one_hot(index & 127, 128))
        summed = dot(jnp.concatenate(spread, axis=1), jnp.concatenate(hots, axis=1), NT)
        parts = [
            summed[h * 16:h * 16 + 3] + summed[h * 16 + 3:h * 16 + 6] + summed[h * 16 + 6:h * 16 + 9] for h in range(8)]
        return jnp.concatenate(parts, axis=1)

    def move_grains(summed):
        radius = rad_ref[...]
        vel = vel_ref[...]
        total = (drag_coef * radius) * (fluid[0:3, :] - vel) + summed
        mass = mass_coef * radius * radius * radius
        falling = jnp.where(iota((3, NYZ), 0) == 2, gravity_z, 0.0)
        moved_vel = vel + total / mass + falling
        state_ref[0:3, :] = pos_ref[...] + moved_vel
        state_ref[3:6, :] = moved_vel
        state_ref[6:7, :] = radius
        state_ref[7:8, :] = jnp.ones_like(radius)

    def leave():
        slots = jnp.concatenate([mig_ref[0:1, :], mig_ref[1:2, :]], axis=1)
        state = jnp.concatenate(split3(state_ref[...]), axis=0).astype(BF16)
        out = dot(state, one_hot(slots, NYZ), NN)
        leaving[...] = out[0:8] + out[8:16] + out[16:24]

    rows_out = []

    def send_region(i):
        rows_out.append(send(10 + i, gathered.at[i], received.at[i], DISTANCE[i], 0))

    for load in loads[9:]:
        load.wait()
    for copy in halo:
        copy.wait()
    for k in range(5):
        ext[X_PLUS[k], TOP - 1:TOP, :] = halo_x[0, k:k + 1, :]
        ext[X_MINUS[k], TOP + NX:TOP + NX + 1, :] = halo_x[1, k:k + 1, :]
        for side in range(2):
            halo_yp[side, k, TOP:TOP + NX, :] = halo_y[side, k]
    halo_yp[0, 1, TOP - 1:TOP, :] = halo_c[0, 0:1, :]
    halo_yp[1, 1, TOP + NX:TOP + NX + 1, :] = halo_c[1, 0:1, :]
    halo_yp[1, 2, TOP - 1:TOP, :] = halo_c[2, 0:1, :]
    halo_yp[0, 2, TOP + NX:TOP + NX + 1, :] = halo_c[3, 0:1, :]
    stream(GROUPS[0])
    fluid_at_grains()
    extract(GROUPS[0], 0, 2)
    contacts_in()
    summed = contacts_out()
    send_region(0)
    send_region(1)
    extract(GROUPS[0], 2, 2)
    move_grains(summed)
    leave()
    migrate = [send(8, leaving, joined.at[0], -1, 0), send(9, leaving, joined.at[1], 1, 0)]
    send_region(2)
    send_region(3)

    for copy in migrate:
        copy.wait()
    mig_lane = iota((8, 128), 1)
    change = jnp.where(iota((8, 128), 0) == 0, jnp.where(mig_lane < 64, float(NX), -float(NX)), 0.0)
    newcomers_ref[...] = jnp.where(mig_lane < 64, joined[0], joined[1]) + change

    for i in range(4):
        cols = slice(i * 256, (i + 1) * 256)
        rows_out[i].wait()
        stays = iota((24, 256), 1).astype(F32) >= counts[i]
        carried = jnp.where(stays, gathered[i], received[i])
        here = iota((NX, 256), 0) == (tgt_packed[:, cols] >> 10)
        for q in range(19):
            for part, value in enumerate(split2(carried[q:q + 1, :])):
                spread_ref[(part * 19 + q) * NX:(part * 19 + q + 1) * NX, cols] = jnp.where(here, value, 0.0).astype(BF16)
        spread_ref[38 * NX:39 * NX, cols] = jnp.where(here, 1.0, 0.0).astype(BF16)


def finish_kernel(
    read_ref, spread_ref, tgtp_ref, state_ref, newcomers_ref, mig_ref, spring_ref,
    next_hbm, pos_hbm, vel_hbm, rad_hbm, spring_hbm,
    blended, pos, vel, rad, sem,
):
    copies = [pltpu.make_async_copy(spring_ref, spring_hbm, sem.at[0])]
    copies[0].start()

    slots = jnp.concatenate([mig_ref[0:1, :], mig_ref[1:2, :]], axis=1)
    arrived = jnp.concatenate(split3(newcomers_ref[...]), axis=0).astype(BF16)
    placed = dot(arrived, one_hot(slots, NYZ), NT)
    placed = placed[0:8] + placed[8:16] + placed[16:24]
    result = jnp.where(placed[7:8] > 0.5, placed, state_ref[...])
    pos[...] = result[0:3]
    vel[...] = result[3:6]
    rad[...] = result[6:7]
    for source, target in ((pos, pos_hbm), (vel, vel_hbm), (rad, rad_hbm)):
        copies.append(pltpu.make_async_copy(source, target, sem.at[len(copies)]))
        copies[-1].start()

    row = tgtp_ref[...] & 1023
    for i in range(4):
        cols = slice(i * 256, (i + 1) * 256)
        got = dot(spread_ref[...], one_hot(row, 256, i * 256), NT)
        hit = got[38 * NX:39 * NX] > 0.5
        for start, stop in ((0, 10), (10, 19)):
            for q in range(start, stop):
                value = read_ref[q, :, cols]
                carried = got[q * NX:(q + 1) * NX] + got[(19 + q) * NX:(20 + q) * NX]
                blended[q, :, cols] = jnp.where(hit, blend_coef * (value + carried), value)
            copies.append(pltpu.make_async_copy(
                blended.at[start:stop, :, cols], next_hbm.at[start:stop, :, cols], sem.at[len(copies)]))
            copies[-1].start()
    for copy in copies:
        copy.wait()


def shards(
    pdfs, link_flags, block_level, grain_pos, grain_vel, grain_radius, grain_cell, contact_pairs, contact_spring, iface_source,
    iface_offset, iface_slot, iface_target, migrant_slots,
):
    row = (1, NYZ)
    vmem = pl.BlockSpec(memory_space=pltpu.VMEM)
    hbm = pl.BlockSpec(memory_space=pl.ANY)
    outs = pl.pallas_call(
        step_kernel,
        name="step",
        out_shape=(
            pltpu.VMEM((19, NX, NYZ), F32),
            pltpu.VMEM((39 * NX, NYZ), BF16),
            pltpu.VMEM(row, jnp.int32),
            pltpu.VMEM((8, NYZ), F32),
            pltpu.VMEM((8, 128), F32),
            pltpu.VMEM((3, 3072), F32),
        ),
        in_specs=[hbm] * 2 + [pl.BlockSpec(memory_space=pltpu.SMEM)] + [hbm] * 11,
        out_specs=(vmem,) * 6,
        scratch_shapes=[
            pltpu.VMEM((19, NX, NYZ), F32),
            pltpu.VMEM((2, NX, NYZ), jnp.int32),
            pltpu.VMEM((3, NYZ), F32),
            pltpu.VMEM((3, NYZ), F32),
            pltpu.VMEM(row, F32),
            pltpu.VMEM(row, jnp.int32),
            pltpu.VMEM((2, 3072), jnp.int32),
            pltpu.VMEM((3, 3072), F32),
            pltpu.VMEM(row, jnp.int32),
            pltpu.VMEM(row, jnp.int32),
            pltpu.VMEM(row, jnp.int32),
            pltpu.VMEM((8, 128), jnp.int32),
            pltpu.VMEM((2, 64), jnp.int32),
            pltpu.VMEM((NYZ, NYZ), BF16),
            pltpu.VMEM((NYZ, NYZ), BF16),
            pltpu.VMEM((8 * NX, NYZ), BF16),
            pltpu.VMEM((19, EXT, NYZ), F32),
            pltpu.VMEM((3 * NX, NYZ), F32),
            pltpu.VMEM((6 * NX, NYZ), BF16),
            pltpu.VMEM((8, NYZ), F32),
            pltpu.VMEM((16, 3072), F32),
            pltpu.VMEM((2, 8, NYZ), F32),
            pltpu.VMEM((2, 5, NX, 128), F32),
            pltpu.VMEM((4, 8, 128), F32),
            pltpu.VMEM((2, 8, NYZ), F32),
            pltpu.VMEM((2, 5, NX, 128), F32),
            pltpu.VMEM((2, 5, EXT, 128), F32),
            pltpu.VMEM((4, 8, 128), F32),
            pltpu.VMEM((38 * NX, NYZ), BF16),
            pltpu.VMEM((4, 24, 256), F32),
            pltpu.VMEM((4, 24, 256), F32),
            pltpu.VMEM((8, 128), F32),
            pltpu.VMEM((2, 8, 128), F32),
            pltpu.VMEM((8, NYZ), F32),
            pltpu.VMEM((4 * NX, NYZ), F32),
            pltpu.SemaphoreType.DMA((14,)),
            pltpu.SemaphoreType.DMA((14,)),
            pltpu.SemaphoreType.DMA((14,)),
        ],
        compiler_params=pltpu.CompilerParams(collective_id=0, has_side_effects=True, vmem_limit_bytes=61_800_000),
    )(
        pdfs, link_flags, block_level, grain_pos, grain_vel, grain_radius.reshape(row), grain_cell.reshape(row), contact_pairs,
        contact_spring, iface_source.reshape(row), iface_offset.reshape(row), iface_slot.reshape(row),
        iface_target.reshape(8, 128), migrant_slots,
    )
    read, spread, tgtp, state, newcomers, spring_next = outs
    result = pl.pallas_call(
        finish_kernel,
        name="finish",
        out_shape=(
            jax.ShapeDtypeStruct((19, NX, NYZ), F32),
            jax.ShapeDtypeStruct((3, NYZ), F32),
            jax.ShapeDtypeStruct((3, NYZ), F32),
            jax.ShapeDtypeStruct(row, F32),
            jax.ShapeDtypeStruct((3, 3072), F32),
        ),
        in_specs=[vmem] * 7,
        out_specs=(hbm,) * 5,
        scratch_shapes=[
            pltpu.VMEM((19, NX, NYZ), F32),
            pltpu.VMEM((3, NYZ), F32),
            pltpu.VMEM((3, NYZ), F32),
            pltpu.VMEM(row, F32),
            pltpu.SemaphoreType.DMA((12,)),
        ],
        compiler_params=pltpu.CompilerParams(vmem_limit_bytes=40 << 20),
    )(read, spread, tgtp, state, newcomers, migrant_slots, spring_next)
    pdfs_next, pos_next, vel_next, rad_next, spring_out = result
    return pdfs_next, pos_next, vel_next, rad_next.reshape(NYZ), spring_out


def solution(mesh):
    both = ("wide", "narrow")
    in_specs = (
        P(None, "wide", "narrow"), P(None, "wide", "narrow"), P("wide", "narrow"), P(None, both), P(None, both), P(both), P(both),
        P(None, both), P(None, both), P(both), P(), P(), P(both), P(None, both),
    )
    out_specs = (P(None, "wide", "narrow"), P(None, both), P(None, both), P(both), P(None, both))
    return jax.shard_map(shards, mesh=mesh, in_specs=in_specs, out_specs=out_specs, check_vma=False)
```

```python
import functools

import jax
import jax.numpy as jnp
from jax import lax
from jax.experimental import pallas as pl
from jax.experimental.pallas import tpu as pltpu
from jax.sharding import PartitionSpec as P

VELOCITY = (
    (0, 0, 0), (1, 0, 0), (-1, 0, 0), (0, 1, 0), (0, -1, 0), (0, 0, 1), (0, 0, -1),
    (1, 1, 0), (-1, -1, 0), (1, -1, 0), (-1, 1, 0), (1, 0, 1), (-1, 0, -1), (1, 0, -1),
    (-1, 0, 1), (0, 1, 1), (0, -1, -1), (0, 1, -1), (0, -1, 1),
)
OPPOSITE = (0, 2, 1, 4, 3, 6, 5, 8, 7, 10, 9, 12, 11, 14, 13, 16, 15, 18, 17)
tau_coarse = 1.0
tau_fine = 1.5
drag_coef = 0.5
mass_coef = 10.0
spring_coef = 0.2
dashpot_coef = 0.05
gravity_z = -0.01
blend_coef = 0.5

ROOT2 = 1.4142135623730951
THREE_BY_ROOT2 = 2.1213203435596424
GROUPS = (tuple(range(19)), ())
NX = 32
NYZ = 1024
TOP = 8
EXT = NX + 16
X_PLUS = (1, 7, 9, 11, 13)
X_MINUS = (2, 8, 10, 12, 14)
Y_PLUS = (3, 7, 10, 15, 17)
Y_MINUS = (4, 8, 9, 16, 18)
DISTANCE = (-2, 2, -1, 1)
MESH = pl.DeviceIdType.MESH
F32 = jnp.float32
BF16 = jnp.bfloat16
NT = (((1,), (1,)), ((), ()))
NN = (((1,), (0,)), ((), ()))


def iota(shape, axis):
    return lax.broadcasted_iota(jnp.int32, shape, axis)


def split2(value):
    high = value.astype(BF16).astype(F32)
    return high, value - high


def split3(value):
    high = value.astype(BF16).astype(F32)
    rest = value - high
    middle = rest.astype(BF16).astype(F32)
    return high, middle, rest - middle


def one_hot(row, size, start=0):
    lanes = row.shape[1]
    return jnp.where(iota((size, lanes), 0) + start == row, 1.0, 0.0).astype(BF16)


def fill_one_hot(ref, row):
    for start in range(0, NYZ, 128):
        ref[start:start + 128, :] = one_hot(row, 128, start)


def dot(a, b, dims):
    return lax.dot_general(a, b, dims, preferred_element_type=F32)


def pack_interface(off_ref, slot_ref, src_ref, tgt_ref):
    off = off_ref[...]
    s8 = iota((8, NYZ), 0)
    dval = jnp.where(s8 == 0, DISTANCE[0], jnp.where(s8 == 1, DISTANCE[1], jnp.where(s8 == 2, DISTANCE[2], jnp.where(
        s8 == 3, DISTANCE[3], jnp.where(s8 == 4, 0, 99)))))
    member = jnp.where(off == dval, 1.0, 0.0)
    blocks = [member[:, b * 128:(b + 1) * 128] for b in range(8)]
    before = jnp.where(iota((128, 128), 0) < iota((128, 128), 1), 1.0, 0.0).astype(BF16)
    local = dot(jnp.concatenate(blocks, axis=0).astype(BF16), before, NN)
    running = jnp.zeros((8, 1), F32)
    ranks = []
    for b in range(8):
        ranks.append(local[b * 8:(b + 1) * 8] + running)
        running = running + jnp.sum(blocks[b], axis=1, keepdims=True)
    counts = [running[i:i + 1, :] for i in range(4)]
    ends = []
    total = jnp.zeros((1, 1), F32)
    for i in range(4):
        total = total + (256.0 - counts[i])
        ends.append(total)
    s128 = iota((8, 128), 0)
    base = (s128 * 256).astype(F32)
    positions = []
    for b in range(8):
        sent = jnp.sum(jnp.where(s128 < 4, blocks[b] * (base + ranks[b]), 0.0), axis=0, keepdims=True)
        z = ranks[b][4:5]
        stay = 768.0 + counts[3] + z - ends[2]
        for i in (2, 1, 0):
            start = ends[i - 1] if i else 0.0
            stay = jnp.where(z < ends[i], 256.0 * i + counts[i] + z - start, stay)
        positions.append(sent + blocks[b][4:5] * stay)
    pos = jnp.concatenate(positions, axis=1).astype(jnp.int32)
    src = src_ref[...]
    slot = slot_ref[...]
    values = jnp.where(s8 == 0, src >> 8, jnp.where(s8 == 1, src & 255, jnp.where(s8 == 2, slot >> 8, jnp.where(
        s8 == 3, slot & 255, 0)))).astype(F32)
    pos_high = pos >> 7
    stacked = jnp.concatenate([jnp.where(pos_high == h, values, 0.0) for h in range(8)], axis=0).astype(BF16)
    packed = dot(stacked, one_hot(pos & 127, 128), NT)
    src_packed = jnp.concatenate([packed[h * 8:h * 8 + 1] * 256.0 + packed[h * 8 + 1:h * 8 + 2] for h in range(8)], axis=1)
    slot_high = jnp.concatenate([packed[h * 8 + 2:h * 8 + 3] for h in range(8)], axis=1).astype(jnp.int32)
    slot_low = jnp.concatenate([packed[h * 8 + 3:h * 8 + 4] for h in range(8)], axis=1).astype(jnp.int32)
    slot_packed = slot_high * 256 + slot_low
    tgt = tgt_ref[...]
    table = jnp.concatenate([(tgt >> 8).astype(F32), (tgt & 255).astype(F32)], axis=0).astype(BF16)
    found = dot(table, one_hot(slot_packed & 127, 128), NN)
    chosen = s8 == (slot_packed >> 7)
    tgt_high = jnp.sum(jnp.where(chosen, found[0:8], 0.0), axis=0, keepdims=True)
    tgt_low = jnp.sum(jnp.where(chosen, found[8:16], 0.0), axis=0, keepdims=True)
    tgt_packed = (tgt_high * 256.0 + tgt_low).astype(jnp.int32)
    return src_packed.astype(jnp.int32), tgt_packed, counts


def step_kernel(
    pdfs_hbm, flags_hbm, level_ref, pos_hbm, vel_hbm, rad_hbm, cell_hbm, pairs_hbm, spring_hbm, src_hbm, off_hbm, slot_hbm,
    tgt_hbm, mig_hbm,
    read_ref, spread_ref, tgtp_ref, result_ref, spring_out_ref,
    pdfs, flags, pos_ref, vel_ref, rad_ref, cell_ref, pairs_ref, spring_ref, src_ref, off_ref, slot_ref, tgt_ref,
    mig_ref,
    onehot, source_hot, moved_in, ext, velf, velb, vel8, rows16, edge_x, edge_y, edge_c, halo_x, halo_y, halo_yp, halo_c, splits,
    gathered, received, leaving, joined, fluid, force, state_ref,
    load_sem, send_sem, recv_sem,
):
    a, b = lax.axis_index("wide"), lax.axis_index("narrow")
    n_wide, n_narrow = lax.axis_size("wide"), lax.axis_size("narrow")

    def device(dx, dy):
        return (lax.rem(a + dx + n_wide, n_wide), lax.rem(b + dy + n_narrow, n_narrow))

    small = [
        (cell_hbm, cell_ref), (off_hbm, off_ref), (slot_hbm, slot_ref), (src_hbm, src_ref), (tgt_hbm, tgt_ref),
        (rad_hbm, rad_ref), (vel_hbm, vel_ref), (pairs_hbm, pairs_ref), (spring_hbm, spring_ref), (pos_hbm, pos_ref),
        (mig_hbm, mig_ref),
    ]
    parts = [slice(i * 256, (i + 1) * 256) for i in range(4)]
    large = [(pdfs_hbm.at[:, :, part], pdfs.at[:, :, part]) for part in parts] + [(flags_hbm, flags)]
    loads = [pltpu.make_async_copy(x, y, load_sem.at[i]) for i, (x, y) in enumerate(small + large)]
    for load in loads:
        load.start()
    around = [(dx, dy) for dx in (-1, 0, 1) for dy in (-1, 0, 1) if dx or dy] + [(-2, 0), (2, 0)]
    barrier = pltpu.get_barrier_semaphore()
    for dx, dy in around:
        pl.semaphore_signal(barrier, inc=1, device_id=device(dx, dy), device_id_type=MESH)
    for load in loads[:11]:
        load.wait()

    src_packed, tgt_packed, counts = pack_interface(off_ref, slot_ref, src_ref, tgt_ref)
    tgtp_ref[...] = tgt_packed

    cell = cell_ref[...]
    grain_x = cell >> 10
    fill_one_hot(onehot, cell & 1023)
    drag = drag_coef * rad_ref[...]
    in_row = iota((NX, NYZ), 0) == grain_x
    weights = [drag] + [drag * vel_ref[c:c + 1, :] for c in range(3)]
    for k, weight in enumerate(weights):
        for part, value in enumerate(split2(weight)):
            moved_in[(part * 4 + k) * NX:(part * 4 + k + 1) * NX, :] = jnp.where(in_row, value, 0.0).astype(BF16)
    fill_one_hot(source_hot, src_packed & 1023)

    fine = level_ref[0, 0] == 1
    tau = jnp.where(fine, tau_fine, tau_coarse).astype(F32)
    omega = jnp.where(fine, 1.0 / tau_fine, 1.0 / tau_coarse).astype(F32)
    keep = jnp.where(fine, 1.0 - 1.0 / tau_fine, 0.0).astype(F32)

    def bring(i):
        cols = slice(i * 512, (i + 1) * 512)
        got = dot(moved_in[...], onehot[cols, :], NT)
        force[:, cols] = got[0:128] + got[128:256]

    def collide(row, col):
        rows = slice(row, row + 8)
        cols = slice(col, col + 128)
        p = [pdfs[q, rows, cols] for q in range(19)]
        pair_sum = {q: p[q] + p[q + 1] for q in range(1, 19, 2)}
        pair_dif = {q: p[q] - p[q + 1] for q in range(1, 19, 2)}
        density = p[0] + ((pair_sum[1] + pair_sum[3]) + (pair_sum[5] + pair_sum[7])) + (
            (pair_sum[9] + pair_sum[11]) + (pair_sum[13] + pair_sum[15]) + pair_sum[17])
        mom = (
            (pair_dif[1] + pair_dif[7]) + (pair_dif[9] + pair_dif[11]) + pair_dif[13],
            (pair_dif[3] + pair_dif[7]) + (pair_dif[15] - pair_dif[9]) + pair_dif[17],
            (pair_dif[5] + pair_dif[11]) + (pair_dif[15] - pair_dif[13]) - pair_dif[17],
        )
        inverse = 1.0 / density
        pull = tau * inverse
        resist = force[rows, cols]
        shifted = []
        for c in range(3):
            v = mom[c] * inverse
            velf[c * NX + row:c * NX + row + 8, cols] = v
            shifted.append(THREE_BY_ROOT2 * (v + pull * (force[(c + 1) * NX + row:(c + 1) * NX + row + 8, cols] - v * resist)))
        base = 1.0 - (shifted[0] * shifted[0] + shifted[1] * shifted[1] + shifted[2] * shifted[2]) * (1.0 / 3.0)
        dense = omega * density
        slim = dense * (1.0 / 36.0)
        wide = slim + slim
        slim_base = slim * base
        wide_base = slim_base + slim_base
        out_rows = slice(TOP + row, TOP + row + 8)
        ext[0, out_rows, cols] = keep * p[0] + 6.0 * wide_base
        for q in range(1, 19, 2):
            along = None
            for c in range(3):
                if VELOCITY[q][c] == 1:
                    along = shifted[c] if along is None else along + shifted[c]
                elif VELOCITY[q][c] == -1:
                    along = along - shifted[c]
            scaled = (wide if q < 7 else slim) * along
            even = (wide_base if q < 7 else slim_base) + scaled * along
            odd = ROOT2 * scaled
            ext[q, out_rows, cols] = keep * p[q] + (even + odd)
            ext[q + 1, out_rows, cols] = keep * p[q + 1] + (even - odd)

    def contacts_in():
        vel8[...] = jnp.zeros_like(vel8)
        vel8[0:3, :] = vel_ref[...]
        vel8[4:7, :] = vel_ref[...]
        tables = [vel8[:, h * 128:(h + 1) * 128] for h in range(8)]
        half = iota((8, 128), 0) < 4
        for c in range(24):
            cols = slice(c * 128, (c + 1) * 128)
            index = jnp.where(half, pairs_ref[0:1, cols], pairs_ref[1:2, cols])
            low = index & 127
            high = index >> 7
            found = jnp.take_along_axis(tables[0], low, axis=1, mode="promise_in_bounds")
            for h in range(1, 8):
                found = jnp.where(high == h, jnp.take_along_axis(tables[h], low, axis=1, mode="promise_in_bounds"), found)
            relative = found[4:7] - found[0:3]
            spring = spring_ref[:, cols]
            spring_out_ref[:, cols] = spring + relative
            contact = spring_coef * spring + dashpot_coef * relative
            for part, value in enumerate(split3(contact)):
                rows16[part * 3:part * 3 + 3, cols] = value

    def contacts_out():
        rows16[9:16, :] = jnp.zeros((7, 3072), F32)
        forces = rows16[...]
        spread = []
        hots = []
        for side in range(2):
            index = pairs_ref[side:side + 1, :]
            high = index >> 7
            signed = -forces if side else forces
            spread.append(jnp.concatenate([jnp.where(high == h, signed, 0.0).astype(BF16) for h in range(8)], axis=0))
            hots.append(one_hot(index & 127, 128))
        summed = dot(jnp.concatenate(spread, axis=1), jnp.concatenate(hots, axis=1), NT)
        parts = [
            summed[h * 16:h * 16 + 3] + summed[h * 16 + 3:h * 16 + 6] + summed[h * 16 + 6:h * 16 + 9] for h in range(8)]
        return jnp.concatenate(parts, axis=1)

    bring(0)
    contacts_in()
    summed = contacts_out()
    for i in range(4):
        loads[11 + i].wait()
    bring(1)
    for col in range(0, NYZ, 128):
        for row in range(0, NX, 8):
            collide(row, col)

    for k in range(5):
        edge_x[0, k:k + 1, :] = ext[X_PLUS[k], TOP + NX - 1:TOP + NX, :]
        edge_x[1, k:k + 1, :] = ext[X_MINUS[k], TOP:TOP + 1, :]
        edge_y[0, k] = ext[Y_PLUS[k], TOP:TOP + NX, 896:1024]
        edge_y[1, k] = ext[Y_MINUS[k], TOP:TOP + NX, 0:128]
    edge_c[0, 0:1, :] = ext[7, TOP + NX - 1:TOP + NX, 896:1024]
    edge_c[1, 0:1, :] = ext[8, TOP:TOP + 1, 0:128]
    edge_c[2, 0:1, :] = ext[9, TOP + NX - 1:TOP + NX, 0:128]
    edge_c[3, 0:1, :] = ext[10, TOP:TOP + 1, 896:1024]
    pl.semaphore_wait(barrier, len(around))

    def send(index, source, target, dx, dy):
        copy = pltpu.make_async_remote_copy(
            src_ref=source, dst_ref=target, send_sem=send_sem.at[index], recv_sem=recv_sem.at[index],
            device_id=device(dx, dy), device_id_type=MESH)
        copy.start()
        return copy

    halo = [
        send(0, edge_x.at[0], halo_x.at[0], 1, 0),
        send(1, edge_x.at[1], halo_x.at[1], -1, 0),
        send(2, edge_y.at[0], halo_y.at[0], 0, 1),
        send(3, edge_y.at[1], halo_y.at[1], 0, -1),
        send(4, edge_c.at[0], halo_c.at[0], 1, 1),
        send(5, edge_c.at[1], halo_c.at[1], -1, -1),
        send(6, edge_c.at[2], halo_c.at[2], 1, -1),
        send(7, edge_c.at[3], halo_c.at[3], -1, 1),
    ]

    def fluid_at_grains():
        for part, value in enumerate(split2(velf[...])):
            velb[part * 96:part * 96 + 96, :] = value.astype(BF16)
        for i in range(2):
            cols = slice(i * 512, (i + 1) * 512)
            got = dot(velb[...], onehot[:, cols], NN)
            got = got[0:96] + got[96:192]
            here = iota((NX, 512), 0) == (cell_ref[:, cols] >> 10)
            for c in range(3):
                fluid[c:c + 1, cols] = jnp.sum(jnp.where(here, got[c * NX:(c + 1) * NX], 0.0), axis=0, keepdims=True)

    lane = iota((NX, 128), 1)

    def stream(group):
        for k, q in enumerate(group):
            cx, cy, cz = VELOCITY[q]
            shift = cy * 32 + cz
            rows = slice(TOP - cx, TOP - cx + NX)
            value = ext[q, rows, :]
            if shift:
                value = pltpu.roll(value, shift % NYZ, 1)
            if cy == 1:
                edge = pltpu.roll(halo_yp[0, Y_PLUS.index(q), rows, :], shift % 128, 1)
                value = jnp.concatenate([jnp.where(lane < 32, edge, value[:, 0:128]), value[:, 128:]], axis=1)
            if cy == -1:
                edge = pltpu.roll(halo_yp[1, Y_MINUS.index(q), rows, :], shift % 128, 1)
                value = jnp.concatenate([value[:, :896], jnp.where(lane >= 96, edge, value[:, 896:])], axis=1)
            if q:
                bit = 1 << (q if q < 10 else q - 10)
                solid = (flags[0 if q < 10 else 1] & bit) != 0
                value = jnp.where(solid, ext[OPPOSITE[q], TOP:TOP + NX, :], value)
            read_ref[q] = value
            high = value.astype(BF16)
            at = group[0] * 2 * NX + k * NX
            splits[at:at + NX, :] = high
            splits[at + len(group) * NX:at + (len(group) + 1) * NX, :] = (value - high.astype(F32)).astype(BF16)

    def extract(group, i, width=1):
        cols = slice(i * 256, (i + width) * 256)
        at, size = group[0] * 2 * NX, len(group) * NX
        got = dot(splits[at:at + 2 * size, :], source_hot[:, cols], NN)
        here = iota((NX, 256 * width), 0) == (src_packed[:, cols] >> 10)
        for k, q in enumerate(group):
            value = got[k * NX:(k + 1) * NX] + got[size + k * NX:size + (k + 1) * NX]
            value = jnp.sum(jnp.where(here, value, 0.0), axis=0, keepdims=True)
            for w in range(width):
                gathered[i + w, q:q + 1, :] = value[:, w * 256:(w + 1) * 256]

    def move_grains(summed):
        radius = rad_ref[...]
        vel = vel_ref[...]
        total = (drag_coef * radius) * (fluid[0:3, :] - vel) + summed
        mass = mass_coef * radius * radius * radius
        falling = jnp.where(iota((3, NYZ), 0) == 2, gravity_z, 0.0)
        moved_vel = vel + total / mass + falling
        state_ref[0:3, :] = pos_ref[...] + moved_vel
        state_ref[3:6, :] = moved_vel
        state_ref[6:7, :] = radius
        state_ref[7:8, :] = jnp.ones_like(radius)

    def leave():
        slots = jnp.concatenate([mig_ref[0:1, :], mig_ref[1:2, :]], axis=1)
        state = jnp.concatenate(split3(state_ref[...]), axis=0).astype(BF16)
        out = dot(state, one_hot(slots, NYZ), NN)
        leaving[...] = out[0:8] + out[8:16] + out[16:24]

    rows_out = []

    def send_region(i):
        rows_out.append(send(10 + i, gathered.at[i], received.at[i], DISTANCE[i], 0))

    fluid_at_grains()
    loads[15].wait()
    for copy in halo:
        copy.wait()
    for k in range(5):
        ext[X_PLUS[k], TOP - 1:TOP, :] = halo_x[0, k:k + 1, :]
        ext[X_MINUS[k], TOP + NX:TOP + NX + 1, :] = halo_x[1, k:k + 1, :]
        for side in range(2):
            halo_yp[side, k, TOP:TOP + NX, :] = halo_y[side, k]
    halo_yp[0, 1, TOP - 1:TOP, :] = halo_c[0, 0:1, :]
    halo_yp[1, 1, TOP + NX:TOP + NX + 1, :] = halo_c[1, 0:1, :]
    halo_yp[1, 2, TOP - 1:TOP, :] = halo_c[2, 0:1, :]
    halo_yp[0, 2, TOP + NX:TOP + NX + 1, :] = halo_c[3, 0:1, :]
    stream(GROUPS[0])
    extract(GROUPS[0], 0, 2)
    send_region(0)
    send_region(1)
    extract(GROUPS[0], 2, 2)
    send_region(2)
    send_region(3)
    move_grains(summed)
    leave()
    migrate = [send(8, leaving, joined.at[0], -1, 0), send(9, leaving, joined.at[1], 1, 0)]

    for i in range(4):
        cols = slice(i * 256, (i + 1) * 256)
        rows_out[i].wait()
        stays = iota((24, 256), 1).astype(F32) >= counts[i]
        carried = jnp.where(stays, gathered[i], received[i])
        here = iota((NX, 256), 0) == (tgt_packed[:, cols] >> 10)
        for q in range(19):
            for part, value in enumerate(split2(carried[q:q + 1, :])):
                spread_ref[(part * 19 + q) * NX:(part * 19 + q + 1) * NX, cols] = jnp.where(here, value, 0.0).astype(BF16)
        spread_ref[38 * NX:39 * NX, cols] = jnp.where(here, 1.0, 0.0).astype(BF16)

    for copy in migrate:
        copy.wait()
    mig_lane = iota((8, 128), 1)
    change = jnp.where(iota((8, 128), 0) == 0, jnp.where(mig_lane < 64, float(NX), -float(NX)), 0.0)
    newcomers = jnp.where(mig_lane < 64, joined[0], joined[1]) + change
    slots = jnp.concatenate([mig_ref[0:1, :], mig_ref[1:2, :]], axis=1)
    placed = dot(jnp.concatenate(split3(newcomers), axis=0).astype(BF16), one_hot(slots, NYZ), NT)
    placed = placed[0:8] + placed[8:16] + placed[16:24]
    result_ref[...] = jnp.where(placed[7:8] > 0.5, placed, state_ref[...])


def finish_kernel(
    read_ref, spread_ref, tgtp_ref, result_ref, spring_ref,
    next_hbm, pos_hbm, vel_hbm, rad_hbm, spring_hbm,
    blended, pos, vel, rad, sem,
):
    pos[...] = result_ref[0:3, :]
    vel[...] = result_ref[3:6, :]
    rad[...] = result_ref[6:7, :]
    copies = []
    for source, target in ((spring_ref, spring_hbm), (pos, pos_hbm), (vel, vel_hbm), (rad, rad_hbm)):
        copies.append(pltpu.make_async_copy(source, target, sem.at[len(copies)]))
        copies[-1].start()

    row = tgtp_ref[...] & 1023
    for i in range(2):
        cols = slice(i * 512, (i + 1) * 512)
        got = dot(spread_ref[...], one_hot(row, 512, i * 512), NT)
        hit = got[38 * NX:39 * NX] > 0.5
        for start, stop in ((0, 10), (10, 19)):
            for q in range(start, stop):
                value = read_ref[q, :, cols]
                carried = got[q * NX:(q + 1) * NX] + got[(19 + q) * NX:(20 + q) * NX]
                blended[q, :, cols] = jnp.where(hit, blend_coef * (value + carried), value)
            copies.append(pltpu.make_async_copy(
                blended.at[start:stop, :, cols], next_hbm.at[start:stop, :, cols], sem.at[len(copies)]))
            copies[-1].start()
    for copy in copies:
        copy.wait()


def shards(
    pdfs, link_flags, block_level, grain_pos, grain_vel, grain_radius, grain_cell, contact_pairs, contact_spring, iface_source,
    iface_offset, iface_slot, iface_target, migrant_slots,
):
    row = (1, NYZ)
    vmem = pl.BlockSpec(memory_space=pltpu.VMEM)
    hbm = pl.BlockSpec(memory_space=pl.ANY)
    outs = pl.pallas_call(
        step_kernel,
        name="step",
        out_shape=(
            pltpu.VMEM((19, NX, NYZ), F32),
            pltpu.VMEM((39 * NX, NYZ), BF16),
            pltpu.VMEM(row, jnp.int32),
            pltpu.VMEM((8, NYZ), F32),
            pltpu.VMEM((3, 3072), F32),
        ),
        in_specs=[hbm] * 2 + [pl.BlockSpec(memory_space=pltpu.SMEM)] + [hbm] * 11,
        out_specs=(vmem,) * 5,
        scratch_shapes=[
            pltpu.VMEM((19, NX, NYZ), F32),
            pltpu.VMEM((2, NX, NYZ), jnp.int32),
            pltpu.VMEM((3, NYZ), F32),
            pltpu.VMEM((3, NYZ), F32),
            pltpu.VMEM(row, F32),
            pltpu.VMEM(row, jnp.int32),
            pltpu.VMEM((2, 3072), jnp.int32),
            pltpu.VMEM((3, 3072), F32),
            pltpu.VMEM(row, jnp.int32),
            pltpu.VMEM(row, jnp.int32),
            pltpu.VMEM(row, jnp.int32),
            pltpu.VMEM((8, 128), jnp.int32),
            pltpu.VMEM((2, 64), jnp.int32),
            pltpu.VMEM((NYZ, NYZ), BF16),
            pltpu.VMEM((NYZ, NYZ), BF16),
            pltpu.VMEM((8 * NX, NYZ), BF16),
            pltpu.VMEM((19, EXT, NYZ), F32),
            pltpu.VMEM((3 * NX, NYZ), F32),
            pltpu.VMEM((6 * NX, NYZ), BF16),
            pltpu.VMEM((8, NYZ), F32),
            pltpu.VMEM((16, 3072), F32),
            pltpu.VMEM((2, 8, NYZ), F32),
            pltpu.VMEM((2, 5, NX, 128), F32),
            pltpu.VMEM((4, 8, 128), F32),
            pltpu.VMEM((2, 8, NYZ), F32),
            pltpu.VMEM((2, 5, NX, 128), F32),
            pltpu.VMEM((2, 5, EXT, 128), F32),
            pltpu.VMEM((4, 8, 128), F32),
            pltpu.VMEM((38 * NX, NYZ), BF16),
            pltpu.VMEM((4, 24, 256), F32),
            pltpu.VMEM((4, 24, 256), F32),
            pltpu.VMEM((8, 128), F32),
            pltpu.VMEM((2, 8, 128), F32),
            pltpu.VMEM((8, NYZ), F32),
            pltpu.VMEM((4 * NX, NYZ), F32),
            pltpu.VMEM((8, NYZ), F32),
            pltpu.SemaphoreType.DMA((16,)),
            pltpu.SemaphoreType.DMA((14,)),
            pltpu.SemaphoreType.DMA((14,)),
        ],
        compiler_params=pltpu.CompilerParams(collective_id=0, has_side_effects=True, vmem_limit_bytes=61_800_000),
    )(
        pdfs, link_flags, block_level, grain_pos, grain_vel, grain_radius.reshape(row), grain_cell.reshape(row), contact_pairs,
        contact_spring, iface_source.reshape(row), iface_offset.reshape(row), iface_slot.reshape(row),
        iface_target.reshape(8, 128), migrant_slots,
    )
    read, spread, tgtp, state, spring_next = outs
    result = pl.pallas_call(
        finish_kernel,
        name="finish",
        out_shape=(
            jax.ShapeDtypeStruct((19, NX, NYZ), F32),
            jax.ShapeDtypeStruct((3, NYZ), F32),
            jax.ShapeDtypeStruct((3, NYZ), F32),
            jax.ShapeDtypeStruct(row, F32),
            jax.ShapeDtypeStruct((3, 3072), F32),
        ),
        in_specs=[vmem] * 5,
        out_specs=(hbm,) * 5,
        scratch_shapes=[
            pltpu.VMEM((19, NX, NYZ), F32),
            pltpu.VMEM((3, NYZ), F32),
            pltpu.VMEM((3, NYZ), F32),
            pltpu.VMEM(row, F32),
            pltpu.SemaphoreType.DMA((12,)),
        ],
        compiler_params=pltpu.CompilerParams(vmem_limit_bytes=40 << 20),
    )(read, spread, tgtp, state, spring_next)
    pdfs_next, pos_next, vel_next, rad_next, spring_out = result
    return pdfs_next, pos_next, vel_next, rad_next.reshape(NYZ), spring_out


def solution(mesh):
    both = ("wide", "narrow")
    in_specs = (
        P(None, "wide", "narrow"), P(None, "wide", "narrow"), P("wide", "narrow"), P(None, both), P(None, both), P(both), P(both),
        P(None, both), P(None, both), P(both), P(), P(), P(both), P(None, both),
    )
    out_specs = (P(None, "wide", "narrow"), P(None, both), P(None, both), P(both), P(None, both))
    return jax.shard_map(shards, mesh=mesh, in_specs=in_specs, out_specs=out_specs, check_vma=False)
```

```python
import functools

import jax
import jax.numpy as jnp
from jax import lax
from jax.experimental import pallas as pl
from jax.experimental.pallas import tpu as pltpu
from jax.sharding import PartitionSpec as P

VELOCITY = (
    (0, 0, 0), (1, 0, 0), (-1, 0, 0), (0, 1, 0), (0, -1, 0), (0, 0, 1), (0, 0, -1),
    (1, 1, 0), (-1, -1, 0), (1, -1, 0), (-1, 1, 0), (1, 0, 1), (-1, 0, -1), (1, 0, -1),
    (-1, 0, 1), (0, 1, 1), (0, -1, -1), (0, 1, -1), (0, -1, 1),
)
OPPOSITE = (0, 2, 1, 4, 3, 6, 5, 8, 7, 10, 9, 12, 11, 14, 13, 16, 15, 18, 17)
tau_coarse = 1.0
tau_fine = 1.5
drag_coef = 0.5
mass_coef = 10.0
spring_coef = 0.2
dashpot_coef = 0.05
gravity_z = -0.01
blend_coef = 0.5

ROOT2 = 1.4142135623730951
THREE_BY_ROOT2 = 2.1213203435596424
GROUPS = (tuple(range(19)), ())
NX = 32
NYZ = 1024
TOP = 8
EXT = NX + 16
X_PLUS = (1, 7, 9, 11, 13)
X_MINUS = (2, 8, 10, 12, 14)
Y_PLUS = (3, 7, 10, 15, 17)
Y_MINUS = (4, 8, 9, 16, 18)
DISTANCE = (-2, 2, -1, 1)
MESH = pl.DeviceIdType.MESH
F32 = jnp.float32
BF16 = jnp.bfloat16
NT = (((1,), (1,)), ((), ()))
NN = (((1,), (0,)), ((), ()))


def iota(shape, axis):
    return lax.broadcasted_iota(jnp.int32, shape, axis)


def split2(value):
    high = value.astype(BF16).astype(F32)
    return high, value - high


def split3(value):
    high = value.astype(BF16).astype(F32)
    rest = value - high
    middle = rest.astype(BF16).astype(F32)
    return high, middle, rest - middle


def one_hot(row, size, start=0):
    lanes = row.shape[1]
    return jnp.where(iota((size, lanes), 0) + start == row, 1.0, 0.0).astype(BF16)


def fill_one_hot(ref, row):
    low = one_hot(row & 31, 32)
    high = one_hot(row >> 5, 32)
    for y in range(32):
        ref[y * 32:y * 32 + 32, :] = low * high[y:y + 1, :]


def dot(a, b, dims):
    return lax.dot_general(a, b, dims, preferred_element_type=F32)


def pack_interface(off_ref, slot_ref, src_ref, tgt_ref):
    off = off_ref[...]
    s8 = iota((8, NYZ), 0)
    dval = jnp.where(s8 == 0, DISTANCE[0], jnp.where(s8 == 1, DISTANCE[1], jnp.where(s8 == 2, DISTANCE[2], jnp.where(
        s8 == 3, DISTANCE[3], jnp.where(s8 == 4, 0, 99)))))
    member = jnp.where(off == dval, 1.0, 0.0)
    blocks = [member[:, b * 128:(b + 1) * 128] for b in range(8)]
    before = jnp.where(iota((128, 128), 0) < iota((128, 128), 1), 1.0, 0.0).astype(BF16)
    local = dot(jnp.concatenate(blocks, axis=0).astype(BF16), before, NN)
    running = jnp.zeros((8, 1), F32)
    ranks = []
    for b in range(8):
        ranks.append(local[b * 8:(b + 1) * 8] + running)
        running = running + jnp.sum(blocks[b], axis=1, keepdims=True)
    counts = [running[i:i + 1, :] for i in range(4)]
    ends = []
    total = jnp.zeros((1, 1), F32)
    for i in range(4):
        total = total + (256.0 - counts[i])
        ends.append(total)
    s128 = iota((8, 128), 0)
    base = (s128 * 256).astype(F32)
    positions = []
    for b in range(8):
        sent = jnp.sum(jnp.where(s128 < 4, blocks[b] * (base + ranks[b]), 0.0), axis=0, keepdims=True)
        z = ranks[b][4:5]
        stay = 768.0 + counts[3] + z - ends[2]
        for i in (2, 1, 0):
            start = ends[i - 1] if i else 0.0
            stay = jnp.where(z < ends[i], 256.0 * i + counts[i] + z - start, stay)
        positions.append(sent + blocks[b][4:5] * stay)
    pos = jnp.concatenate(positions, axis=1).astype(jnp.int32)
    src = src_ref[...]
    slot = slot_ref[...]
    values = jnp.where(s8 == 0, src >> 8, jnp.where(s8 == 1, src & 255, jnp.where(s8 == 2, slot >> 8, jnp.where(
        s8 == 3, slot & 255, 0)))).astype(F32)
    pos_high = pos >> 7
    stacked = jnp.concatenate([jnp.where(pos_high == h, values, 0.0) for h in range(8)], axis=0).astype(BF16)
    packed = dot(stacked, one_hot(pos & 127, 128), NT)
    src_packed = jnp.concatenate([packed[h * 8:h * 8 + 1] * 256.0 + packed[h * 8 + 1:h * 8 + 2] for h in range(8)], axis=1)
    slot_high = jnp.concatenate([packed[h * 8 + 2:h * 8 + 3] for h in range(8)], axis=1).astype(jnp.int32)
    slot_low = jnp.concatenate([packed[h * 8 + 3:h * 8 + 4] for h in range(8)], axis=1).astype(jnp.int32)
    slot_packed = slot_high * 256 + slot_low
    tgt = tgt_ref[...]
    table = jnp.concatenate([(tgt >> 8).astype(F32), (tgt & 255).astype(F32)], axis=0).astype(BF16)
    found = dot(table, one_hot(slot_packed & 127, 128), NN)
    chosen = s8 == (slot_packed >> 7)
    tgt_high = jnp.sum(jnp.where(chosen, found[0:8], 0.0), axis=0, keepdims=True)
    tgt_low = jnp.sum(jnp.where(chosen, found[8:16], 0.0), axis=0, keepdims=True)
    tgt_packed = (tgt_high * 256.0 + tgt_low).astype(jnp.int32)
    return src_packed.astype(jnp.int32), tgt_packed, counts


def step_kernel(
    pdfs_hbm, flags_hbm, level_hbm, pos_hbm, vel_hbm, rad_hbm, cell_hbm, pairs_hbm, spring_hbm, src_hbm, off_hbm, slot_hbm,
    tgt_hbm, mig_hbm,
    read_ref, spread_ref, tgtp_ref, result_ref, spring_out_ref,
    pdfs, flags, level, pos_ref, vel_ref, rad_ref, cell_ref, pairs_ref, spring_ref, src_ref, off_ref, slot_ref, tgt_ref,
    mig_ref,
    onehot, source_hot, moved_in, ext, velf, velb, vel8, rows16, edge_x, edge_y, edge_c, halo_x, halo_y, halo_yp, halo_c, splits,
    gathered, received, leaving, joined, fluid, force, state_ref,
    load_sem, send_sem, recv_sem,
):
    a, b = lax.axis_index("wide"), lax.axis_index("narrow")
    n_wide, n_narrow = lax.axis_size("wide"), lax.axis_size("narrow")

    def device(dx, dy):
        return (lax.rem(a + dx + n_wide, n_wide), lax.rem(b + dy + n_narrow, n_narrow))

    small = [
        (cell_hbm, cell_ref), (off_hbm, off_ref), (slot_hbm, slot_ref), (src_hbm, src_ref), (tgt_hbm, tgt_ref),
        (rad_hbm, rad_ref), (vel_hbm, vel_ref), (pairs_hbm, pairs_ref), (spring_hbm, spring_ref), (pos_hbm, pos_ref),
        (mig_hbm, mig_ref), (level_hbm, level),
    ]
    parts = [slice(i * 256, (i + 1) * 256) for i in range(4)]
    large = [(pdfs_hbm.at[:, :, part], pdfs.at[:, :, part]) for part in parts] + [(flags_hbm, flags)]
    loads = [pltpu.make_async_copy(x, y, load_sem.at[i]) for i, (x, y) in enumerate(small + large)]
    for load in loads:
        load.start()
    around = [(dx, dy) for dx in (-1, 0, 1) for dy in (-1, 0, 1) if dx or dy] + [(-2, 0), (2, 0)]
    barrier = pltpu.get_barrier_semaphore()
    for dx, dy in around:
        pl.semaphore_signal(barrier, inc=1, device_id=device(dx, dy), device_id_type=MESH)
    for load in loads[:12]:
        load.wait()

    src_packed, tgt_packed, counts = pack_interface(off_ref, slot_ref, src_ref, tgt_ref)
    tgtp_ref[...] = tgt_packed

    cell = cell_ref[...]
    grain_x = cell >> 10
    fill_one_hot(onehot, cell & 1023)
    drag = drag_coef * rad_ref[...]
    in_row = one_hot(grain_x, NX)
    weights = [drag] + [drag * vel_ref[c:c + 1, :] for c in range(3)]
    for k, weight in enumerate(weights):
        for part, value in enumerate(split2(weight)):
            moved_in[(part * 4 + k) * NX:(part * 4 + k + 1) * NX, :] = in_row * value.astype(BF16)
    fill_one_hot(source_hot, src_packed & 1023)

    fine = level[0] == 1
    tau = jnp.where(fine, tau_fine, tau_coarse).astype(F32)
    omega = jnp.where(fine, 1.0 / tau_fine, 1.0 / tau_coarse).astype(F32)
    keep = jnp.where(fine, 1.0 - 1.0 / tau_fine, 0.0).astype(F32)

    def bring(i):
        cols = slice(i * 512, (i + 1) * 512)
        got = dot(moved_in[...], onehot[cols, :], NT)
        force[:, cols] = got[0:128] + got[128:256]

    def collide(row, col):
        rows = slice(row, row + 8)
        cols = slice(col, col + 128)
        p = [pdfs[q, rows, cols] for q in range(19)]
        pair_sum = {q: p[q] + p[q + 1] for q in range(1, 19, 2)}
        pair_dif = {q: p[q] - p[q + 1] for q in range(1, 19, 2)}
        density = p[0] + ((pair_sum[1] + pair_sum[3]) + (pair_sum[5] + pair_sum[7])) + (
            (pair_sum[9] + pair_sum[11]) + (pair_sum[13] + pair_sum[15]) + pair_sum[17])
        mom = (
            (pair_dif[1] + pair_dif[7]) + (pair_dif[9] + pair_dif[11]) + pair_dif[13],
            (pair_dif[3] + pair_dif[7]) + (pair_dif[15] - pair_dif[9]) + pair_dif[17],
            (pair_dif[5] + pair_dif[11]) + (pair_dif[15] - pair_dif[13]) - pair_dif[17],
        )
        inverse = 1.0 / density
        pull = tau * inverse
        resist = force[rows, cols]
        shifted = []
        for c in range(3):
            v = mom[c] * inverse
            velf[c * NX + row:c * NX + row + 8, cols] = v
            shifted.append(THREE_BY_ROOT2 * (v + pull * (force[(c + 1) * NX + row:(c + 1) * NX + row + 8, cols] - v * resist)))
        base = 1.0 - (shifted[0] * shifted[0] + shifted[1] * shifted[1] + shifted[2] * shifted[2]) * (1.0 / 3.0)
        dense = omega * density
        slim = dense * (1.0 / 36.0)
        wide = slim + slim
        slim_base = slim * base
        wide_base = slim_base + slim_base
        out_rows = slice(TOP + row, TOP + row + 8)
        ext[0, out_rows, cols] = keep * p[0] + 6.0 * wide_base
        for q in range(1, 19, 2):
            along = None
            for c in range(3):
                if VELOCITY[q][c] == 1:
                    along = shifted[c] if along is None else along + shifted[c]
                elif VELOCITY[q][c] == -1:
                    along = along - shifted[c]
            scaled = (wide if q < 7 else slim) * along
            even = (wide_base if q < 7 else slim_base) + scaled * along
            odd = ROOT2 * scaled
            ext[q, out_rows, cols] = keep * p[q] + (even + odd)
            ext[q + 1, out_rows, cols] = keep * p[q + 1] + (even - odd)

    def contacts_in():
        vel8[...] = jnp.zeros_like(vel8)
        vel8[0:3, :] = vel_ref[...]
        vel8[4:7, :] = vel_ref[...]
        tables = [vel8[:, h * 128:(h + 1) * 128] for h in range(8)]
        half = iota((8, 128), 0) < 4
        for c in range(24):
            cols = slice(c * 128, (c + 1) * 128)
            index = jnp.where(half, pairs_ref[0:1, cols], pairs_ref[1:2, cols])
            low = index & 127
            high = index >> 7
            found = jnp.take_along_axis(tables[0], low, axis=1, mode="promise_in_bounds")
            for h in range(1, 8):
                found = jnp.where(high == h, jnp.take_along_axis(tables[h], low, axis=1, mode="promise_in_bounds"), found)
            relative = found[4:7] - found[0:3]
            spring = spring_ref[:, cols]
            spring_out_ref[:, cols] = spring + relative
            contact = spring_coef * spring + dashpot_coef * relative
            for part, value in enumerate(split3(contact)):
                rows16[part * 3:part * 3 + 3, cols] = value

    def contacts_out():
        rows16[9:16, :] = jnp.zeros((7, 3072), F32)
        forces = rows16[...]
        spread = []
        hots = []
        for side in range(2):
            index = pairs_ref[side:side + 1, :]
            high = index >> 7
            signed = -forces if side else forces
            spread.append(jnp.concatenate([jnp.where(high == h, signed, 0.0).astype(BF16) for h in range(8)], axis=0))
            hots.append(one_hot(index & 127, 128))
        summed = dot(jnp.concatenate(spread, axis=1), jnp.concatenate(hots, axis=1), NT)
        parts = [
            summed[h * 16:h * 16 + 3] + summed[h * 16 + 3:h * 16 + 6] + summed[h * 16 + 6:h * 16 + 9] for h in range(8)]
        return jnp.concatenate(parts, axis=1)

    bring(0)
    contacts_in()
    summed = contacts_out()
    for i in range(4):
        loads[12 + i].wait()
    bring(1)
    for col in range(0, NYZ, 128):
        for row in range(0, NX, 8):
            collide(row, col)

    for k in range(5):
        edge_x[0, k:k + 1, :] = ext[X_PLUS[k], TOP + NX - 1:TOP + NX, :]
        edge_x[1, k:k + 1, :] = ext[X_MINUS[k], TOP:TOP + 1, :]
    group = iota((NX, 128), 1) >> 5
    for side, (dirs, start, base) in enumerate(((Y_PLUS, 896, 32), (Y_MINUS, 0, 0))):
        tiles = [ext[q, TOP:TOP + NX, start:start + 128] for q in dirs]
        moved = [pltpu.roll(t, (base + 32 * k) % 128, 1) if (base + 32 * k) % 128 else t for k, t in enumerate(tiles)]
        edge_y[side, 0] = jnp.where(group == 0, moved[0], jnp.where(group == 1, moved[1], jnp.where(group == 2, moved[2], moved[3])))
        edge_y[side, 1] = moved[4]
    edge_c[0, 0:1, :] = ext[7, TOP + NX - 1:TOP + NX, 896:1024]
    edge_c[1, 0:1, :] = ext[8, TOP:TOP + 1, 0:128]
    edge_c[2, 0:1, :] = ext[9, TOP + NX - 1:TOP + NX, 0:128]
    edge_c[3, 0:1, :] = ext[10, TOP:TOP + 1, 896:1024]
    pl.semaphore_wait(barrier, len(around))

    def send(index, source, target, dx, dy):
        copy = pltpu.make_async_remote_copy(
            src_ref=source, dst_ref=target, send_sem=send_sem.at[index], recv_sem=recv_sem.at[index],
            device_id=device(dx, dy), device_id_type=MESH)
        copy.start()
        return copy

    halo = [
        send(4, edge_c.at[0], halo_c.at[0], 1, 1),
        send(5, edge_c.at[1], halo_c.at[1], -1, -1),
        send(6, edge_c.at[2], halo_c.at[2], 1, -1),
        send(7, edge_c.at[3], halo_c.at[3], -1, 1),
        send(0, edge_x.at[0], halo_x.at[0], 1, 0),
        send(1, edge_x.at[1], halo_x.at[1], -1, 0),
        send(2, edge_y.at[0], halo_y.at[0], 0, 1),
        send(3, edge_y.at[1], halo_y.at[1], 0, -1),
    ]

    def fluid_at_grains():
        for part, value in enumerate(split2(velf[...])):
            velb[part * 96:part * 96 + 96, :] = value.astype(BF16)
        for i in range(2):
            cols = slice(i * 512, (i + 1) * 512)
            got = dot(velb[...], onehot[:, cols], NN)
            got = got[0:96] + got[96:192]
            here = iota((NX, 512), 0) == (cell_ref[:, cols] >> 10)
            for c in range(3):
                fluid[c:c + 1, cols] = jnp.sum(jnp.where(here, got[c * NX:(c + 1) * NX], 0.0), axis=0, keepdims=True)

    lane = iota((NX, 128), 1)

    def stream(group):
        for k, q in enumerate(group):
            cx, cy, cz = VELOCITY[q]
            shift = cy * 32 + cz
            rows = slice(TOP - cx, TOP - cx + NX)
            value = ext[q, rows, :]
            if shift:
                value = pltpu.roll(value, shift % NYZ, 1)
            if cy == 1:
                edge = pltpu.roll(halo_yp[0, Y_PLUS.index(q), rows, :], shift % 128, 1)
                value = jnp.concatenate([jnp.where(lane < 32, edge, value[:, 0:128]), value[:, 128:]], axis=1)
            if cy == -1:
                edge = pltpu.roll(halo_yp[1, Y_MINUS.index(q), rows, :], shift % 128, 1)
                value = jnp.concatenate([value[:, :896], jnp.where(lane >= 96, edge, value[:, 896:])], axis=1)
            if q:
                bit = 1 << (q if q < 10 else q - 10)
                solid = (flags[0 if q < 10 else 1] & bit) != 0
                value = jnp.where(solid, ext[OPPOSITE[q], TOP:TOP + NX, :], value)
            read_ref[q] = value
            high = value.astype(BF16)
            at = group[0] * 2 * NX + k * NX
            splits[at:at + NX, :] = high
            splits[at + len(group) * NX:at + (len(group) + 1) * NX, :] = (value - high.astype(F32)).astype(BF16)

    def extract(group, i, width=1):
        cols = slice(i * 256, (i + width) * 256)
        at, size = group[0] * 2 * NX, len(group) * NX
        got = dot(splits[at:at + 2 * size, :], source_hot[:, cols], NN)
        here = iota((NX, 256 * width), 0) == (src_packed[:, cols] >> 10)
        for k, q in enumerate(group):
            value = got[k * NX:(k + 1) * NX] + got[size + k * NX:size + (k + 1) * NX]
            value = jnp.sum(jnp.where(here, value, 0.0), axis=0, keepdims=True)
            for w in range(width):
                gathered[i + w, q:q + 1, :] = value[:, w * 256:(w + 1) * 256]

    def move_grains(summed):
        radius = rad_ref[...]
        vel = vel_ref[...]
        total = (drag_coef * radius) * (fluid[0:3, :] - vel) + summed
        mass = mass_coef * radius * radius * radius
        falling = jnp.where(iota((3, NYZ), 0) == 2, gravity_z, 0.0)
        moved_vel = vel + total / mass + falling
        state_ref[0:3, :] = pos_ref[...] + moved_vel
        state_ref[3:6, :] = moved_vel
        state_ref[6:7, :] = radius
        state_ref[7:8, :] = jnp.ones_like(radius)

    def leave():
        slots = jnp.concatenate([mig_ref[0:1, :], mig_ref[1:2, :]], axis=1)
        state = jnp.concatenate(split3(state_ref[...]), axis=0).astype(BF16)
        out = dot(state, one_hot(slots, NYZ), NN)
        leaving[...] = out[0:8] + out[8:16] + out[16:24]

    rows_out = []

    def send_region(i):
        rows_out.append(send(10 + i, gathered.at[i], received.at[i], DISTANCE[i], 0))

    fluid_at_grains()
    loads[16].wait()
    for copy in halo:
        copy.wait()
    for k in range(5):
        ext[X_PLUS[k], TOP - 1:TOP, :] = halo_x[0, k:k + 1, :]
        ext[X_MINUS[k], TOP + NX:TOP + NX + 1, :] = halo_x[1, k:k + 1, :]
        for side, base in enumerate((96, 0)):
            back = (base - 32 * k) % 128
            tile = halo_y[side, k // 4]
            halo_yp[side, k, TOP:TOP + NX, :] = pltpu.roll(tile, back, 1) if back else tile
    halo_yp[0, 1, TOP - 1:TOP, :] = halo_c[0, 0:1, :]
    halo_yp[1, 1, TOP + NX:TOP + NX + 1, :] = halo_c[1, 0:1, :]
    halo_yp[1, 2, TOP - 1:TOP, :] = halo_c[2, 0:1, :]
    halo_yp[0, 2, TOP + NX:TOP + NX + 1, :] = halo_c[3, 0:1, :]
    stream(GROUPS[0])
    extract(GROUPS[0], 0, 2)
    send_region(0)
    send_region(1)
    extract(GROUPS[0], 2, 2)
    send_region(2)
    send_region(3)
    move_grains(summed)
    leave()
    migrate = [send(8, leaving, joined.at[0], -1, 0), send(9, leaving, joined.at[1], 1, 0)]

    for i in range(4):
        cols = slice(i * 256, (i + 1) * 256)
        rows_out[i].wait()
        stays = iota((24, 256), 1).astype(F32) >= counts[i]
        carried = jnp.where(stays, gathered[i], received[i])
        here = one_hot(tgt_packed[:, cols] >> 10, NX)
        for q in range(19):
            for part, value in enumerate(split2(carried[q:q + 1, :])):
                spread_ref[(part * 19 + q) * NX:(part * 19 + q + 1) * NX, cols] = here * value.astype(BF16)
        spread_ref[38 * NX:39 * NX, cols] = here

    for copy in migrate:
        copy.wait()
    mig_lane = iota((8, 128), 1)
    change = jnp.where(iota((8, 128), 0) == 0, jnp.where(mig_lane < 64, float(NX), -float(NX)), 0.0)
    newcomers = jnp.where(mig_lane < 64, joined[0], joined[1]) + change
    slots = jnp.concatenate([mig_ref[0:1, :], mig_ref[1:2, :]], axis=1)
    placed = dot(jnp.concatenate(split3(newcomers), axis=0).astype(BF16), one_hot(slots, NYZ), NT)
    placed = placed[0:8] + placed[8:16] + placed[16:24]
    result_ref[...] = jnp.where(placed[7:8] > 0.5, placed, state_ref[...])


def finish_kernel(
    read_ref, spread_ref, tgtp_ref, result_ref, spring_ref,
    next_hbm, pos_hbm, vel_hbm, rad_hbm, spring_hbm,
    blended, pos, vel, rad, sem,
):
    pos[...] = result_ref[0:3, :]
    vel[...] = result_ref[3:6, :]
    rad[...] = result_ref[6:7, :]
    copies = []
    for source, target in ((spring_ref, spring_hbm), (pos, pos_hbm), (vel, vel_hbm), (rad, rad_hbm)):
        copies.append(pltpu.make_async_copy(source, target, sem.at[len(copies)]))
        copies[-1].start()

    row = tgtp_ref[...] & 1023
    for i in range(2):
        cols = slice(i * 512, (i + 1) * 512)
        got = dot(spread_ref[...], one_hot(row, 512, i * 512), NT)
        hit = got[38 * NX:39 * NX] > 0.5
        for start, stop in ((0, 10), (10, 19)):
            for q in range(start, stop):
                value = read_ref[q, :, cols]
                carried = got[q * NX:(q + 1) * NX] + got[(19 + q) * NX:(20 + q) * NX]
                blended[q, :, cols] = jnp.where(hit, blend_coef * (value + carried), value)
            copies.append(pltpu.make_async_copy(
                blended.at[start:stop, :, cols], next_hbm.at[start:stop, :, cols], sem.at[len(copies)]))
            copies[-1].start()
    for copy in copies:
        copy.wait()


def shards(
    pdfs, link_flags, block_level, grain_pos, grain_vel, grain_radius, grain_cell, contact_pairs, contact_spring, iface_source,
    iface_offset, iface_slot, iface_target, migrant_slots,
):
    row = (1, NYZ)
    vmem = pl.BlockSpec(memory_space=pltpu.VMEM)
    hbm = pl.BlockSpec(memory_space=pl.ANY)
    outs = pl.pallas_call(
        step_kernel,
        name="step",
        out_shape=(
            pltpu.VMEM((19, NX, NYZ), F32),
            pltpu.VMEM((39 * NX, NYZ), BF16),
            pltpu.VMEM(row, jnp.int32),
            pltpu.VMEM((8, NYZ), F32),
            pltpu.VMEM((3, 3072), F32),
        ),
        in_specs=[hbm] * 14,
        out_specs=(vmem,) * 5,
        scratch_shapes=[
            pltpu.VMEM((19, NX, NYZ), F32),
            pltpu.VMEM((2, NX, NYZ), jnp.int32),
            pltpu.SMEM((1,), jnp.int32),
            pltpu.VMEM((3, NYZ), F32),
            pltpu.VMEM((3, NYZ), F32),
            pltpu.VMEM(row, F32),
            pltpu.VMEM(row, jnp.int32),
            pltpu.VMEM((2, 3072), jnp.int32),
            pltpu.VMEM((3, 3072), F32),
            pltpu.VMEM(row, jnp.int32),
            pltpu.VMEM(row, jnp.int32),
            pltpu.VMEM(row, jnp.int32),
            pltpu.VMEM((8, 128), jnp.int32),
            pltpu.VMEM((2, 64), jnp.int32),
            pltpu.VMEM((NYZ, NYZ), BF16),
            pltpu.VMEM((NYZ, NYZ), BF16),
            pltpu.VMEM((8 * NX, NYZ), BF16),
            pltpu.VMEM((19, EXT, NYZ), F32),
            pltpu.VMEM((3 * NX, NYZ), F32),
            pltpu.VMEM((6 * NX, NYZ), BF16),
            pltpu.VMEM((8, NYZ), F32),
            pltpu.VMEM((16, 3072), F32),
            pltpu.VMEM((2, 8, NYZ), F32),
            pltpu.VMEM((2, 2, NX, 128), F32),
            pltpu.VMEM((4, 8, 128), F32),
            pltpu.VMEM((2, 8, NYZ), F32),
            pltpu.VMEM((2, 2, NX, 128), F32),
            pltpu.VMEM((2, 5, EXT, 128), F32),
            pltpu.VMEM((4, 8, 128), F32),
            pltpu.VMEM((38 * NX, NYZ), BF16),
            pltpu.VMEM((4, 24, 256), F32),
            pltpu.VMEM((4, 24, 256), F32),
            pltpu.VMEM((8, 128), F32),
            pltpu.VMEM((2, 8, 128), F32),
            pltpu.VMEM((8, NYZ), F32),
            pltpu.VMEM((4 * NX, NYZ), F32),
            pltpu.VMEM((8, NYZ), F32),
            pltpu.SemaphoreType.DMA((17,)),
            pltpu.SemaphoreType.DMA((14,)),
            pltpu.SemaphoreType.DMA((14,)),
        ],
        compiler_params=pltpu.CompilerParams(collective_id=0, has_side_effects=True, vmem_limit_bytes=61_800_000),
    )(
        pdfs, link_flags, block_level.reshape(1), grain_pos, grain_vel, grain_radius.reshape(row), grain_cell.reshape(row), contact_pairs,
        contact_spring, iface_source.reshape(row), iface_offset.reshape(row), iface_slot.reshape(row),
        iface_target.reshape(8, 128), migrant_slots,
    )
    read, spread, tgtp, state, spring_next = outs
    result = pl.pallas_call(
        finish_kernel,
        name="finish",
        out_shape=(
            jax.ShapeDtypeStruct((19, NX, NYZ), F32),
            jax.ShapeDtypeStruct((3, NYZ), F32),
            jax.ShapeDtypeStruct((3, NYZ), F32),
            jax.ShapeDtypeStruct(row, F32),
            jax.ShapeDtypeStruct((3, 3072), F32),
        ),
        in_specs=[vmem] * 5,
        out_specs=(hbm,) * 5,
        scratch_shapes=[
            pltpu.VMEM((19, NX, NYZ), F32),
            pltpu.VMEM((3, NYZ), F32),
            pltpu.VMEM((3, NYZ), F32),
            pltpu.VMEM(row, F32),
            pltpu.SemaphoreType.DMA((12,)),
        ],
        compiler_params=pltpu.CompilerParams(vmem_limit_bytes=40 << 20),
    )(read, spread, tgtp, state, spring_next)
    pdfs_next, pos_next, vel_next, rad_next, spring_out = result
    return pdfs_next, pos_next, vel_next, rad_next.reshape(NYZ), spring_out


def solution(mesh):
    both = ("wide", "narrow")
    in_specs = (
        P(None, "wide", "narrow"), P(None, "wide", "narrow"), P("wide", "narrow"), P(None, both), P(None, both), P(both), P(both),
        P(None, both), P(None, both), P(both), P(), P(), P(both), P(None, both),
    )
    out_specs = (P(None, "wide", "narrow"), P(None, both), P(None, both), P(both), P(None, both))
    return jax.shard_map(shards, mesh=mesh, in_specs=in_specs, out_specs=out_specs, check_vma=False)
```

```python
import functools

import jax
import jax.numpy as jnp
from jax import lax
from jax.experimental import pallas as pl
from jax.experimental.pallas import tpu as pltpu
from jax.sharding import PartitionSpec as P

VELOCITY = (
    (0, 0, 0), (1, 0, 0), (-1, 0, 0), (0, 1, 0), (0, -1, 0), (0, 0, 1), (0, 0, -1),
    (1, 1, 0), (-1, -1, 0), (1, -1, 0), (-1, 1, 0), (1, 0, 1), (-1, 0, -1), (1, 0, -1),
    (-1, 0, 1), (0, 1, 1), (0, -1, -1), (0, 1, -1), (0, -1, 1),
)
OPPOSITE = (0, 2, 1, 4, 3, 6, 5, 8, 7, 10, 9, 12, 11, 14, 13, 16, 15, 18, 17)
tau_coarse = 1.0
tau_fine = 1.5
drag_coef = 0.5
mass_coef = 10.0
spring_coef = 0.2
dashpot_coef = 0.05
gravity_z = -0.01
blend_coef = 0.5

ROOT2 = 1.4142135623730951
THREE_BY_ROOT2 = 2.1213203435596424
GROUPS = (tuple(range(19)), ())
NX = 32
NYZ = 1024
TOP = 8
EXT = NX + 16
X_PLUS = (1, 7, 9, 11, 13)
X_MINUS = (2, 8, 10, 12, 14)
Y_PLUS = (3, 7, 10, 15, 17)
Y_MINUS = (4, 8, 9, 16, 18)
DISTANCE = (-2, 2, -1, 1)
MESH = pl.DeviceIdType.MESH
F32 = jnp.float32
BF16 = jnp.bfloat16
NT = (((1,), (1,)), ((), ()))
NN = (((1,), (0,)), ((), ()))


def iota(shape, axis):
    return lax.broadcasted_iota(jnp.int32, shape, axis)


def split2(value):
    high = value.astype(BF16).astype(F32)
    return high, value - high


def split3(value):
    high = value.astype(BF16).astype(F32)
    rest = value - high
    middle = rest.astype(BF16).astype(F32)
    return high, middle, rest - middle


def one_hot(row, size, start=0):
    lanes = row.shape[1]
    return jnp.where(iota((size, lanes), 0) + start == row, 1.0, 0.0).astype(BF16)


def fill_one_hot(ref, row):
    low = one_hot(row & 31, 32)
    high = one_hot(row >> 5, 32)
    for y in range(32):
        ref[y * 32:y * 32 + 32, :] = low * high[y:y + 1, :]


def dot(a, b, dims):
    return lax.dot_general(a, b, dims, preferred_element_type=F32)


def pack_interface(off_ref, slot_ref, src_ref, tgt_ref):
    off = off_ref[...]
    s8 = iota((8, NYZ), 0)
    dval = jnp.where(s8 == 0, DISTANCE[0], jnp.where(s8 == 1, DISTANCE[1], jnp.where(s8 == 2, DISTANCE[2], jnp.where(
        s8 == 3, DISTANCE[3], jnp.where(s8 == 4, 0, 99)))))
    member = jnp.where(off == dval, 1.0, 0.0)
    blocks = [member[:, b * 128:(b + 1) * 128] for b in range(8)]
    before = jnp.where(iota((128, 128), 0) < iota((128, 128), 1), 1.0, 0.0).astype(BF16)
    local = dot(jnp.concatenate(blocks, axis=0).astype(BF16), before, NN)
    running = jnp.zeros((8, 1), F32)
    ranks = []
    for b in range(8):
        ranks.append(local[b * 8:(b + 1) * 8] + running)
        running = running + jnp.sum(blocks[b], axis=1, keepdims=True)
    counts = [running[i:i + 1, :] for i in range(4)]
    ends = []
    total = jnp.zeros((1, 1), F32)
    for i in range(4):
        total = total + (256.0 - counts[i])
        ends.append(total)
    s128 = iota((8, 128), 0)
    base = (s128 * 256).astype(F32)
    positions = []
    for b in range(8):
        sent = jnp.sum(jnp.where(s128 < 4, blocks[b] * (base + ranks[b]), 0.0), axis=0, keepdims=True)
        z = ranks[b][4:5]
        stay = 768.0 + counts[3] + z - ends[2]
        for i in (2, 1, 0):
            start = ends[i - 1] if i else 0.0
            stay = jnp.where(z < ends[i], 256.0 * i + counts[i] + z - start, stay)
        positions.append(sent + blocks[b][4:5] * stay)
    pos = jnp.concatenate(positions, axis=1).astype(jnp.int32)
    src = src_ref[...]
    slot = slot_ref[...]
    values = jnp.where(s8 == 0, src >> 8, jnp.where(s8 == 1, src & 255, jnp.where(s8 == 2, slot >> 8, jnp.where(
        s8 == 3, slot & 255, 0)))).astype(F32)
    pos_high = pos >> 7
    stacked = jnp.concatenate([jnp.where(pos_high == h, values, 0.0) for h in range(8)], axis=0).astype(BF16)
    packed = dot(stacked, one_hot(pos & 127, 128), NT)
    src_packed = jnp.concatenate([packed[h * 8:h * 8 + 1] * 256.0 + packed[h * 8 + 1:h * 8 + 2] for h in range(8)], axis=1)
    slot_high = jnp.concatenate([packed[h * 8 + 2:h * 8 + 3] for h in range(8)], axis=1).astype(jnp.int32)
    slot_low = jnp.concatenate([packed[h * 8 + 3:h * 8 + 4] for h in range(8)], axis=1).astype(jnp.int32)
    slot_packed = slot_high * 256 + slot_low
    tgt = tgt_ref[...]
    table = jnp.concatenate([(tgt >> 8).astype(F32), (tgt & 255).astype(F32)], axis=0).astype(BF16)
    found = dot(table, one_hot(slot_packed & 127, 128), NN)
    chosen = s8 == (slot_packed >> 7)
    tgt_high = jnp.sum(jnp.where(chosen, found[0:8], 0.0), axis=0, keepdims=True)
    tgt_low = jnp.sum(jnp.where(chosen, found[8:16], 0.0), axis=0, keepdims=True)
    tgt_packed = (tgt_high * 256.0 + tgt_low).astype(jnp.int32)
    return src_packed.astype(jnp.int32), tgt_packed, counts


def step_kernel(
    pdfs_hbm, flags_hbm, level_hbm, pos_hbm, vel_hbm, rad_hbm, cell_hbm, pairs_hbm, spring_hbm, src_hbm, off_hbm, slot_hbm,
    tgt_hbm, mig_hbm,
    read_ref, spread_ref, tgtp_ref, result_ref, spring_out_ref,
    pdfs, flags, level, pos_ref, vel_ref, rad_ref, cell_ref, pairs_ref, spring_ref, src_ref, off_ref, slot_ref, tgt_ref,
    mig_ref,
    onehot, source_hot, moved_in, ext, velf, velb, vel8, rows16, edge_x, edge_y, edge_c, halo_x, halo_y, halo_yp, halo_c, splits,
    gathered, received, leaving, joined, fluid, force, state_ref, pull_ref,
    load_sem, send_sem, recv_sem,
):
    a, b = lax.axis_index("wide"), lax.axis_index("narrow")
    n_wide, n_narrow = lax.axis_size("wide"), lax.axis_size("narrow")

    def device(dx, dy):
        return (lax.rem(a + dx + n_wide, n_wide), lax.rem(b + dy + n_narrow, n_narrow))

    small = [
        (cell_hbm, cell_ref), (off_hbm, off_ref), (slot_hbm, slot_ref), (src_hbm, src_ref), (tgt_hbm, tgt_ref),
        (rad_hbm, rad_ref), (vel_hbm, vel_ref), (pairs_hbm, pairs_ref), (spring_hbm, spring_ref), (pos_hbm, pos_ref),
        (mig_hbm, mig_ref), (level_hbm, level),
    ]
    parts = [slice(i * 256, (i + 1) * 256) for i in range(4)]
    large = [(pdfs_hbm.at[:, :, part], pdfs.at[:, :, part]) for part in parts] + [(flags_hbm, flags)]
    loads = [pltpu.make_async_copy(x, y, load_sem.at[i]) for i, (x, y) in enumerate(small + large)]
    for load in loads:
        load.start()
    around = [(dx, dy) for dx in (-1, 0, 1) for dy in (-1, 0, 1) if dx or dy] + [(-2, 0), (2, 0)]
    barrier = pltpu.get_barrier_semaphore()
    for dx, dy in around:
        pl.semaphore_signal(barrier, inc=1, device_id=device(dx, dy), device_id_type=MESH)
    for load in loads[:12]:
        load.wait()

    src_packed, tgt_packed, counts = pack_interface(off_ref, slot_ref, src_ref, tgt_ref)
    tgtp_ref[...] = tgt_packed

    cell = cell_ref[...]
    grain_x = cell >> 10
    fill_one_hot(onehot, cell & 1023)
    drag = drag_coef * rad_ref[...]
    in_row = one_hot(grain_x, NX)
    weights = [drag] + [drag * vel_ref[c:c + 1, :] for c in range(3)]
    for k, weight in enumerate(weights):
        for part, value in enumerate(split2(weight)):
            moved_in[(part * 4 + k) * NX:(part * 4 + k + 1) * NX, :] = in_row * value.astype(BF16)
    fill_one_hot(source_hot, src_packed & 1023)

    fine = level[0] == 1
    tau = jnp.where(fine, tau_fine, tau_coarse).astype(F32)
    omega = jnp.where(fine, 1.0 / tau_fine, 1.0 / tau_coarse).astype(F32)
    keep = jnp.where(fine, 1.0 - 1.0 / tau_fine, 0.0).astype(F32)

    def bring(i):
        cols = slice(i * 512, (i + 1) * 512)
        got = dot(moved_in[...], onehot[cols, :], NT)
        force[:, cols] = got[0:128] + got[128:256]

    def collide(row, col):
        rows = slice(row, row + 8)
        cols = slice(col, col + 128)
        p = [pdfs[q, rows, cols] for q in range(19)]
        pair_sum = {q: p[q] + p[q + 1] for q in range(1, 19, 2)}
        pair_dif = {q: p[q] - p[q + 1] for q in range(1, 19, 2)}
        density = p[0] + ((pair_sum[1] + pair_sum[3]) + (pair_sum[5] + pair_sum[7])) + (
            (pair_sum[9] + pair_sum[11]) + (pair_sum[13] + pair_sum[15]) + pair_sum[17])
        mom = (
            (pair_dif[1] + pair_dif[7]) + (pair_dif[9] + pair_dif[11]) + pair_dif[13],
            (pair_dif[3] + pair_dif[7]) + (pair_dif[15] - pair_dif[9]) + pair_dif[17],
            (pair_dif[5] + pair_dif[11]) + (pair_dif[15] - pair_dif[13]) - pair_dif[17],
        )
        inverse = 1.0 / density
        pull = tau * inverse
        resist = force[rows, cols]
        shifted = []
        for c in range(3):
            v = mom[c] * inverse
            velf[c * NX + row:c * NX + row + 8, cols] = v
            shifted.append(THREE_BY_ROOT2 * (v + pull * (force[(c + 1) * NX + row:(c + 1) * NX + row + 8, cols] - v * resist)))
        base = 1.0 - (shifted[0] * shifted[0] + shifted[1] * shifted[1] + shifted[2] * shifted[2]) * (1.0 / 3.0)
        dense = omega * density
        slim = dense * (1.0 / 36.0)
        wide = slim + slim
        slim_base = slim * base
        wide_base = slim_base + slim_base
        out_rows = slice(TOP + row, TOP + row + 8)
        ext[0, out_rows, cols] = keep * p[0] + 6.0 * wide_base
        for q in range(1, 19, 2):
            along = None
            for c in range(3):
                if VELOCITY[q][c] == 1:
                    along = shifted[c] if along is None else along + shifted[c]
                elif VELOCITY[q][c] == -1:
                    along = along - shifted[c]
            scaled = (wide if q < 7 else slim) * along
            even = (wide_base if q < 7 else slim_base) + scaled * along
            odd = ROOT2 * scaled
            ext[q, out_rows, cols] = keep * p[q] + (even + odd)
            ext[q + 1, out_rows, cols] = keep * p[q + 1] + (even - odd)

    def contacts_in():
        vel8[...] = jnp.zeros_like(vel8)
        vel8[0:3, :] = vel_ref[...]
        vel8[4:7, :] = vel_ref[...]
        tables = [vel8[:, h * 128:(h + 1) * 128] for h in range(8)]
        half = iota((8, 128), 0) < 4
        for c in range(24):
            cols = slice(c * 128, (c + 1) * 128)
            index = jnp.where(half, pairs_ref[0:1, cols], pairs_ref[1:2, cols])
            low = index & 127
            high = index >> 7
            found = jnp.take_along_axis(tables[0], low, axis=1, mode="promise_in_bounds")
            for h in range(1, 8):
                found = jnp.where(high == h, jnp.take_along_axis(tables[h], low, axis=1, mode="promise_in_bounds"), found)
            relative = found[4:7] - found[0:3]
            spring = spring_ref[:, cols]
            spring_out_ref[:, cols] = spring + relative
            contact = spring_coef * spring + dashpot_coef * relative
            for part, value in enumerate(split3(contact)):
                rows16[part * 3:part * 3 + 3, cols] = value

    def contacts_out():
        rows16[9:16, :] = jnp.zeros((7, 3072), F32)
        forces = rows16[...]
        spread = []
        hots = []
        for side in range(2):
            index = pairs_ref[side:side + 1, :]
            high = index >> 7
            signed = -forces if side else forces
            spread.append(jnp.concatenate([jnp.where(high == h, signed, 0.0).astype(BF16) for h in range(8)], axis=0))
            hots.append(one_hot(index & 127, 128))
        summed = dot(jnp.concatenate(spread, axis=1), jnp.concatenate(hots, axis=1), NT)
        parts = [
            summed[h * 16:h * 16 + 3] + summed[h * 16 + 3:h * 16 + 6] + summed[h * 16 + 6:h * 16 + 9] for h in range(8)]
        return jnp.concatenate(parts, axis=1)

    bring(0)
    for i in range(4):
        loads[12 + i].wait()
    bring(1)
    for col in range(0, NYZ, 128):
        for row in range(0, NX, 8):
            collide(row, col)

    for k in range(5):
        edge_x[0, k:k + 1, :] = ext[X_PLUS[k], TOP + NX - 1:TOP + NX, :]
        edge_x[1, k:k + 1, :] = ext[X_MINUS[k], TOP:TOP + 1, :]
    group = iota((NX, 128), 1) >> 5
    for side, (dirs, start, base) in enumerate(((Y_PLUS, 896, 32), (Y_MINUS, 0, 0))):
        tiles = [ext[q, TOP:TOP + NX, start:start + 128] for q in dirs]
        moved = [pltpu.roll(t, (base + 32 * k) % 128, 1) if (base + 32 * k) % 128 else t for k, t in enumerate(tiles)]
        edge_y[side, 0] = jnp.where(group == 0, moved[0], jnp.where(group == 1, moved[1], jnp.where(group == 2, moved[2], moved[3])))
        edge_y[side, 1] = moved[4]
    edge_c[0, 0:1, :] = ext[7, TOP + NX - 1:TOP + NX, 896:1024]
    edge_c[1, 0:1, :] = ext[8, TOP:TOP + 1, 0:128]
    edge_c[2, 0:1, :] = ext[9, TOP + NX - 1:TOP + NX, 0:128]
    edge_c[3, 0:1, :] = ext[10, TOP:TOP + 1, 896:1024]
    pl.semaphore_wait(barrier, len(around))

    def send(index, source, target, dx, dy):
        copy = pltpu.make_async_remote_copy(
            src_ref=source, dst_ref=target, send_sem=send_sem.at[index], recv_sem=recv_sem.at[index],
            device_id=device(dx, dy), device_id_type=MESH)
        copy.start()
        return copy

    halo = [
        send(4, edge_c.at[0], halo_c.at[0], 1, 1),
        send(5, edge_c.at[1], halo_c.at[1], -1, -1),
        send(6, edge_c.at[2], halo_c.at[2], 1, -1),
        send(7, edge_c.at[3], halo_c.at[3], -1, 1),
        send(0, edge_x.at[0], halo_x.at[0], 1, 0),
        send(1, edge_x.at[1], halo_x.at[1], -1, 0),
        send(2, edge_y.at[0], halo_y.at[0], 0, 1),
        send(3, edge_y.at[1], halo_y.at[1], 0, -1),
    ]

    def fluid_at_grains():
        for part, value in enumerate(split2(velf[...])):
            velb[part * 96:part * 96 + 96, :] = value.astype(BF16)
        for i in range(2):
            cols = slice(i * 512, (i + 1) * 512)
            got = dot(velb[...], onehot[:, cols], NN)
            got = got[0:96] + got[96:192]
            here = iota((NX, 512), 0) == (cell_ref[:, cols] >> 10)
            for c in range(3):
                fluid[c:c + 1, cols] = jnp.sum(jnp.where(here, got[c * NX:(c + 1) * NX], 0.0), axis=0, keepdims=True)

    lane = iota((NX, 128), 1)

    def stream(group):
        for k, q in enumerate(group):
            cx, cy, cz = VELOCITY[q]
            shift = cy * 32 + cz
            rows = slice(TOP - cx, TOP - cx + NX)
            value = ext[q, rows, :]
            if shift:
                value = pltpu.roll(value, shift % NYZ, 1)
            if cy == 1:
                edge = pltpu.roll(halo_yp[0, Y_PLUS.index(q), rows, :], shift % 128, 1)
                value = jnp.concatenate([jnp.where(lane < 32, edge, value[:, 0:128]), value[:, 128:]], axis=1)
            if cy == -1:
                edge = pltpu.roll(halo_yp[1, Y_MINUS.index(q), rows, :], shift % 128, 1)
                value = jnp.concatenate([value[:, :896], jnp.where(lane >= 96, edge, value[:, 896:])], axis=1)
            if q:
                bit = 1 << (q if q < 10 else q - 10)
                solid = (flags[0 if q < 10 else 1] & bit) != 0
                value = jnp.where(solid, ext[OPPOSITE[q], TOP:TOP + NX, :], value)
            read_ref[q] = value
            high = value.astype(BF16)
            at = group[0] * 2 * NX + k * NX
            splits[at:at + NX, :] = high
            splits[at + len(group) * NX:at + (len(group) + 1) * NX, :] = (value - high.astype(F32)).astype(BF16)

    def extract(group, i, width=1):
        cols = slice(i * 256, (i + width) * 256)
        at, size = group[0] * 2 * NX, len(group) * NX
        got = dot(splits[at:at + 2 * size, :], source_hot[:, cols], NN)
        here = iota((NX, 256 * width), 0) == (src_packed[:, cols] >> 10)
        for k, q in enumerate(group):
            value = got[k * NX:(k + 1) * NX] + got[size + k * NX:size + (k + 1) * NX]
            value = jnp.sum(jnp.where(here, value, 0.0), axis=0, keepdims=True)
            for w in range(width):
                gathered[i + w, q:q + 1, :] = value[:, w * 256:(w + 1) * 256]

    def move_grains(summed):
        radius = rad_ref[...]
        vel = vel_ref[...]
        total = (drag_coef * radius) * (fluid[0:3, :] - vel) + summed
        mass = mass_coef * radius * radius * radius
        falling = jnp.where(iota((3, NYZ), 0) == 2, gravity_z, 0.0)
        moved_vel = vel + total / mass + falling
        state_ref[0:3, :] = pos_ref[...] + moved_vel
        state_ref[3:6, :] = moved_vel
        state_ref[6:7, :] = radius
        state_ref[7:8, :] = jnp.ones_like(radius)

    def leave():
        slots = jnp.concatenate([mig_ref[0:1, :], mig_ref[1:2, :]], axis=1)
        state = jnp.concatenate(split3(state_ref[...]), axis=0).astype(BF16)
        out = dot(state, one_hot(slots, NYZ), NN)
        leaving[...] = out[0:8] + out[8:16] + out[16:24]

    rows_out = []

    def send_region(i):
        rows_out.append(send(10 + i, gathered.at[i], received.at[i], DISTANCE[i], 0))

    contacts_in()
    pull_ref[...] = contacts_out()
    fluid_at_grains()
    loads[16].wait()
    for copy in halo:
        copy.wait()
    for k in range(5):
        ext[X_PLUS[k], TOP - 1:TOP, :] = halo_x[0, k:k + 1, :]
        ext[X_MINUS[k], TOP + NX:TOP + NX + 1, :] = halo_x[1, k:k + 1, :]
        for side, base in enumerate((96, 0)):
            back = (base - 32 * k) % 128
            tile = halo_y[side, k // 4]
            halo_yp[side, k, TOP:TOP + NX, :] = pltpu.roll(tile, back, 1) if back else tile
    halo_yp[0, 1, TOP - 1:TOP, :] = halo_c[0, 0:1, :]
    halo_yp[1, 1, TOP + NX:TOP + NX + 1, :] = halo_c[1, 0:1, :]
    halo_yp[1, 2, TOP - 1:TOP, :] = halo_c[2, 0:1, :]
    halo_yp[0, 2, TOP + NX:TOP + NX + 1, :] = halo_c[3, 0:1, :]
    stream(GROUPS[0])
    extract(GROUPS[0], 0, 2)
    send_region(0)
    send_region(1)
    extract(GROUPS[0], 2, 2)
    send_region(2)
    send_region(3)
    move_grains(pull_ref[...])
    leave()
    migrate = [send(8, leaving, joined.at[0], -1, 0), send(9, leaving, joined.at[1], 1, 0)]

    for i in range(4):
        cols = slice(i * 256, (i + 1) * 256)
        rows_out[i].wait()
        stays = iota((24, 256), 1).astype(F32) >= counts[i]
        carried = jnp.where(stays, gathered[i], received[i])
        here = one_hot(tgt_packed[:, cols] >> 10, NX)
        for q in range(19):
            for part, value in enumerate(split2(carried[q:q + 1, :])):
                spread_ref[(part * 19 + q) * NX:(part * 19 + q + 1) * NX, cols] = here * value.astype(BF16)
        spread_ref[38 * NX:39 * NX, cols] = here

    for copy in migrate:
        copy.wait()
    mig_lane = iota((8, 128), 1)
    change = jnp.where(iota((8, 128), 0) == 0, jnp.where(mig_lane < 64, float(NX), -float(NX)), 0.0)
    newcomers = jnp.where(mig_lane < 64, joined[0], joined[1]) + change
    slots = jnp.concatenate([mig_ref[0:1, :], mig_ref[1:2, :]], axis=1)
    placed = dot(jnp.concatenate(split3(newcomers), axis=0).astype(BF16), one_hot(slots, NYZ), NT)
    placed = placed[0:8] + placed[8:16] + placed[16:24]
    result_ref[...] = jnp.where(placed[7:8] > 0.5, placed, state_ref[...])


def finish_kernel(
    read_ref, spread_ref, tgtp_ref, result_ref, spring_ref,
    next_hbm, pos_hbm, vel_hbm, rad_hbm, spring_hbm,
    blended, pos, vel, rad, sem,
):
    pos[...] = result_ref[0:3, :]
    vel[...] = result_ref[3:6, :]
    rad[...] = result_ref[6:7, :]
    copies = []
    for source, target in ((spring_ref, spring_hbm), (pos, pos_hbm), (vel, vel_hbm), (rad, rad_hbm)):
        copies.append(pltpu.make_async_copy(source, target, sem.at[len(copies)]))
        copies[-1].start()

    row = tgtp_ref[...] & 1023
    for i in range(2):
        cols = slice(i * 512, (i + 1) * 512)
        got = dot(spread_ref[...], one_hot(row, 512, i * 512), NT)
        hit = got[38 * NX:39 * NX] > 0.5
        for start, stop in ((0, 10), (10, 19)):
            for q in range(start, stop):
                value = read_ref[q, :, cols]
                carried = got[q * NX:(q + 1) * NX] + got[(19 + q) * NX:(20 + q) * NX]
                blended[q, :, cols] = jnp.where(hit, blend_coef * (value + carried), value)
            copies.append(pltpu.make_async_copy(
                blended.at[start:stop, :, cols], next_hbm.at[start:stop, :, cols], sem.at[len(copies)]))
            copies[-1].start()
    for copy in copies:
        copy.wait()


def shards(
    pdfs, link_flags, block_level, grain_pos, grain_vel, grain_radius, grain_cell, contact_pairs, contact_spring, iface_source,
    iface_offset, iface_slot, iface_target, migrant_slots,
):
    row = (1, NYZ)
    vmem = pl.BlockSpec(memory_space=pltpu.VMEM)
    hbm = pl.BlockSpec(memory_space=pl.ANY)
    outs = pl.pallas_call(
        step_kernel,
        name="step",
        out_shape=(
            pltpu.VMEM((19, NX, NYZ), F32),
            pltpu.VMEM((39 * NX, NYZ), BF16),
            pltpu.VMEM(row, jnp.int32),
            pltpu.VMEM((8, NYZ), F32),
            pltpu.VMEM((3, 3072), F32),
        ),
        in_specs=[hbm] * 14,
        out_specs=(vmem,) * 5,
        scratch_shapes=[
            pltpu.VMEM((19, NX, NYZ), F32),
            pltpu.VMEM((2, NX, NYZ), jnp.int32),
            pltpu.SMEM((1,), jnp.int32),
            pltpu.VMEM((3, NYZ), F32),
            pltpu.VMEM((3, NYZ), F32),
            pltpu.VMEM(row, F32),
            pltpu.VMEM(row, jnp.int32),
            pltpu.VMEM((2, 3072), jnp.int32),
            pltpu.VMEM((3, 3072), F32),
            pltpu.VMEM(row, jnp.int32),
            pltpu.VMEM(row, jnp.int32),
            pltpu.VMEM(row, jnp.int32),
            pltpu.VMEM((8, 128), jnp.int32),
            pltpu.VMEM((2, 64), jnp.int32),
            pltpu.VMEM((NYZ, NYZ), BF16),
            pltpu.VMEM((NYZ, NYZ), BF16),
            pltpu.VMEM((8 * NX, NYZ), BF16),
            pltpu.VMEM((19, EXT, NYZ), F32),
            pltpu.VMEM((3 * NX, NYZ), F32),
            pltpu.VMEM((6 * NX, NYZ), BF16),
            pltpu.VMEM((8, NYZ), F32),
            pltpu.VMEM((16, 3072), F32),
            pltpu.VMEM((2, 8, NYZ), F32),
            pltpu.VMEM((2, 2, NX, 128), F32),
            pltpu.VMEM((4, 8, 128), F32),
            pltpu.VMEM((2, 8, NYZ), F32),
            pltpu.VMEM((2, 2, NX, 128), F32),
            pltpu.VMEM((2, 5, EXT, 128), F32),
            pltpu.VMEM((4, 8, 128), F32),
            pltpu.VMEM((38 * NX, NYZ), BF16),
            pltpu.VMEM((4, 24, 256), F32),
            pltpu.VMEM((4, 24, 256), F32),
            pltpu.VMEM((8, 128), F32),
            pltpu.VMEM((2, 8, 128), F32),
            pltpu.VMEM((8, NYZ), F32),
            pltpu.VMEM((4 * NX, NYZ), F32),
            pltpu.VMEM((8, NYZ), F32),
            pltpu.VMEM((3, NYZ), F32),
            pltpu.SemaphoreType.DMA((17,)),
            pltpu.SemaphoreType.DMA((14,)),
            pltpu.SemaphoreType.DMA((14,)),
        ],
        compiler_params=pltpu.CompilerParams(collective_id=0, has_side_effects=True, vmem_limit_bytes=61_800_000),
    )(
        pdfs, link_flags, block_level.reshape(1), grain_pos, grain_vel, grain_radius.reshape(row), grain_cell.reshape(row), contact_pairs,
        contact_spring, iface_source.reshape(row), iface_offset.reshape(row), iface_slot.reshape(row),
        iface_target.reshape(8, 128), migrant_slots,
    )
    read, spread, tgtp, state, spring_next = outs
    result = pl.pallas_call(
        finish_kernel,
        name="finish",
        out_shape=(
            jax.ShapeDtypeStruct((19, NX, NYZ), F32),
            jax.ShapeDtypeStruct((3, NYZ), F32),
            jax.ShapeDtypeStruct((3, NYZ), F32),
            jax.ShapeDtypeStruct(row, F32),
            jax.ShapeDtypeStruct((3, 3072), F32),
        ),
        in_specs=[vmem] * 5,
        out_specs=(hbm,) * 5,
        scratch_shapes=[
            pltpu.VMEM((19, NX, NYZ), F32),
            pltpu.VMEM((3, NYZ), F32),
            pltpu.VMEM((3, NYZ), F32),
            pltpu.VMEM(row, F32),
            pltpu.SemaphoreType.DMA((12,)),
        ],
        compiler_params=pltpu.CompilerParams(vmem_limit_bytes=40 << 20),
    )(read, spread, tgtp, state, spring_next)
    pdfs_next, pos_next, vel_next, rad_next, spring_out = result
    return pdfs_next, pos_next, vel_next, rad_next.reshape(NYZ), spring_out


def solution(mesh):
    both = ("wide", "narrow")
    in_specs = (
        P(None, "wide", "narrow"), P(None, "wide", "narrow"), P("wide", "narrow"), P(None, both), P(None, both), P(both), P(both),
        P(None, both), P(None, both), P(both), P(), P(), P(both), P(None, both),
    )
    out_specs = (P(None, "wide", "narrow"), P(None, both), P(None, both), P(both), P(None, both))
    return jax.shard_map(shards, mesh=mesh, in_specs=in_specs, out_specs=out_specs, check_vma=False)
```

```python
import functools

import jax
import jax.numpy as jnp
from jax import lax
from jax.experimental import pallas as pl
from jax.experimental.pallas import tpu as pltpu
from jax.sharding import PartitionSpec as P

VELOCITY = (
    (0, 0, 0), (1, 0, 0), (-1, 0, 0), (0, 1, 0), (0, -1, 0), (0, 0, 1), (0, 0, -1),
    (1, 1, 0), (-1, -1, 0), (1, -1, 0), (-1, 1, 0), (1, 0, 1), (-1, 0, -1), (1, 0, -1),
    (-1, 0, 1), (0, 1, 1), (0, -1, -1), (0, 1, -1), (0, -1, 1),
)
OPPOSITE = (0, 2, 1, 4, 3, 6, 5, 8, 7, 10, 9, 12, 11, 14, 13, 16, 15, 18, 17)
tau_coarse = 1.0
tau_fine = 1.5
drag_coef = 0.5
mass_coef = 10.0
spring_coef = 0.2
dashpot_coef = 0.05
gravity_z = -0.01
blend_coef = 0.5

ROOT2 = 1.4142135623730951
THREE_BY_ROOT2 = 2.1213203435596424
GROUPS = (tuple(range(19)), ())
NX = 32
NYZ = 1024
TOP = 8
EXT = NX + 16
X_PLUS = (1, 7, 9, 11, 13)
X_MINUS = (2, 8, 10, 12, 14)
Y_PLUS = (3, 7, 10, 15, 17)
Y_MINUS = (4, 8, 9, 16, 18)
DISTANCE = (-2, 2, -1, 1)
MESH = pl.DeviceIdType.MESH
F32 = jnp.float32
BF16 = jnp.bfloat16
NT = (((1,), (1,)), ((), ()))
NN = (((1,), (0,)), ((), ()))


def iota(shape, axis):
    return lax.broadcasted_iota(jnp.int32, shape, axis)


def split2(value):
    high = value.astype(BF16).astype(F32)
    return high, value - high


def split3(value):
    high = value.astype(BF16).astype(F32)
    rest = value - high
    middle = rest.astype(BF16).astype(F32)
    return high, middle, rest - middle


def one_hot(row, size, start=0):
    lanes = row.shape[1]
    return jnp.where(iota((size, lanes), 0) + start == row, 1.0, 0.0).astype(BF16)


def fill_one_hot(ref, row):
    low = one_hot(row & 31, 32)
    high = one_hot(row >> 5, 32)
    for y in range(32):
        ref[y * 32:y * 32 + 32, :] = low * high[y:y + 1, :]


def dot(a, b, dims):
    return lax.dot_general(a, b, dims, preferred_element_type=F32)


def pack_interface(off_ref, slot_ref, src_ref, tgt_ref):
    off = off_ref[...]
    s8 = iota((8, NYZ), 0)
    dval = jnp.where(s8 == 0, DISTANCE[0], jnp.where(s8 == 1, DISTANCE[1], jnp.where(s8 == 2, DISTANCE[2], jnp.where(
        s8 == 3, DISTANCE[3], jnp.where(s8 == 4, 0, 99)))))
    member = jnp.where(off == dval, 1.0, 0.0)
    blocks = [member[:, b * 128:(b + 1) * 128] for b in range(8)]
    before = jnp.where(iota((128, 128), 0) < iota((128, 128), 1), 1.0, 0.0).astype(BF16)
    local = dot(jnp.concatenate(blocks, axis=0).astype(BF16), before, NN)
    running = jnp.zeros((8, 1), F32)
    ranks = []
    for b in range(8):
        ranks.append(local[b * 8:(b + 1) * 8] + running)
        running = running + jnp.sum(blocks[b], axis=1, keepdims=True)
    counts = [running[i:i + 1, :] for i in range(4)]
    ends = []
    total = jnp.zeros((1, 1), F32)
    for i in range(4):
        total = total + (256.0 - counts[i])
        ends.append(total)
    s128 = iota((8, 128), 0)
    base = (s128 * 256).astype(F32)
    positions = []
    for b in range(8):
        sent = jnp.sum(jnp.where(s128 < 4, blocks[b] * (base + ranks[b]), 0.0), axis=0, keepdims=True)
        z = ranks[b][4:5]
        stay = 768.0 + counts[3] + z - ends[2]
        for i in (2, 1, 0):
            start = ends[i - 1] if i else 0.0
            stay = jnp.where(z < ends[i], 256.0 * i + counts[i] + z - start, stay)
        positions.append(sent + blocks[b][4:5] * stay)
    pos = jnp.concatenate(positions, axis=1).astype(jnp.int32)
    src = src_ref[...]
    slot = slot_ref[...]
    values = jnp.where(s8 == 0, src >> 8, jnp.where(s8 == 1, src & 255, jnp.where(s8 == 2, slot >> 8, jnp.where(
        s8 == 3, slot & 255, 0)))).astype(F32)
    pos_high = pos >> 7
    stacked = jnp.concatenate([jnp.where(pos_high == h, values, 0.0) for h in range(8)], axis=0).astype(BF16)
    packed = dot(stacked, one_hot(pos & 127, 128), NT)
    src_packed = jnp.concatenate([packed[h * 8:h * 8 + 1] * 256.0 + packed[h * 8 + 1:h * 8 + 2] for h in range(8)], axis=1)
    slot_high = jnp.concatenate([packed[h * 8 + 2:h * 8 + 3] for h in range(8)], axis=1).astype(jnp.int32)
    slot_low = jnp.concatenate([packed[h * 8 + 3:h * 8 + 4] for h in range(8)], axis=1).astype(jnp.int32)
    slot_packed = slot_high * 256 + slot_low
    tgt = tgt_ref[...]
    table = jnp.concatenate([(tgt >> 8).astype(F32), (tgt & 255).astype(F32)], axis=0).astype(BF16)
    found = dot(table, one_hot(slot_packed & 127, 128), NN)
    chosen = s8 == (slot_packed >> 7)
    tgt_high = jnp.sum(jnp.where(chosen, found[0:8], 0.0), axis=0, keepdims=True)
    tgt_low = jnp.sum(jnp.where(chosen, found[8:16], 0.0), axis=0, keepdims=True)
    tgt_packed = (tgt_high * 256.0 + tgt_low).astype(jnp.int32)
    return src_packed.astype(jnp.int32), tgt_packed, counts


def step_kernel(
    pdfs_hbm, flags_hbm, level_hbm, pos_hbm, vel_hbm, rad_hbm, cell_hbm, pairs_hbm, spring_hbm, src_hbm, off_hbm, slot_hbm,
    tgt_hbm, mig_hbm,
    read_ref, spread_ref, tgtp_ref, result_ref, spring_out_ref,
    pdfs, flags, level, pos_ref, vel_ref, rad_ref, cell_ref, pairs_ref, spring_ref, src_ref, off_ref, slot_ref, tgt_ref,
    mig_ref,
    onehot, source_hot, moved_in, ext, velf, velb, vel8, rows16, edge_x, edge_y, edge_c, halo_x, halo_y, halo_yp, halo_c, splits,
    gathered, received, leaving, joined, fluid, force, state_ref, pull_ref,
    load_sem, send_sem, recv_sem,
):
    a, b = lax.axis_index("wide"), lax.axis_index("narrow")
    n_wide, n_narrow = lax.axis_size("wide"), lax.axis_size("narrow")

    def device(dx, dy):
        return (lax.rem(a + dx + n_wide, n_wide), lax.rem(b + dy + n_narrow, n_narrow))

    small = [
        (cell_hbm, cell_ref), (off_hbm, off_ref), (slot_hbm, slot_ref), (src_hbm, src_ref), (tgt_hbm, tgt_ref),
        (rad_hbm, rad_ref), (vel_hbm, vel_ref), (pairs_hbm, pairs_ref), (spring_hbm, spring_ref), (pos_hbm, pos_ref),
        (mig_hbm, mig_ref), (level_hbm, level),
    ]
    parts = [slice(i * 256, (i + 1) * 256) for i in range(4)]
    large = [(pdfs_hbm.at[:, :, part], pdfs.at[:, :, part]) for part in parts] + [(flags_hbm, flags)]
    loads = [pltpu.make_async_copy(x, y, load_sem.at[i]) for i, (x, y) in enumerate(small + large)]
    for load in loads:
        load.start()
    around = [(dx, dy) for dx in (-1, 0, 1) for dy in (-1, 0, 1) if dx or dy] + [(-2, 0), (2, 0)]
    barrier = pltpu.get_barrier_semaphore()
    for dx, dy in around:
        pl.semaphore_signal(barrier, inc=1, device_id=device(dx, dy), device_id_type=MESH)
    for load in loads[:12]:
        load.wait()

    src_packed, tgt_packed, counts = pack_interface(off_ref, slot_ref, src_ref, tgt_ref)
    tgtp_ref[...] = tgt_packed

    cell = cell_ref[...]
    grain_x = cell >> 10
    fill_one_hot(onehot, cell & 1023)
    drag = drag_coef * rad_ref[...]
    in_row = one_hot(grain_x, NX)
    weights = [drag] + [drag * vel_ref[c:c + 1, :] for c in range(3)]
    for k, weight in enumerate(weights):
        for part, value in enumerate(split2(weight)):
            moved_in[(part * 4 + k) * NX:(part * 4 + k + 1) * NX, :] = in_row * value.astype(BF16)
    fill_one_hot(source_hot, src_packed & 1023)

    fine = level[0] == 1
    tau = jnp.where(fine, tau_fine, tau_coarse).astype(F32)
    omega = jnp.where(fine, 1.0 / tau_fine, 1.0 / tau_coarse).astype(F32)
    keep = jnp.where(fine, 1.0 - 1.0 / tau_fine, 0.0).astype(F32)

    def bring(i):
        cols = slice(i * 512, (i + 1) * 512)
        got = dot(moved_in[...], onehot[cols, :], NT)
        force[:, cols] = got[0:128] + got[128:256]

    def collide(row, col):
        rows = slice(row, row + 8)
        cols = slice(col, col + 128)
        p = [pdfs[q, rows, cols] for q in range(19)]
        pair_sum = {q: p[q] + p[q + 1] for q in range(1, 19, 2)}
        pair_dif = {q: p[q] - p[q + 1] for q in range(1, 19, 2)}
        density = p[0] + ((pair_sum[1] + pair_sum[3]) + (pair_sum[5] + pair_sum[7])) + (
            (pair_sum[9] + pair_sum[11]) + (pair_sum[13] + pair_sum[15]) + pair_sum[17])
        mom = (
            (pair_dif[1] + pair_dif[7]) + (pair_dif[9] + pair_dif[11]) + pair_dif[13],
            (pair_dif[3] + pair_dif[7]) + (pair_dif[15] - pair_dif[9]) + pair_dif[17],
            (pair_dif[5] + pair_dif[11]) + (pair_dif[15] - pair_dif[13]) - pair_dif[17],
        )
        inverse = 1.0 / density
        pull = tau * inverse
        resist = force[rows, cols]
        shifted = []
        for c in range(3):
            v = mom[c] * inverse
            velf[c * NX + row:c * NX + row + 8, cols] = v
            shifted.append(THREE_BY_ROOT2 * (v + pull * (force[(c + 1) * NX + row:(c + 1) * NX + row + 8, cols] - v * resist)))
        base = 1.0 - (shifted[0] * shifted[0] + shifted[1] * shifted[1] + shifted[2] * shifted[2]) * (1.0 / 3.0)
        dense = omega * density
        slim = dense * (1.0 / 36.0)
        wide = slim + slim
        slim_base = slim * base
        wide_base = slim_base + slim_base
        out_rows = slice(TOP + row, TOP + row + 8)
        ext[0, out_rows, cols] = keep * p[0] + 6.0 * wide_base
        for q in range(1, 19, 2):
            along = None
            for c in range(3):
                if VELOCITY[q][c] == 1:
                    along = shifted[c] if along is None else along + shifted[c]
                elif VELOCITY[q][c] == -1:
                    along = along - shifted[c]
            scaled = (wide if q < 7 else slim) * along
            even = (wide_base if q < 7 else slim_base) + scaled * along
            odd = ROOT2 * scaled
            ext[q, out_rows, cols] = keep * p[q] + (even + odd)
            ext[q + 1, out_rows, cols] = keep * p[q + 1] + (even - odd)

    def contacts_in():
        vel8[...] = jnp.zeros_like(vel8)
        vel8[0:3, :] = vel_ref[...]
        vel8[4:7, :] = vel_ref[...]
        tables = [vel8[:, h * 128:(h + 1) * 128] for h in range(8)]
        half = iota((8, 128), 0) < 4
        for c in range(24):
            cols = slice(c * 128, (c + 1) * 128)
            index = jnp.where(half, pairs_ref[0:1, cols], pairs_ref[1:2, cols])
            low = index & 127
            high = index >> 7
            found = jnp.take_along_axis(tables[0], low, axis=1, mode="promise_in_bounds")
            for h in range(1, 8):
                found = jnp.where(high == h, jnp.take_along_axis(tables[h], low, axis=1, mode="promise_in_bounds"), found)
            relative = found[4:7] - found[0:3]
            spring = spring_ref[:, cols]
            spring_out_ref[:, cols] = spring + relative
            contact = spring_coef * spring + dashpot_coef * relative
            for part, value in enumerate(split3(contact)):
                rows16[part * 3:part * 3 + 3, cols] = value

    def contacts_out():
        rows16[9:16, :] = jnp.zeros((7, 3072), F32)
        forces = rows16[...]
        spread = []
        hots = []
        for side in range(2):
            index = pairs_ref[side:side + 1, :]
            high = index >> 7
            signed = -forces if side else forces
            spread.append(jnp.concatenate([jnp.where(high == h, signed, 0.0).astype(BF16) for h in range(8)], axis=0))
            hots.append(one_hot(index & 127, 128))
        summed = dot(jnp.concatenate(spread, axis=1), jnp.concatenate(hots, axis=1), NT)
        parts = [
            summed[h * 16:h * 16 + 3] + summed[h * 16 + 3:h * 16 + 6] + summed[h * 16 + 6:h * 16 + 9] for h in range(8)]
        return jnp.concatenate(parts, axis=1)

    bring(0)
    for half in range(2):
        loads[12 + 2 * half].wait()
        loads[13 + 2 * half].wait()
        if half == 0:
            bring(1)
        for col in range(half * 512, half * 512 + 512, 128):
            for row in range(0, NX, 8):
                collide(row, col)

    for k in range(5):
        edge_x[0, k:k + 1, :] = ext[X_PLUS[k], TOP + NX - 1:TOP + NX, :]
        edge_x[1, k:k + 1, :] = ext[X_MINUS[k], TOP:TOP + 1, :]
    group = iota((NX, 128), 1) >> 5
    for side, (dirs, start, base) in enumerate(((Y_PLUS, 896, 32), (Y_MINUS, 0, 0))):
        tiles = [ext[q, TOP:TOP + NX, start:start + 128] for q in dirs]
        moved = [pltpu.roll(t, (base + 32 * k) % 128, 1) if (base + 32 * k) % 128 else t for k, t in enumerate(tiles)]
        edge_y[side, 0] = jnp.where(group == 0, moved[0], jnp.where(group == 1, moved[1], jnp.where(group == 2, moved[2], moved[3])))
        edge_y[side, 1] = moved[4]
    edge_c[0, 0:1, :] = ext[7, TOP + NX - 1:TOP + NX, 896:1024]
    edge_c[1, 0:1, :] = ext[8, TOP:TOP + 1, 0:128]
    edge_c[2, 0:1, :] = ext[9, TOP + NX - 1:TOP + NX, 0:128]
    edge_c[3, 0:1, :] = ext[10, TOP:TOP + 1, 896:1024]
    pl.semaphore_wait(barrier, len(around))

    def send(index, source, target, dx, dy):
        copy = pltpu.make_async_remote_copy(
            src_ref=source, dst_ref=target, send_sem=send_sem.at[index], recv_sem=recv_sem.at[index],
            device_id=device(dx, dy), device_id_type=MESH)
        copy.start()
        return copy

    halo = [
        send(4, edge_c.at[0], halo_c.at[0], 1, 1),
        send(5, edge_c.at[1], halo_c.at[1], -1, -1),
        send(6, edge_c.at[2], halo_c.at[2], 1, -1),
        send(7, edge_c.at[3], halo_c.at[3], -1, 1),
        send(0, edge_x.at[0], halo_x.at[0], 1, 0),
        send(1, edge_x.at[1], halo_x.at[1], -1, 0),
        send(2, edge_y.at[0], halo_y.at[0], 0, 1),
        send(3, edge_y.at[1], halo_y.at[1], 0, -1),
    ]

    def fluid_at_grains():
        for part, value in enumerate(split2(velf[...])):
            velb[part * 96:part * 96 + 96, :] = value.astype(BF16)
        for i in range(2):
            cols = slice(i * 512, (i + 1) * 512)
            got = dot(velb[...], onehot[:, cols], NN)
            got = got[0:96] + got[96:192]
            here = iota((NX, 512), 0) == (cell_ref[:, cols] >> 10)
            for c in range(3):
                fluid[c:c + 1, cols] = jnp.sum(jnp.where(here, got[c * NX:(c + 1) * NX], 0.0), axis=0, keepdims=True)

    lane = iota((NX, 128), 1)

    def stream(group):
        for k, q in enumerate(group):
            cx, cy, cz = VELOCITY[q]
            shift = cy * 32 + cz
            rows = slice(TOP - cx, TOP - cx + NX)
            value = ext[q, rows, :]
            if shift:
                value = pltpu.roll(value, shift % NYZ, 1)
            if cy == 1:
                edge = pltpu.roll(halo_yp[0, Y_PLUS.index(q), rows, :], shift % 128, 1)
                value = jnp.concatenate([jnp.where(lane < 32, edge, value[:, 0:128]), value[:, 128:]], axis=1)
            if cy == -1:
                edge = pltpu.roll(halo_yp[1, Y_MINUS.index(q), rows, :], shift % 128, 1)
                value = jnp.concatenate([value[:, :896], jnp.where(lane >= 96, edge, value[:, 896:])], axis=1)
            if q:
                bit = 1 << (q if q < 10 else q - 10)
                solid = (flags[0 if q < 10 else 1] & bit) != 0
                value = jnp.where(solid, ext[OPPOSITE[q], TOP:TOP + NX, :], value)
            read_ref[q] = value
            high = value.astype(BF16)
            at = group[0] * 2 * NX + k * NX
            splits[at:at + NX, :] = high
            splits[at + len(group) * NX:at + (len(group) + 1) * NX, :] = (value - high.astype(F32)).astype(BF16)

    def extract(group, i, width=1):
        cols = slice(i * 256, (i + width) * 256)
        at, size = group[0] * 2 * NX, len(group) * NX
        got = dot(splits[at:at + 2 * size, :], source_hot[:, cols], NN)
        here = iota((NX, 256 * width), 0) == (src_packed[:, cols] >> 10)
        for k, q in enumerate(group):
            value = got[k * NX:(k + 1) * NX] + got[size + k * NX:size + (k + 1) * NX]
            value = jnp.sum(jnp.where(here, value, 0.0), axis=0, keepdims=True)
            for w in range(width):
                gathered[i + w, q:q + 1, :] = value[:, w * 256:(w + 1) * 256]

    def move_grains(summed):
        radius = rad_ref[...]
        vel = vel_ref[...]
        total = (drag_coef * radius) * (fluid[0:3, :] - vel) + summed
        mass = mass_coef * radius * radius * radius
        falling = jnp.where(iota((3, NYZ), 0) == 2, gravity_z, 0.0)
        moved_vel = vel + total / mass + falling
        state_ref[0:3, :] = pos_ref[...] + moved_vel
        state_ref[3:6, :] = moved_vel
        state_ref[6:7, :] = radius
        state_ref[7:8, :] = jnp.ones_like(radius)

    def leave():
        slots = jnp.concatenate([mig_ref[0:1, :], mig_ref[1:2, :]], axis=1)
        state = jnp.concatenate(split3(state_ref[...]), axis=0).astype(BF16)
        out = dot(state, one_hot(slots, NYZ), NN)
        leaving[...] = out[0:8] + out[8:16] + out[16:24]

    rows_out = []

    def send_region(i):
        rows_out.append(send(10 + i, gathered.at[i], received.at[i], DISTANCE[i], 0))

    contacts_in()
    pull_ref[...] = contacts_out()
    fluid_at_grains()
    loads[16].wait()
    for copy in halo:
        copy.wait()
    for k in range(5):
        ext[X_PLUS[k], TOP - 1:TOP, :] = halo_x[0, k:k + 1, :]
        ext[X_MINUS[k], TOP + NX:TOP + NX + 1, :] = halo_x[1, k:k + 1, :]
        for side, base in enumerate((96, 0)):
            back = (base - 32 * k) % 128
            tile = halo_y[side, k // 4]
            halo_yp[side, k, TOP:TOP + NX, :] = pltpu.roll(tile, back, 1) if back else tile
    halo_yp[0, 1, TOP - 1:TOP, :] = halo_c[0, 0:1, :]
    halo_yp[1, 1, TOP + NX:TOP + NX + 1, :] = halo_c[1, 0:1, :]
    halo_yp[1, 2, TOP - 1:TOP, :] = halo_c[2, 0:1, :]
    halo_yp[0, 2, TOP + NX:TOP + NX + 1, :] = halo_c[3, 0:1, :]
    stream(GROUPS[0])
    extract(GROUPS[0], 0, 2)
    send_region(0)
    send_region(1)

    @pl.when(a >= 0)
    def _():
        extract(GROUPS[0], 2, 2)

    send_region(2)
    send_region(3)
    move_grains(pull_ref[...])
    leave()
    migrate = [send(8, leaving, joined.at[0], -1, 0), send(9, leaving, joined.at[1], 1, 0)]

    for i in range(4):
        cols = slice(i * 256, (i + 1) * 256)
        rows_out[i].wait()
        stays = iota((24, 256), 1).astype(F32) >= counts[i]
        carried = jnp.where(stays, gathered[i], received[i])
        here = one_hot(tgt_packed[:, cols] >> 10, NX)
        for q in range(19):
            for part, value in enumerate(split2(carried[q:q + 1, :])):
                spread_ref[(part * 19 + q) * NX:(part * 19 + q + 1) * NX, cols] = here * value.astype(BF16)
        spread_ref[38 * NX:39 * NX, cols] = here

    for copy in migrate:
        copy.wait()
    mig_lane = iota((8, 128), 1)
    change = jnp.where(iota((8, 128), 0) == 0, jnp.where(mig_lane < 64, float(NX), -float(NX)), 0.0)
    newcomers = jnp.where(mig_lane < 64, joined[0], joined[1]) + change
    slots = jnp.concatenate([mig_ref[0:1, :], mig_ref[1:2, :]], axis=1)
    placed = dot(jnp.concatenate(split3(newcomers), axis=0).astype(BF16), one_hot(slots, NYZ), NT)
    placed = placed[0:8] + placed[8:16] + placed[16:24]
    result_ref[...] = jnp.where(placed[7:8] > 0.5, placed, state_ref[...])


def finish_kernel(
    read_ref, spread_ref, tgtp_ref, result_ref, spring_ref,
    next_hbm, pos_hbm, vel_hbm, rad_hbm, spring_hbm,
    blended, pos, vel, rad, sem,
):
    pos[...] = result_ref[0:3, :]
    vel[...] = result_ref[3:6, :]
    rad[...] = result_ref[6:7, :]
    copies = []
    for source, target in ((spring_ref, spring_hbm), (pos, pos_hbm), (vel, vel_hbm), (rad, rad_hbm)):
        copies.append(pltpu.make_async_copy(source, target, sem.at[len(copies)]))
        copies[-1].start()

    row = tgtp_ref[...] & 1023
    for i in range(2):
        cols = slice(i * 512, (i + 1) * 512)
        got = dot(spread_ref[...], one_hot(row, 512, i * 512), NT)
        hit = got[38 * NX:39 * NX] > 0.5
        for start, stop in ((0, 10), (10, 19)):
            for q in range(start, stop):
                value = read_ref[q, :, cols]
                carried = got[q * NX:(q + 1) * NX] + got[(19 + q) * NX:(20 + q) * NX]
                blended[q, :, cols] = jnp.where(hit, blend_coef * (value + carried), value)
            copies.append(pltpu.make_async_copy(
                blended.at[start:stop, :, cols], next_hbm.at[start:stop, :, cols], sem.at[len(copies)]))
            copies[-1].start()
    for copy in copies:
        copy.wait()


def shards(
    pdfs, link_flags, block_level, grain_pos, grain_vel, grain_radius, grain_cell, contact_pairs, contact_spring, iface_source,
    iface_offset, iface_slot, iface_target, migrant_slots,
):
    row = (1, NYZ)
    vmem = pl.BlockSpec(memory_space=pltpu.VMEM)
    hbm = pl.BlockSpec(memory_space=pl.ANY)
    outs = pl.pallas_call(
        step_kernel,
        name="step",
        out_shape=(
            pltpu.VMEM((19, NX, NYZ), F32),
            pltpu.VMEM((39 * NX, NYZ), BF16),
            pltpu.VMEM(row, jnp.int32),
            pltpu.VMEM((8, NYZ), F32),
            pltpu.VMEM((3, 3072), F32),
        ),
        in_specs=[hbm] * 14,
        out_specs=(vmem,) * 5,
        scratch_shapes=[
            pltpu.VMEM((19, NX, NYZ), F32),
            pltpu.VMEM((2, NX, NYZ), jnp.int32),
            pltpu.SMEM((1,), jnp.int32),
            pltpu.VMEM((3, NYZ), F32),
            pltpu.VMEM((3, NYZ), F32),
            pltpu.VMEM(row, F32),
            pltpu.VMEM(row, jnp.int32),
            pltpu.VMEM((2, 3072), jnp.int32),
            pltpu.VMEM((3, 3072), F32),
            pltpu.VMEM(row, jnp.int32),
            pltpu.VMEM(row, jnp.int32),
            pltpu.VMEM(row, jnp.int32),
            pltpu.VMEM((8, 128), jnp.int32),
            pltpu.VMEM((2, 64), jnp.int32),
            pltpu.VMEM((NYZ, NYZ), BF16),
            pltpu.VMEM((NYZ, NYZ), BF16),
            pltpu.VMEM((8 * NX, NYZ), BF16),
            pltpu.VMEM((19, EXT, NYZ), F32),
            pltpu.VMEM((3 * NX, NYZ), F32),
            pltpu.VMEM((6 * NX, NYZ), BF16),
            pltpu.VMEM((8, NYZ), F32),
            pltpu.VMEM((16, 3072), F32),
            pltpu.VMEM((2, 8, NYZ), F32),
            pltpu.VMEM((2, 2, NX, 128), F32),
            pltpu.VMEM((4, 8, 128), F32),
            pltpu.VMEM((2, 8, NYZ), F32),
            pltpu.VMEM((2, 2, NX, 128), F32),
            pltpu.VMEM((2, 5, EXT, 128), F32),
            pltpu.VMEM((4, 8, 128), F32),
            pltpu.VMEM((38 * NX, NYZ), BF16),
            pltpu.VMEM((4, 24, 256), F32),
            pltpu.VMEM((4, 24, 256), F32),
            pltpu.VMEM((8, 128), F32),
            pltpu.VMEM((2, 8, 128), F32),
            pltpu.VMEM((8, NYZ), F32),
            pltpu.VMEM((4 * NX, NYZ), F32),
            pltpu.VMEM((8, NYZ), F32),
            pltpu.VMEM((3, NYZ), F32),
            pltpu.SemaphoreType.DMA((17,)),
            pltpu.SemaphoreType.DMA((14,)),
            pltpu.SemaphoreType.DMA((14,)),
        ],
        compiler_params=pltpu.CompilerParams(collective_id=0, has_side_effects=True, vmem_limit_bytes=61_800_000),
    )(
        pdfs, link_flags, block_level.reshape(1), grain_pos, grain_vel, grain_radius.reshape(row), grain_cell.reshape(row), contact_pairs,
        contact_spring, iface_source.reshape(row), iface_offset.reshape(row), iface_slot.reshape(row),
        iface_target.reshape(8, 128), migrant_slots,
    )
    read, spread, tgtp, state, spring_next = outs
    result = pl.pallas_call(
        finish_kernel,
        name="finish",
        out_shape=(
            jax.ShapeDtypeStruct((19, NX, NYZ), F32),
            jax.ShapeDtypeStruct((3, NYZ), F32),
            jax.ShapeDtypeStruct((3, NYZ), F32),
            jax.ShapeDtypeStruct(row, F32),
            jax.ShapeDtypeStruct((3, 3072), F32),
        ),
        in_specs=[vmem] * 5,
        out_specs=(hbm,) * 5,
        scratch_shapes=[
            pltpu.VMEM((19, NX, NYZ), F32),
            pltpu.VMEM((3, NYZ), F32),
            pltpu.VMEM((3, NYZ), F32),
            pltpu.VMEM(row, F32),
            pltpu.SemaphoreType.DMA((12,)),
        ],
        compiler_params=pltpu.CompilerParams(vmem_limit_bytes=40 << 20),
    )(read, spread, tgtp, state, spring_next)
    pdfs_next, pos_next, vel_next, rad_next, spring_out = result
    return pdfs_next, pos_next, vel_next, rad_next.reshape(NYZ), spring_out


def solution(mesh):
    both = ("wide", "narrow")
    in_specs = (
        P(None, "wide", "narrow"), P(None, "wide", "narrow"), P("wide", "narrow"), P(None, both), P(None, both), P(both), P(both),
        P(None, both), P(None, both), P(both), P(), P(), P(both), P(None, both),
    )
    out_specs = (P(None, "wide", "narrow"), P(None, both), P(None, both), P(both), P(None, both))
    return jax.shard_map(shards, mesh=mesh, in_specs=in_specs, out_specs=out_specs, check_vma=False)
```

```python
import functools

import jax
import jax.numpy as jnp
from jax import lax
from jax.experimental import pallas as pl
from jax.experimental.pallas import tpu as pltpu
from jax.sharding import PartitionSpec as P

VELOCITY = (
    (0, 0, 0), (1, 0, 0), (-1, 0, 0), (0, 1, 0), (0, -1, 0), (0, 0, 1), (0, 0, -1),
    (1, 1, 0), (-1, -1, 0), (1, -1, 0), (-1, 1, 0), (1, 0, 1), (-1, 0, -1), (1, 0, -1),
    (-1, 0, 1), (0, 1, 1), (0, -1, -1), (0, 1, -1), (0, -1, 1),
)
OPPOSITE = (0, 2, 1, 4, 3, 6, 5, 8, 7, 10, 9, 12, 11, 14, 13, 16, 15, 18, 17)
tau_coarse = 1.0
tau_fine = 1.5
drag_coef = 0.5
mass_coef = 10.0
spring_coef = 0.2
dashpot_coef = 0.05
gravity_z = -0.01
blend_coef = 0.5

ROOT2 = 1.4142135623730951
THREE_BY_ROOT2 = 2.1213203435596424
GROUPS = (tuple(range(19)), ())
NX = 32
NYZ = 1024
TOP = 8
EXT = NX + 16
X_PLUS = (1, 7, 9, 11, 13)
X_MINUS = (2, 8, 10, 12, 14)
Y_PLUS = (3, 7, 10, 15, 17)
Y_MINUS = (4, 8, 9, 16, 18)
DISTANCE = (-2, 2, -1, 1)
MESH = pl.DeviceIdType.MESH
F32 = jnp.float32
BF16 = jnp.bfloat16
NT = (((1,), (1,)), ((), ()))
NN = (((1,), (0,)), ((), ()))


def iota(shape, axis):
    return lax.broadcasted_iota(jnp.int32, shape, axis)


def split2(value):
    high = value.astype(BF16).astype(F32)
    return high, value - high


def split3(value):
    high = value.astype(BF16).astype(F32)
    rest = value - high
    middle = rest.astype(BF16).astype(F32)
    return high, middle, rest - middle


def one_hot(row, size, start=0):
    lanes = row.shape[1]
    return jnp.where(iota((size, lanes), 0) + start == row, 1.0, 0.0).astype(BF16)


def fill_one_hot(ref, row):
    low = one_hot(row & 31, 32)
    high = one_hot(row >> 5, 32)
    for y in range(32):
        ref[y * 32:y * 32 + 32, :] = low * high[y:y + 1, :]


def dot(a, b, dims):
    return lax.dot_general(a, b, dims, preferred_element_type=F32)


def pack_interface(off_ref, slot_ref, src_ref, tgt_ref):
    off = off_ref[...]
    s8 = iota((8, NYZ), 0)
    dval = jnp.where(s8 == 0, DISTANCE[0], jnp.where(s8 == 1, DISTANCE[1], jnp.where(s8 == 2, DISTANCE[2], jnp.where(
        s8 == 3, DISTANCE[3], jnp.where(s8 == 4, 0, 99)))))
    member = jnp.where(off == dval, 1.0, 0.0)
    blocks = [member[:, b * 128:(b + 1) * 128] for b in range(8)]
    before = jnp.where(iota((128, 128), 0) < iota((128, 128), 1), 1.0, 0.0).astype(BF16)
    local = dot(jnp.concatenate(blocks, axis=0).astype(BF16), before, NN)
    running = jnp.zeros((8, 1), F32)
    ranks = []
    for b in range(8):
        ranks.append(local[b * 8:(b + 1) * 8] + running)
        running = running + jnp.sum(blocks[b], axis=1, keepdims=True)
    counts = [running[i:i + 1, :] for i in range(4)]
    ends = []
    total = jnp.zeros((1, 1), F32)
    for i in range(4):
        total = total + (256.0 - counts[i])
        ends.append(total)
    s128 = iota((8, 128), 0)
    base = (s128 * 256).astype(F32)
    positions = []
    for b in range(8):
        sent = jnp.sum(jnp.where(s128 < 4, blocks[b] * (base + ranks[b]), 0.0), axis=0, keepdims=True)
        z = ranks[b][4:5]
        stay = 768.0 + counts[3] + z - ends[2]
        for i in (2, 1, 0):
            start = ends[i - 1] if i else 0.0
            stay = jnp.where(z < ends[i], 256.0 * i + counts[i] + z - start, stay)
        positions.append(sent + blocks[b][4:5] * stay)
    pos = jnp.concatenate(positions, axis=1).astype(jnp.int32)
    src = src_ref[...]
    slot = slot_ref[...]
    values = jnp.where(s8 == 0, src >> 8, jnp.where(s8 == 1, src & 255, jnp.where(s8 == 2, slot >> 8, jnp.where(
        s8 == 3, slot & 255, 0)))).astype(F32)
    pos_high = pos >> 7
    stacked = jnp.concatenate([jnp.where(pos_high == h, values, 0.0) for h in range(8)], axis=0).astype(BF16)
    packed = dot(stacked, one_hot(pos & 127, 128), NT)
    src_packed = jnp.concatenate([packed[h * 8:h * 8 + 1] * 256.0 + packed[h * 8 + 1:h * 8 + 2] for h in range(8)], axis=1)
    slot_high = jnp.concatenate([packed[h * 8 + 2:h * 8 + 3] for h in range(8)], axis=1).astype(jnp.int32)
    slot_low = jnp.concatenate([packed[h * 8 + 3:h * 8 + 4] for h in range(8)], axis=1).astype(jnp.int32)
    slot_packed = slot_high * 256 + slot_low
    tgt = tgt_ref[...]
    table = jnp.concatenate([(tgt >> 8).astype(F32), (tgt & 255).astype(F32)], axis=0).astype(BF16)
    found = dot(table, one_hot(slot_packed & 127, 128), NN)
    chosen = s8 == (slot_packed >> 7)
    tgt_high = jnp.sum(jnp.where(chosen, found[0:8], 0.0), axis=0, keepdims=True)
    tgt_low = jnp.sum(jnp.where(chosen, found[8:16], 0.0), axis=0, keepdims=True)
    tgt_packed = (tgt_high * 256.0 + tgt_low).astype(jnp.int32)
    return src_packed.astype(jnp.int32), tgt_packed, counts


def step_kernel(
    pdfs_hbm, flags_hbm, level_hbm, pos_hbm, vel_hbm, rad_hbm, cell_hbm, pairs_hbm, spring_hbm, src_hbm, off_hbm, slot_hbm,
    tgt_hbm, mig_hbm,
    read_ref, spread_ref, tgtp_ref, result_ref, spring_out_ref,
    pdfs, flags, level, pos_ref, vel_ref, rad_ref, cell_ref, pairs_ref, spring_ref, src_ref, off_ref, slot_ref, tgt_ref,
    mig_ref,
    onehot, source_hot, moved_in, ext, velf, velb, vel8, rows16, edge_x, edge_y, edge_c, halo_x, halo_y, halo_yp, halo_c, splits,
    gathered, received, leaving, joined, fluid, force, state_ref, pull_ref,
    load_sem, send_sem, recv_sem,
):
    a, b = lax.axis_index("wide"), lax.axis_index("narrow")
    n_wide, n_narrow = lax.axis_size("wide"), lax.axis_size("narrow")

    def device(dx, dy):
        return (lax.rem(a + dx + n_wide, n_wide), lax.rem(b + dy + n_narrow, n_narrow))

    small = [
        (cell_hbm, cell_ref), (off_hbm, off_ref), (slot_hbm, slot_ref), (src_hbm, src_ref), (tgt_hbm, tgt_ref),
        (rad_hbm, rad_ref), (vel_hbm, vel_ref), (pairs_hbm, pairs_ref), (spring_hbm, spring_ref), (pos_hbm, pos_ref),
        (mig_hbm, mig_ref), (level_hbm, level),
    ]
    parts = [slice(i * 256, (i + 1) * 256) for i in range(4)]
    large = [(pdfs_hbm.at[:, :, part], pdfs.at[:, :, part]) for part in parts] + [(flags_hbm, flags)]
    loads = [pltpu.make_async_copy(x, y, load_sem.at[i]) for i, (x, y) in enumerate(small + large)]
    for load in loads:
        load.start()
    around = [(dx, dy) for dx in (-1, 0, 1) for dy in (-1, 0, 1) if dx or dy] + [(-2, 0), (2, 0)]
    barrier = pltpu.get_barrier_semaphore()
    for dx, dy in around:
        pl.semaphore_signal(barrier, inc=1, device_id=device(dx, dy), device_id_type=MESH)
    for load in loads[:12]:
        load.wait()

    src_packed, tgt_packed, counts = pack_interface(off_ref, slot_ref, src_ref, tgt_ref)
    tgtp_ref[...] = tgt_packed

    cell = cell_ref[...]
    grain_x = cell >> 10
    fill_one_hot(onehot, cell & 1023)
    drag = drag_coef * rad_ref[...]
    in_row = one_hot(grain_x, NX)
    weights = [drag] + [drag * vel_ref[c:c + 1, :] for c in range(3)]
    for k, weight in enumerate(weights):
        for part, value in enumerate(split2(weight)):
            moved_in[(part * 4 + k) * NX:(part * 4 + k + 1) * NX, :] = in_row * value.astype(BF16)
    fill_one_hot(source_hot, src_packed & 1023)

    fine = level[0] == 1
    tau = jnp.where(fine, tau_fine, tau_coarse).astype(F32)
    omega = jnp.where(fine, 1.0 / tau_fine, 1.0 / tau_coarse).astype(F32)
    keep = jnp.where(fine, 1.0 - 1.0 / tau_fine, 0.0).astype(F32)

    def bring(i):
        cols = slice(i * 512, (i + 1) * 512)
        got = dot(moved_in[...], onehot[cols, :], NT)
        force[:, cols] = got[0:128] + got[128:256]

    def collide(row, col):
        rows = slice(row, row + 8)
        cols = slice(col, col + 128)
        p = [pdfs[q, rows, cols] for q in range(19)]
        pair_sum = {q: p[q] + p[q + 1] for q in range(1, 19, 2)}
        pair_dif = {q: p[q] - p[q + 1] for q in range(1, 19, 2)}
        density = p[0] + ((pair_sum[1] + pair_sum[3]) + (pair_sum[5] + pair_sum[7])) + (
            (pair_sum[9] + pair_sum[11]) + (pair_sum[13] + pair_sum[15]) + pair_sum[17])
        mom = (
            (pair_dif[1] + pair_dif[7]) + (pair_dif[9] + pair_dif[11]) + pair_dif[13],
            (pair_dif[3] + pair_dif[7]) + (pair_dif[15] - pair_dif[9]) + pair_dif[17],
            (pair_dif[5] + pair_dif[11]) + (pair_dif[15] - pair_dif[13]) - pair_dif[17],
        )
        inverse = 1.0 / density
        pull = tau * inverse
        resist = force[rows, cols]
        shifted = []
        for c in range(3):
            v = mom[c] * inverse
            velf[c * NX + row:c * NX + row + 8, cols] = v
            shifted.append(THREE_BY_ROOT2 * (v + pull * (force[(c + 1) * NX + row:(c + 1) * NX + row + 8, cols] - v * resist)))
        base = 1.0 - (shifted[0] * shifted[0] + shifted[1] * shifted[1] + shifted[2] * shifted[2]) * (1.0 / 3.0)
        dense = omega * density
        slim = dense * (1.0 / 36.0)
        wide = slim + slim
        slim_base = slim * base
        wide_base = slim_base + slim_base
        out_rows = slice(TOP + row, TOP + row + 8)
        ext[0, out_rows, cols] = keep * p[0] + 6.0 * wide_base
        for q in range(1, 19, 2):
            along = None
            for c in range(3):
                if VELOCITY[q][c] == 1:
                    along = shifted[c] if along is None else along + shifted[c]
                elif VELOCITY[q][c] == -1:
                    along = along - shifted[c]
            scaled = (wide if q < 7 else slim) * along
            even = (wide_base if q < 7 else slim_base) + scaled * along
            odd = ROOT2 * scaled
            ext[q, out_rows, cols] = keep * p[q] + (even + odd)
            ext[q + 1, out_rows, cols] = keep * p[q + 1] + (even - odd)

    def contacts_in():
        vel8[...] = jnp.zeros_like(vel8)
        vel8[0:3, :] = vel_ref[...]
        vel8[4:7, :] = vel_ref[...]
        tables = [vel8[:, h * 128:(h + 1) * 128] for h in range(8)]
        half = iota((8, 128), 0) < 4
        for c in range(24):
            cols = slice(c * 128, (c + 1) * 128)
            index = jnp.where(half, pairs_ref[0:1, cols], pairs_ref[1:2, cols])
            low = index & 127
            high = index >> 7
            found = jnp.take_along_axis(tables[0], low, axis=1, mode="promise_in_bounds")
            for h in range(1, 8):
                found = jnp.where(high == h, jnp.take_along_axis(tables[h], low, axis=1, mode="promise_in_bounds"), found)
            relative = found[4:7] - found[0:3]
            spring = spring_ref[:, cols]
            spring_out_ref[:, cols] = spring + relative
            contact = spring_coef * spring + dashpot_coef * relative
            for part, value in enumerate(split3(contact)):
                rows16[part * 3:part * 3 + 3, cols] = value

    def contacts_out():
        rows16[9:16, :] = jnp.zeros((7, 3072), F32)
        forces = rows16[...]
        spread = []
        hots = []
        for side in range(2):
            index = pairs_ref[side:side + 1, :]
            high = index >> 7
            signed = -forces if side else forces
            spread.append(jnp.concatenate([jnp.where(high == h, signed, 0.0).astype(BF16) for h in range(8)], axis=0))
            hots.append(one_hot(index & 127, 128))
        summed = dot(jnp.concatenate(spread, axis=1), jnp.concatenate(hots, axis=1), NT)
        parts = [
            summed[h * 16:h * 16 + 3] + summed[h * 16 + 3:h * 16 + 6] + summed[h * 16 + 6:h * 16 + 9] for h in range(8)]
        return jnp.concatenate(parts, axis=1)

    bring(0)
    for half in range(2):
        loads[12 + 2 * half].wait()
        loads[13 + 2 * half].wait()
        if half == 0:
            bring(1)
        for col in range(half * 512, half * 512 + 512, 128):
            for row in range(0, NX, 8):
                collide(row, col)

    for k in range(5):
        edge_x[0, k:k + 1, :] = ext[X_PLUS[k], TOP + NX - 1:TOP + NX, :]
        edge_x[1, k:k + 1, :] = ext[X_MINUS[k], TOP:TOP + 1, :]
    group = iota((NX, 128), 1) >> 5
    for side, (dirs, start, base) in enumerate(((Y_PLUS, 896, 32), (Y_MINUS, 0, 0))):
        tiles = [ext[q, TOP:TOP + NX, start:start + 128] for q in dirs]
        moved = [pltpu.roll(t, (base + 32 * k) % 128, 1) if (base + 32 * k) % 128 else t for k, t in enumerate(tiles)]
        edge_y[side, 0] = jnp.where(group == 0, moved[0], jnp.where(group == 1, moved[1], jnp.where(group == 2, moved[2], moved[3])))
        edge_y[side, 1] = moved[4]
    edge_c[0, 0:1, :] = ext[7, TOP + NX - 1:TOP + NX, 896:1024]
    edge_c[1, 0:1, :] = ext[8, TOP:TOP + 1, 0:128]
    edge_c[2, 0:1, :] = ext[9, TOP + NX - 1:TOP + NX, 0:128]
    edge_c[3, 0:1, :] = ext[10, TOP:TOP + 1, 896:1024]
    pl.semaphore_wait(barrier, len(around))

    def send(index, source, target, dx, dy):
        copy = pltpu.make_async_remote_copy(
            src_ref=source, dst_ref=target, send_sem=send_sem.at[index], recv_sem=recv_sem.at[index],
            device_id=device(dx, dy), device_id_type=MESH)
        copy.start()
        return copy

    halo = [
        send(4, edge_c.at[0], halo_c.at[0], 1, 1),
        send(5, edge_c.at[1], halo_c.at[1], -1, -1),
        send(6, edge_c.at[2], halo_c.at[2], 1, -1),
        send(7, edge_c.at[3], halo_c.at[3], -1, 1),
        send(0, edge_x.at[0], halo_x.at[0], 1, 0),
        send(1, edge_x.at[1], halo_x.at[1], -1, 0),
        send(2, edge_y.at[0], halo_y.at[0], 0, 1),
        send(3, edge_y.at[1], halo_y.at[1], 0, -1),
    ]

    def fluid_at_grains():
        for part, value in enumerate(split2(velf[...])):
            velb[part * 96:part * 96 + 96, :] = value.astype(BF16)
        for i in range(2):
            cols = slice(i * 512, (i + 1) * 512)
            got = dot(velb[...], onehot[:, cols], NN)
            got = got[0:96] + got[96:192]
            here = iota((NX, 512), 0) == (cell_ref[:, cols] >> 10)
            for c in range(3):
                fluid[c:c + 1, cols] = jnp.sum(jnp.where(here, got[c * NX:(c + 1) * NX], 0.0), axis=0, keepdims=True)

    lane = iota((NX, 128), 1)

    def stream(group):
        for k, q in enumerate(group):
            cx, cy, cz = VELOCITY[q]
            shift = cy * 32 + cz
            rows = slice(TOP - cx, TOP - cx + NX)
            value = ext[q, rows, :]
            if shift:
                value = pltpu.roll(value, shift % NYZ, 1)
            if cy == 1:
                edge = pltpu.roll(halo_yp[0, Y_PLUS.index(q), rows, :], shift % 128, 1)
                value = jnp.concatenate([jnp.where(lane < 32, edge, value[:, 0:128]), value[:, 128:]], axis=1)
            if cy == -1:
                edge = pltpu.roll(halo_yp[1, Y_MINUS.index(q), rows, :], shift % 128, 1)
                value = jnp.concatenate([value[:, :896], jnp.where(lane >= 96, edge, value[:, 896:])], axis=1)
            if q:
                bit = 1 << (q if q < 10 else q - 10)
                solid = (flags[0 if q < 10 else 1] & bit) != 0
                value = jnp.where(solid, ext[OPPOSITE[q], TOP:TOP + NX, :], value)
            read_ref[q] = value
            high = value.astype(BF16)
            at = group[0] * 2 * NX + k * NX
            splits[at:at + NX, :] = high
            splits[at + len(group) * NX:at + (len(group) + 1) * NX, :] = (value - high.astype(F32)).astype(BF16)

    def extract(group, i, width=1):
        cols = slice(i * 256, (i + width) * 256)
        at, size = group[0] * 2 * NX, len(group) * NX
        got = dot(splits[at:at + 2 * size, :], source_hot[:, cols], NN)
        here = iota((NX, 256 * width), 0) == (src_packed[:, cols] >> 10)
        for k, q in enumerate(group):
            value = got[k * NX:(k + 1) * NX] + got[size + k * NX:size + (k + 1) * NX]
            value = jnp.sum(jnp.where(here, value, 0.0), axis=0, keepdims=True)
            for w in range(width):
                gathered[i + w, q:q + 1, :] = value[:, w * 256:(w + 1) * 256]

    def move_grains(summed):
        radius = rad_ref[...]
        vel = vel_ref[...]
        total = (drag_coef * radius) * (fluid[0:3, :] - vel) + summed
        mass = mass_coef * radius * radius * radius
        falling = jnp.where(iota((3, NYZ), 0) == 2, gravity_z, 0.0)
        moved_vel = vel + total / mass + falling
        state_ref[0:3, :] = pos_ref[...] + moved_vel
        state_ref[3:6, :] = moved_vel
        state_ref[6:7, :] = radius
        state_ref[7:8, :] = jnp.ones_like(radius)

    def leave():
        slots = jnp.concatenate([mig_ref[0:1, :], mig_ref[1:2, :]], axis=1)
        state = jnp.concatenate(split3(state_ref[...]), axis=0).astype(BF16)
        out = dot(state, one_hot(slots, NYZ), NN)
        leaving[...] = out[0:8] + out[8:16] + out[16:24]

    rows_out = []

    def send_region(i):
        rows_out.append(send(10 + i, gathered.at[i], received.at[i], DISTANCE[i], 0))

    contacts_in()
    pull_ref[...] = contacts_out()
    fluid_at_grains()
    loads[16].wait()
    for copy in halo:
        copy.wait()
    for k in range(5):
        ext[X_PLUS[k], TOP - 1:TOP, :] = halo_x[0, k:k + 1, :]
        ext[X_MINUS[k], TOP + NX:TOP + NX + 1, :] = halo_x[1, k:k + 1, :]
        for side, base in enumerate((96, 0)):
            back = (base - 32 * k) % 128
            tile = halo_y[side, k // 4]
            halo_yp[side, k, TOP:TOP + NX, :] = pltpu.roll(tile, back, 1) if back else tile
    halo_yp[0, 1, TOP - 1:TOP, :] = halo_c[0, 0:1, :]
    halo_yp[1, 1, TOP + NX:TOP + NX + 1, :] = halo_c[1, 0:1, :]
    halo_yp[1, 2, TOP - 1:TOP, :] = halo_c[2, 0:1, :]
    halo_yp[0, 2, TOP + NX:TOP + NX + 1, :] = halo_c[3, 0:1, :]
    stream(GROUPS[0])
    extract(GROUPS[0], 0, 2)
    send_region(0)
    send_region(1)
    extract(GROUPS[0], 2, 2)
    send_region(2)
    send_region(3)
    move_grains(pull_ref[...])
    leave()
    migrate = [send(8, leaving, joined.at[0], -1, 0), send(9, leaving, joined.at[1], 1, 0)]

    for i in range(4):
        cols = slice(i * 256, (i + 1) * 256)
        rows_out[i].wait()
        stays = iota((24, 256), 1).astype(F32) >= counts[i]
        carried = jnp.where(stays, gathered[i], received[i])
        here = one_hot(tgt_packed[:, cols] >> 10, NX)
        for q in range(19):
            for part, value in enumerate(split2(carried[q:q + 1, :])):
                spread_ref[(part * 19 + q) * NX:(part * 19 + q + 1) * NX, cols] = here * value.astype(BF16)
        spread_ref[38 * NX:39 * NX, cols] = here

    for copy in migrate:
        copy.wait()
    mig_lane = iota((8, 128), 1)
    change = jnp.where(iota((8, 128), 0) == 0, jnp.where(mig_lane < 64, float(NX), -float(NX)), 0.0)
    newcomers = jnp.where(mig_lane < 64, joined[0], joined[1]) + change
    slots = jnp.concatenate([mig_ref[0:1, :], mig_ref[1:2, :]], axis=1)
    placed = dot(jnp.concatenate(split3(newcomers), axis=0).astype(BF16), one_hot(slots, NYZ), NT)
    placed = placed[0:8] + placed[8:16] + placed[16:24]
    result_ref[...] = jnp.where(placed[7:8] > 0.5, placed, state_ref[...])


def finish_kernel(
    read_ref, spread_ref, tgtp_ref, result_ref, spring_ref,
    next_hbm, pos_hbm, vel_hbm, rad_hbm, spring_hbm,
    blended, pos, vel, rad, sem,
):
    pos[...] = result_ref[0:3, :]
    vel[...] = result_ref[3:6, :]
    rad[...] = result_ref[6:7, :]
    copies = []
    for source, target in ((spring_ref, spring_hbm), (pos, pos_hbm), (vel, vel_hbm), (rad, rad_hbm)):
        copies.append(pltpu.make_async_copy(source, target, sem.at[len(copies)]))
        copies[-1].start()

    row = tgtp_ref[...] & 1023
    for i in range(2):
        cols = slice(i * 512, (i + 1) * 512)
        got = dot(spread_ref[...], one_hot(row, 512, i * 512), NT)
        hit = got[38 * NX:39 * NX] > 0.5
        for start, stop in ((0, 10), (10, 19)):
            for q in range(start, stop):
                value = read_ref[q, :, cols]
                carried = got[q * NX:(q + 1) * NX] + got[(19 + q) * NX:(20 + q) * NX]
                blended[q, :, cols] = jnp.where(hit, blend_coef * (value + carried), value)
            copies.append(pltpu.make_async_copy(
                blended.at[start:stop, :, cols], next_hbm.at[start:stop, :, cols], sem.at[len(copies)]))
            copies[-1].start()
    for copy in copies:
        copy.wait()


def shards(
    pdfs, link_flags, block_level, grain_pos, grain_vel, grain_radius, grain_cell, contact_pairs, contact_spring, iface_source,
    iface_offset, iface_slot, iface_target, migrant_slots,
):
    row = (1, NYZ)
    vmem = pl.BlockSpec(memory_space=pltpu.VMEM)
    hbm = pl.BlockSpec(memory_space=pl.ANY)
    outs = pl.pallas_call(
        step_kernel,
        name="step",
        out_shape=(
            pltpu.VMEM((19, NX, NYZ), F32),
            pltpu.VMEM((39 * NX, NYZ), BF16),
            pltpu.VMEM(row, jnp.int32),
            pltpu.VMEM((8, NYZ), F32),
            pltpu.VMEM((3, 3072), F32),
        ),
        in_specs=[hbm] * 14,
        out_specs=(vmem,) * 5,
        scratch_shapes=[
            pltpu.VMEM((19, NX, NYZ), F32),
            pltpu.VMEM((2, NX, NYZ), jnp.int32),
            pltpu.SMEM((1,), jnp.int32),
            pltpu.VMEM((3, NYZ), F32),
            pltpu.VMEM((3, NYZ), F32),
            pltpu.VMEM(row, F32),
            pltpu.VMEM(row, jnp.int32),
            pltpu.VMEM((2, 3072), jnp.int32),
            pltpu.VMEM((3, 3072), F32),
            pltpu.VMEM(row, jnp.int32),
            pltpu.VMEM(row, jnp.int32),
            pltpu.VMEM(row, jnp.int32),
            pltpu.VMEM((8, 128), jnp.int32),
            pltpu.VMEM((2, 64), jnp.int32),
            pltpu.VMEM((NYZ, NYZ), BF16),
            pltpu.VMEM((NYZ, NYZ), BF16),
            pltpu.VMEM((8 * NX, NYZ), BF16),
            pltpu.VMEM((19, EXT, NYZ), F32),
            pltpu.VMEM((3 * NX, NYZ), F32),
            pltpu.VMEM((6 * NX, NYZ), BF16),
            pltpu.VMEM((8, NYZ), F32),
            pltpu.VMEM((16, 3072), F32),
            pltpu.VMEM((2, 8, NYZ), F32),
            pltpu.VMEM((2, 2, NX, 128), F32),
            pltpu.VMEM((4, 8, 128), F32),
            pltpu.VMEM((2, 8, NYZ), F32),
            pltpu.VMEM((2, 2, NX, 128), F32),
            pltpu.VMEM((2, 5, EXT, 128), F32),
            pltpu.VMEM((4, 8, 128), F32),
            pltpu.VMEM((38 * NX, NYZ), BF16),
            pltpu.VMEM((4, 24, 256), F32),
            pltpu.VMEM((4, 24, 256), F32),
            pltpu.VMEM((8, 128), F32),
            pltpu.VMEM((2, 8, 128), F32),
            pltpu.VMEM((8, NYZ), F32),
            pltpu.VMEM((4 * NX, NYZ), F32),
            pltpu.VMEM((8, NYZ), F32),
            pltpu.VMEM((3, NYZ), F32),
            pltpu.SemaphoreType.DMA((17,)),
            pltpu.SemaphoreType.DMA((14,)),
            pltpu.SemaphoreType.DMA((14,)),
        ],
        compiler_params=pltpu.CompilerParams(collective_id=0, has_side_effects=True, vmem_limit_bytes=61_800_000),
    )(
        pdfs, link_flags, block_level.reshape(1), grain_pos, grain_vel, grain_radius.reshape(row), grain_cell.reshape(row), contact_pairs,
        contact_spring, iface_source.reshape(row), iface_offset.reshape(row), iface_slot.reshape(row),
        iface_target.reshape(8, 128), migrant_slots,
    )
    read, spread, tgtp, state, spring_next = outs
    result = pl.pallas_call(
        finish_kernel,
        name="finish",
        out_shape=(
            jax.ShapeDtypeStruct((19, NX, NYZ), F32),
            jax.ShapeDtypeStruct((3, NYZ), F32),
            jax.ShapeDtypeStruct((3, NYZ), F32),
            jax.ShapeDtypeStruct(row, F32),
            jax.ShapeDtypeStruct((3, 3072), F32),
        ),
        in_specs=[vmem] * 5,
        out_specs=(hbm,) * 5,
        scratch_shapes=[
            pltpu.VMEM((19, NX, NYZ), F32),
            pltpu.VMEM((3, NYZ), F32),
            pltpu.VMEM((3, NYZ), F32),
            pltpu.VMEM(row, F32),
            pltpu.SemaphoreType.DMA((12,)),
        ],
        compiler_params=pltpu.CompilerParams(vmem_limit_bytes=40 << 20),
    )(read, spread, tgtp, state, spring_next)
    pdfs_next, pos_next, vel_next, rad_next, spring_out = result
    return pdfs_next, pos_next, vel_next, rad_next.reshape(NYZ), spring_out


def solution(mesh):
    both = ("wide", "narrow")
    in_specs = (
        P(None, "wide", "narrow"), P(None, "wide", "narrow"), P("wide", "narrow"), P(None, both), P(None, both), P(both), P(both),
        P(None, both), P(None, both), P(both), P(), P(), P(both), P(None, both),
    )
    out_specs = (P(None, "wide", "narrow"), P(None, both), P(None, both), P(both), P(None, both))
    return jax.shard_map(shards, mesh=mesh, in_specs=in_specs, out_specs=out_specs, check_vma=False)
```
